32 devices in a mesh: dp: 16 (over z, y, core), tensor: 2 (over x).
Axes of the slice: x: 2, y: 2, z: 4, core: 2. Of those that a mesh axis runs over, the one named last changes fastest.
Arguments:
- hidden_in: bfloat16 [1024, 16, 1024], P('tensor', 'dp'), may hold values from -12 to 12
- query_w: bfloat16 [1024, 1024], P(None, 'tensor'), may hold values from -0.125 to 0.125
- key_w: bfloat16 [1024, 1024], P(None, 'tensor'), may hold values from -0.1875 to 0.1875
- value_w: bfloat16 [1024, 1024], P(None, 'tensor'), may hold values from -0.1875 to 0.1875
- query_b: bfloat16 [1024], P('tensor'), may hold values from -3 to 3
- value_b: bfloat16 [1024], P('tensor'), may hold values from -3 to 3
- out_w: bfloat16 [1024, 1024], P('tensor'), may hold values from -1.5 to 1.5
- out_b: bfloat16 [1024], replicated, may hold values from -3 to 3
- gain_attn: bfloat16 [1024], replicated, may hold values from 0.5 to 1.5
- shift_attn: bfloat16 [1024], replicated, may hold values from -3 to 3
- up_w: bfloat16 [1024, 4096], P(None, 'tensor'), may hold values from -0.1875 to 0.1875
- up_b: bfloat16 [4096], P('tensor'), may hold values from -3 to 3
- down_w: bfloat16 [4096, 1024], P('tensor'), may hold values from -0.125 to 0.125
- down_b: bfloat16 [1024], replicated, may hold values from -3 to 3
- gain_ffn: bfloat16 [1024], replicated, may hold values from 0.5 to 1.5
- shift_ffn: bfloat16 [1024], replicated, may hold values from -3 to 3
- random_blocks: int32 [16, 14, 3], P('tensor'), may hold values from 1 to 14, as said below
- cotangent: bfloat16 [1024, 16, 1024], P('tensor', 'dp'), may hold values from -6 to 6
Outputs:
- layer_out: bfloat16 [1024, 16, 1024], P('tensor', 'dp')
- grad_input: bfloat16 [1024, 16, 1024], P('tensor', 'dp')
- grad_query_w: float32 [1024, 1024], P(None, 'tensor')
- grad_key_w: float32 [1024, 1024], P(None, 'tensor')
- grad_value_w: float32 [1024, 1024], P(None, 'tensor')
- grad_query_b: float32 [1024], P('tensor')
- grad_value_b: float32 [1024], P('tensor')
- grad_out_w: float32 [1024, 1024], P('tensor')
- grad_out_b: float32 [1024], replicated
- grad_gain_attn: float32 [1024], replicated
- grad_shift_attn: float32 [1024], replicated
- grad_up_w: float32 [1024, 4096], P(None, 'tensor')
- grad_up_b: float32 [4096], P('tensor')
- grad_down_w: float32 [4096, 1024], P('tensor')
- grad_down_b: float32 [1024], replicated
- grad_gain_ffn: float32 [1024], replicated
- grad_shift_ffn: float32 [1024], replicated
- rms_stats: float32 [3], replicated
The draws below stay inside these ranges and needn't reach their ends.
Inputs may be any that keep to these rules, and one draw needn't show every extreme that they name: `random_blocks`: entry [h, i, :] names 3 different key blocks for head h and query block i + 1, none of them 0, 15, i, i + 1 or i + 2.
All inputs are finite; a program needn't handle non-finite values.
Results may differ from the reference program's by a relative error of at most 0.025.
Values may be sent and summed in bfloat16 or wider, within the bound.
No kernel may reach another device: no remote copies, remote signals or barrier semaphores. Data moves between devices by JAX's collectives and lax.ppermute only.
A program may use at most 256 MiB of HBM per device.

```python
import jax
import jax.numpy as jnp
from jax import lax

D = 1024
H = 16
HD = 64
FF = 4096
BLOCK = 64
RAND = 3
NB = 16
SEQ_DEV = 1
L = 1024
SEQS = 16


def draw_hidden_in(key, part):
    seq_ids = jnp.arange(SEQS, dtype=jnp.float32)
    seq_scale = 2.0 ** (seq_ids / max(SEQS - 1, 1))
    base = jnp.clip(jax.random.normal(key, (L, SEQS, D), jnp.float32), -6.0, 6.0)
    return (base * seq_scale[None, :, None]).astype(jnp.bfloat16)


def draw_random_blocks(key, part):
    random_keys = jax.random.randint(key, (H, NB - 2, NB), 0, 1048576)
    column = jnp.arange(NB, dtype=jnp.int32)
    query_ids = jnp.arange(NB - 2, dtype=jnp.int32)[:, None] + 1
    scores = random_keys * NB + column
    banned = (column == 0) | (column == NB - 1) | (jnp.abs(column - query_ids) <= 1)
    scores = jnp.where(banned, 1048576 * NB + column, scores)
    ranking = jnp.argsort(scores, axis=-1, stable=True)
    return ranking[..., :RAND].astype(jnp.int32)


def level_of(rng, extent, split, least, top_value):
    def one(axis_at, blocks):
        heights = jax.random.uniform(jax.random.fold_in(jax.random.fold_in(rng, 6), axis_at), (blocks,), jnp.float32, least / len(split), top_value / len(split))
        return jnp.repeat(jnp.exp(heights), extent[axis_at] // blocks).reshape((-1,) + (1,) * (len(extent) - axis_at - 1))

    level = one(*split[0])
    for cut in split[1:]:
        level = level * one(*cut)
    return level


def normal_values(rng, extent, deviation, reach, cuts=(), kind=jnp.bfloat16):
    level = level_of(rng, extent, cuts, -0.22, 0.18) if cuts else 1.0
    result = jax.random.normal(rng, extent, jnp.float32) * deviation * level
    return jnp.minimum(jnp.maximum(result, -reach), reach).astype(kind)


def setup_inputs(seed: int = 0) -> dict:
    keys = jax.random.split(jax.random.key(seed), 19)
    hidden_in = draw_hidden_in(jax.random.fold_in(keys[18], 71), 0)
    query_w = normal_values(keys[1], (D, D), (2 * D) ** -0.5, 0.125, ((1, 2),))
    key_w = normal_values(keys[2], (D, D), D ** -0.5, 0.1875, ((1, 2),))
    value_w = normal_values(keys[3], (D, D), D ** -0.5, 0.1875, ((1, 2),))
    query_b = normal_values(keys[4], (D,), 0.5, 3.0, ((0, 2),))
    value_b = normal_values(keys[5], (D,), 0.5, 3.0, ((0, 2),))
    out_w = normal_values(keys[6], (D, D), (D // 64) ** -0.5, 1.5, ((0, 2),))
    out_b = normal_values(keys[7], (D,), 0.5, 3.0)
    gain_attn = jnp.clip(1.0 + 0.1 * jax.random.normal(keys[8], (D,), jnp.float32), 0.5, 1.5).astype(jnp.bfloat16)
    shift_attn = normal_values(keys[9], (D,), 0.3, 3.0)
    up_w = normal_values(keys[10], (D, FF), D ** -0.5, 0.1875, ((1, 2),))
    up_b = normal_values(keys[11], (FF,), 0.5, 3.0, ((0, 2),))
    down_w = normal_values(keys[12], (FF, D), (FF // 2) ** -0.5, 0.125, ((0, 2),))
    down_b = normal_values(keys[13], (D,), 0.5, 3.0)
    gain_ffn = jnp.clip(1.0 + 0.1 * jax.random.normal(keys[14], (D,), jnp.float32), 0.5, 1.5).astype(jnp.bfloat16)
    shift_ffn = normal_values(keys[15], (D,), 0.3, 3.0)
    random_blocks = draw_random_blocks(jax.random.fold_in(keys[18], 71), 0)
    cotangent = normal_values(keys[17], (L, SEQS, D), 1.0, 6.0, ((0, 2), (1, 16)))
    return {"hidden_in": hidden_in, "query_w": query_w, "key_w": key_w, "value_w": value_w, "query_b": query_b, "value_b": value_b, "out_w": out_w, "out_b": out_b, "gain_attn": gain_attn, "shift_attn": shift_attn, "up_w": up_w, "up_b": up_b, "down_w": down_w, "down_b": down_b, "gain_ffn": gain_ffn, "shift_ffn": shift_ffn, "random_blocks": random_blocks, "cotangent": cotangent}


@jax.custom_vjp
def low(v):
    return lax.optimization_barrier(v.astype(jnp.bfloat16)).astype(jnp.float32)

@jax.custom_vjp
def low_back(v):
    return v

def low_keep(v):
    return (low(v), None)

def low_pass(kept, grad):
    return (grad,)

def back_keep(v):
    return (v, None)

def back_low(kept, grad):
    return (low(grad),)
low.defvjp(low_keep, low_pass)
low_back.defvjp(back_keep, back_low)
HIGH = lax.Precision.HIGHEST
NEG = -1e+30
EPS = 1e-12

def matmul(left, right):
    return jnp.dot(left, right, precision=HIGH, preferred_element_type=jnp.float32)

def key_table(random_ids):
    middle = random_ids.shape[-2]
    blocks = middle + 2
    query_ids = jnp.arange(middle, dtype=jnp.int32) + 1
    fixed_ids = jnp.stack([query_ids - 1, query_ids, query_ids + 1, jnp.zeros_like(query_ids), jnp.full_like(query_ids, blocks - 1)], -1)
    fixed_ids = jnp.broadcast_to(fixed_ids, random_ids.shape[:-1] + (5,))
    tile_ids = jnp.concatenate([fixed_ids, random_ids.astype(jnp.int32)], -1)
    tile_keep = jnp.concatenate([jnp.ones((middle, 3), bool), (query_ids != 1)[:, None], (query_ids != blocks - 2)[:, None], jnp.ones((middle, random_ids.shape[-1]), bool)], -1)
    return (tile_ids, tile_keep)

def softmax_rows(scores):
    row_top = lax.optimization_barrier(jnp.max(scores, -1, keepdims=True))
    log_total = row_top + jnp.log(lax.optimization_barrier(jnp.sum(jnp.exp(scores - row_top), -1, keepdims=True)))
    return jnp.exp(scores - log_total)

def head_attend(operands):
    queries, key_rows, value_rows, random_ids = operands
    seqs_here, length, head_dim = queries.shape
    score_scale = head_dim ** (-0.5)
    blocks = length // BLOCK
    query_blocks = queries.reshape(seqs_here, blocks, BLOCK, head_dim)
    key_blocks = key_rows.reshape(seqs_here, blocks, BLOCK, head_dim)
    value_blocks = value_rows.reshape(seqs_here, blocks, BLOCK, head_dim)
    tile_ids, tile_keep = key_table(random_ids)
    key_tiles = key_blocks[:, tile_ids].reshape(seqs_here, blocks - 2, -1, head_dim)
    value_tiles = value_blocks[:, tile_ids].reshape(seqs_here, blocks - 2, -1, head_dim)
    key_mask = jnp.repeat(tile_keep, BLOCK, axis=-1)
    mid_scores = low_back(jnp.einsum('smqd,smkd->smqk', query_blocks[:, 1:-1], key_tiles, precision=HIGH) * score_scale)
    mid_scores = jnp.where(key_mask[None, :, None, :], mid_scores, NEG)
    mid_probs = low(softmax_rows(mid_scores))
    mid_out = jnp.einsum('smqk,smkd->smqd', mid_probs, value_tiles, precision=HIGH)
    end_queries = jnp.concatenate([query_blocks[:, :1], query_blocks[:, -1:]], 1)
    end_scores = low_back(jnp.einsum('sgqd,skd->sgqk', end_queries, key_rows, precision=HIGH) * score_scale)
    end_probs = low(softmax_rows(end_scores))
    end_out = jnp.einsum('sgqk,skd->sgqd', end_probs, value_rows, precision=HIGH)
    joined = jnp.concatenate([end_out[:, :1], mid_out, end_out[:, 1:]], 1)
    return joined.reshape(seqs_here, length, head_dim)

def layer_norm(rows, gain, shift):
    centre = rows - lax.optimization_barrier(jnp.mean(rows, -1, keepdims=True))
    inverse = lax.rsqrt(lax.optimization_barrier(jnp.mean(centre * centre, -1, keepdims=True)) + EPS)
    return gain * (centre * inverse) + shift

def layer(params, seq_rows, random_blocks):
    query_w, key_w, value_w, query_b, value_b, out_w, out_b, gain_attn, shift_attn, up_w, up_b, down_w, down_b, gain_ffn, shift_ffn = params
    length, seqs_here, width = seq_rows.shape
    flat_rows = seq_rows.reshape(-1, width)
    queries = low_back(low(matmul(flat_rows, query_w) + query_b))
    key_rows = low_back(low(matmul(flat_rows, key_w)))
    value_rows = low_back(low(matmul(flat_rows, value_w) + value_b))

    def split_heads(rows):
        return rows.reshape(length, seqs_here, H, HD).transpose(2, 1, 0, 3)
    context = lax.map(jax.checkpoint(head_attend), (split_heads(queries), split_heads(key_rows), split_heads(value_rows), random_blocks))
    context = context.transpose(2, 1, 0, 3).reshape(-1, width)
    context = low_back(low(context))
    attn_out = low_back(matmul(context, out_w))
    resid = flat_rows + attn_out + out_b
    hidden = layer_norm(resid, gain_attn, shift_attn)
    up_rows = low_back(matmul(low(hidden), up_w) + up_b)
    act_rows = low(jax.nn.gelu(up_rows, approximate=True))
    mlp_out = low_back(matmul(act_rows, down_w))
    resid2 = hidden + mlp_out + down_b
    output = layer_norm(resid2, gain_ffn, shift_ffn)
    squares = jnp.stack([jnp.sum(resid * resid), jnp.sum(attn_out * attn_out), jnp.sum(mlp_out * mlp_out)])
    return (output.reshape(length, seqs_here, width), squares)

def reference(hidden_in, query_w, key_w, value_w, query_b, value_b, out_w, out_b, gain_attn, shift_attn, up_w, up_b, down_w, down_b, gain_ffn, shift_ffn, random_blocks, cotangent):
    params = tuple((p.astype(jnp.float32) for p in (query_w, key_w, value_w, query_b, value_b, out_w, out_b, gain_attn, shift_attn, up_w, up_b, down_w, down_b, gain_ffn, shift_ffn)))
    inputs = hidden_in.astype(jnp.float32)
    groups = SEQS // SEQ_DEV

    def whole(params, inputs):
        grouped = inputs.reshape(L, groups, SEQ_DEV, D).transpose(1, 0, 2, 3)
        run_group = jax.checkpoint(lambda p, rows: layer(p, rows, random_blocks))

        def step(carry, rows):
            output, squares = run_group(params, rows)
            return (carry + squares, output)
        squares, outputs = lax.scan(step, jnp.zeros((3,), jnp.float32), grouped)
        return (outputs.transpose(1, 0, 2, 3).reshape(L, SEQS, D), squares)
    output, vjp_fn, squares = jax.vjp(whole, params, inputs, has_aux=True)
    grads, grad_in = vjp_fn(cotangent.astype(jnp.float32))
    rms_stats = jnp.sqrt(squares / (SEQS * L * D))
    return (output.astype(jnp.bfloat16), grad_in.astype(jnp.bfloat16), grads[0], grads[1], grads[2], grads[3], grads[4], grads[5], grads[6], grads[7], grads[8], grads[9], grads[10], grads[11], grads[12], grads[13], grads[14], rms_stats)
```

```python
import functools
import math

import jax
import jax.numpy as jnp
from jax import lax
from jax.experimental import pallas as pl
from jax.experimental.pallas import tpu as pltpu
from jax.sharding import PartitionSpec as P

HD = 64
BLOCK = 64
NEG = -1e30
EPS = 1e-12
GELU_C = math.sqrt(2.0 / math.pi)
CHUNKS = 2
LOW = jnp.bfloat16


def dot_on(left, right, left_dim, right_dim):
    return lax.dot_general(
        left,
        right,
        (((left_dim,), (right_dim,)), ((), ())),
        preferred_element_type=jnp.float32,
    )


def lane_masks(width, value):
    lane = lax.broadcasted_iota(jnp.int32, (1, width), 1) // HD
    return [jnp.where(lane == h, value, 0.0).astype(LOW) for h in range(width // HD)]


def stack_heads(rows, masks):
    return jnp.concatenate([rows * m for m in masks], 0)


def unstack_heads(stacked, heads):
    lane = lax.broadcasted_iota(jnp.int32, (1, stacked.shape[1]), 1) // HD
    out = stacked[:BLOCK]
    for h in range(1, heads):
        out = jnp.where(lane == h, stacked[h * BLOCK : (h + 1) * BLOCK], out)
    return out


def block_at(index):
    return pl.ds(pl.multiple_of(index * BLOCK, BLOCK), BLOCK)


class Plan:
    def __init__(self, chunk, chunks, ranks, length, rand, heads):
        self.blocks = length // BLOCK
        self.rank_blocks = self.blocks // ranks
        self.chunk_blocks = self.rank_blocks // chunks
        self.chunk = chunk
        self.rand = rand
        self.heads = heads
        taken = [
            j * self.rank_blocks + chunk * self.chunk_blocks + r
            for j in range(ranks)
            for r in range(self.chunk_blocks)
        ]
        self.ends = [b for b in taken if b in (0, self.blocks - 1)]
        middles = [b for b in taken if b not in self.ends]
        self.ranges = []
        for b in middles:
            if self.ranges and self.ranges[-1][1] == b:
                self.ranges[-1][1] = b + 1
            else:
                self.ranges.append([b, b + 1])

    def local(self, block, first):
        return lax.rem(block - first + self.blocks, self.blocks)

    def inner(self, local):
        part = lax.div(local, self.rank_blocks)
        rest = local - part * self.rank_blocks
        return part * self.chunk_blocks + rest - self.chunk * self.chunk_blocks

    def fixed(self, block, first):
        wanted = (jnp.int32(0), jnp.int32(self.blocks - 1), block - 1, block, block + 1)
        return [self.local(w, first) for w in wanted]

    def random(self, rb_ref, group, block, first):
        return [
            [
                self.local(rb_ref[group * self.heads + h, (block - 1) * self.rand + r], first)
                for h in range(self.heads)
            ]
            for r in range(self.rand)
        ]

    def run(self, one, unroll):
        for low, high in self.ranges:
            count = high - low
            main = count - count % unroll
            if main > unroll:

                @pl.loop(0, main // unroll)
                def _(step, low=low):
                    for u in range(unroll):
                        one(low + step * unroll + u)
            else:
                main = 0
            for x in range(main, count):
                one(jnp.int32(low + x))


def pick_tiles(ref, fixed, rands):
    width = ref.shape[1]
    column = min(128, width)
    per = column // HD
    lane = lax.broadcasted_iota(jnp.int32, (1, column), 1) // HD
    parts = [ref[block_at(f), :] for f in fixed]
    for per_head in rands:
        columns = []
        for c in range(width // column):
            tile = None
            for p in range(per):
                x = ref[block_at(per_head[c * per + p]), c * column : (c + 1) * column]
                tile = x if tile is None else jnp.where(lane == p, x, tile)
            columns.append(tile)
        parts.append(jnp.concatenate(columns, 1) if len(columns) > 1 else columns[0])
    return jnp.concatenate(parts, 0)


def attend_kernel(plan, unroll, first_ref, rb_ref, q_ref, k_ref, v_ref, o_ref, lse_ref):
    group = pl.program_id(0)
    first = first_ref[0]
    heads = plan.heads
    masks = lane_masks(q_ref.shape[1], HD**-0.5)

    def finish(scores, values, place):
        top = jnp.max(scores, 1, keepdims=True)
        weights = jnp.exp(scores - top)
        total = jnp.sum(weights, 1, keepdims=True)
        out = dot_on(weights.astype(LOW), values, 1, 0) * (1.0 / total)
        o_ref[block_at(place), :] = unstack_heads(out, heads).astype(LOW)
        wide = jnp.broadcast_to(top + jnp.log(total), (heads * BLOCK, 128))
        lse_ref[0, pl.ds(place, 1), :] = jnp.transpose(wide)[0:1, :]

    def one(block):
        fixed = plan.fixed(block, first)
        rands = plan.random(rb_ref, group, block, first)
        queries = stack_heads(q_ref[block_at(fixed[3]), :], masks)
        scores = dot_on(queries, pick_tiles(k_ref, fixed, rands), 1, 1)
        lane = lax.broadcasted_iota(jnp.int32, (1, 2 * BLOCK), 1)
        drop = ((block == 1) & (lane < BLOCK)) | (
            (block == plan.blocks - 2) & (lane >= BLOCK)
        )
        scores = jnp.concatenate(
            [jnp.where(drop, NEG, scores[:, : 2 * BLOCK]), scores[:, 2 * BLOCK :]], 1
        )
        finish(scores, pick_tiles(v_ref, fixed, rands), plan.inner(fixed[3]))

    plan.run(one, unroll)
    for b in plan.ends:
        local = plan.local(jnp.int32(b), first)
        queries = stack_heads(q_ref[block_at(local), :], masks)
        finish(dot_on(queries, k_ref[...], 1, 1), v_ref[...], plan.inner(local))


def attend_back_kernel(plan, unroll, started, last, first_ref, rb_ref, q_ref, k_ref, v_ref, *refs):
    do_ref, lse_ref, *refs = refs
    if started:
        dk_in, dv_in, *refs = refs
    dq_ref, dk_ref, dv_ref, *refs = refs
    dk_acc, dv_acc = refs if last else (dk_ref, dv_ref)
    group = pl.program_id(0)
    first = first_ref[0]
    heads = plan.heads
    width = q_ref.shape[1]
    query_masks, out_masks = lane_masks(width, HD**-0.5), lane_masks(width, 1.0)
    column = min(128, width)
    per = column // HD
    lane = lax.broadcasted_iota(jnp.int32, (1, column), 1) // HD
    if started:
        dk_acc[...] = dk_in[...]
        dv_acc[...] = dv_in[...]
    else:
        dk_acc[...] = jnp.zeros_like(dk_acc)
        dv_acc[...] = jnp.zeros_like(dv_acc)

    def core(scores, keys, values, queries, douts, place):
        probs = jnp.exp(scores - lse_ref[0, pl.ds(place, 1), :])
        dprobs = dot_on(values, douts, 1, 1)
        row_dot = jnp.sum(probs * dprobs, 0, keepdims=True)
        dscores = (probs * (dprobs - row_dot)).astype(LOW)
        dv = dot_on(probs.astype(LOW), douts, 1, 0)
        dk = dot_on(dscores, queries, 1, 0)
        dq = unstack_heads(dot_on(dscores, keys, 0, 0), heads) * (HD**-0.5)
        dq_ref[block_at(place), :] = dq.astype(LOW)
        return dk, dv

    def add_tiles(acc, value, fixed, rands):
        for n, f in enumerate(fixed):
            acc[block_at(f), :] += value[n * BLOCK : (n + 1) * BLOCK]
        for r, per_head in enumerate(rands):
            tile = value[(5 + r) * BLOCK : (6 + r) * BLOCK]
            for h in range(heads):
                c = h // per
                cut = slice(c * column, (c + 1) * column)
                acc[block_at(per_head[h]), cut] += jnp.where(lane == h % per, tile[:, cut], 0.0)

    def one(block):
        fixed = plan.fixed(block, first)
        rands = plan.random(rb_ref, group, block, first)
        place = plan.inner(fixed[3])
        queries = stack_heads(q_ref[block_at(fixed[3]), :], query_masks)
        douts = stack_heads(do_ref[block_at(place), :], out_masks)
        keys = pick_tiles(k_ref, fixed, rands)
        values = pick_tiles(v_ref, fixed, rands)
        scores = dot_on(keys, queries, 1, 1)
        scores = jnp.concatenate(
            [
                jnp.where(block == 1, NEG, scores[:BLOCK]),
                jnp.where(block == plan.blocks - 2, NEG, scores[BLOCK : 2 * BLOCK]),
                scores[2 * BLOCK :],
            ],
            0,
        )
        dk, dv = core(scores, keys, values, queries, douts, place)
        add_tiles(dk_acc, dk, fixed, rands)
        add_tiles(dv_acc, dv, fixed, rands)

    for b in plan.ends:
        local = plan.local(jnp.int32(b), first)
        place = plan.inner(local)
        queries = stack_heads(q_ref[block_at(local), :], query_masks)
        douts = stack_heads(do_ref[block_at(place), :], out_masks)
        scores = dot_on(k_ref[...], queries, 1, 1)
        dk, dv = core(scores, k_ref[...], v_ref[...], queries, douts, place)
        dk_acc[...] += dk
        dv_acc[...] += dv
    plan.run(one, unroll)
    if last:
        dk_ref[...] = dk_acc[...].astype(LOW)
        dv_ref[...] = dv_acc[...].astype(LOW)


def group_width(channels):
    return min(256, channels)


def packed_specs(length, channels):
    width = group_width(channels)
    groups = channels // width
    return [
        pl.BlockSpec((length, width), lambda g, *_, n=n: (0, n * groups + g)) for n in range(3)
    ]


def attend(qkv, random_ids, first, chunk, chunks, ranks):
    length, channels = qkv.shape[0], qkv.shape[1] // 3
    width = group_width(channels)
    groups, heads = channels // width, width // HD
    plan = Plan(chunk, chunks, ranks, length, random_ids.shape[1] // (length // BLOCK - 2), heads)
    rows = length // chunks
    return pl.pallas_call(
        functools.partial(attend_kernel, plan, 4),
        grid_spec=pltpu.PrefetchScalarGridSpec(
            num_scalar_prefetch=2,
            grid=(groups,),
            in_specs=packed_specs(length, channels),
            out_specs=[
                pl.BlockSpec((rows, width), lambda g, *_: (0, g)),
                pl.BlockSpec((1, rows // BLOCK, width), lambda g, *_: (g, 0, 0)),
            ],
        ),
        out_shape=[
            jax.ShapeDtypeStruct((rows, channels), LOW),
            jax.ShapeDtypeStruct((groups, rows // BLOCK, width), jnp.float32),
        ],
        compiler_params=pltpu.CompilerParams(vmem_limit_bytes=24 << 20),
        cost_estimate=pl.CostEstimate(
            flops=6 << 30, bytes_accessed=8 * length * channels, transcendentals=0
        ),
        name="attend",
    )(first, random_ids, qkv, qkv, qkv)


def attend_back(qkv, dout, lse, random_ids, first, sums, chunk, chunks, ranks):
    length, channels = qkv.shape[0], qkv.shape[1] // 3
    width = group_width(channels)
    groups, heads = channels // width, width // HD
    plan = Plan(chunk, chunks, ranks, length, random_ids.shape[1] // (length // BLOCK - 2), heads)
    rows = length // chunks
    last = chunk == chunks - 1
    part = pl.BlockSpec((rows, width), lambda g, *_: (0, g))
    full = pl.BlockSpec((length, width), lambda g, *_: (0, g))
    sum_shape = jax.ShapeDtypeStruct((length, channels), LOW if last else jnp.float32)
    return pl.pallas_call(
        functools.partial(attend_back_kernel, plan, 3, bool(sums), last),
        grid_spec=pltpu.PrefetchScalarGridSpec(
            num_scalar_prefetch=2,
            grid=(groups,),
            in_specs=packed_specs(length, channels)
            + [part, pl.BlockSpec((1, rows // BLOCK, width), lambda g, *_: (g, 0, 0))]
            + [full] * len(sums),
            out_specs=[part, full, full],
            scratch_shapes=[pltpu.VMEM((length, width), jnp.float32)] * (2 if last else 0),
        ),
        out_shape=[jax.ShapeDtypeStruct((rows, channels), LOW), sum_shape, sum_shape],
        compiler_params=pltpu.CompilerParams(vmem_limit_bytes=32 << 20),
        cost_estimate=pl.CostEstimate(
            flops=12 << 30, bytes_accessed=16 * length * channels, transcendentals=0
        ),
        name="attend_back",
    )(first, random_ids, qkv, qkv, qkv, dout, lse, *sums)


def fetch(rows, ranks):
    parts = [rows]
    for s in range(1, ranks):
        parts.append(lax.ppermute(rows, "tensor", [((k + s) % ranks, k) for k in range(ranks)]))
    return parts


def share_sum(term, parts, ranks):
    moved = []
    for s in range(1, ranks):
        share = term(parts[s]).astype(LOW)
        moved.append(lax.ppermute(share, "tensor", [(k, (k + s) % ranks) for k in range(ranks)]))
    total = term(parts[0])
    for m in moved:
        total = total + m.astype(jnp.float32)
    return total


class Ring:
    def __init__(self, size):
        self.size = size
        self.chips = size // 2
        self.order = list(range(0, self.chips, 2)) + list(range(1, self.chips, 2))[::-1]
        self.ahead = self.chips // 2
        self.behind = self.chips - 1 - self.ahead
        index = lax.axis_index("dp")
        self.core = lax.rem(index, 2)
        chip = lax.div(index, 2)
        half = lax.div(chip, 2)
        self.place = jnp.where(lax.rem(chip, 2) == 0, half, self.chips - 1 - half)
        self.place_core = jnp.stack([self.core, self.place]).astype(jnp.int32)

    def shift(self, value, by):
        pairs = []
        for q in range(self.chips):
            source, target = self.order[q], self.order[(q + by) % self.chips]
            pairs += [(2 * source + c, 2 * target + c) for c in range(2)]
        return lax.ppermute(value, "dp", pairs)

    def mate(self, value):
        return lax.ppermute(value, "dp", [(i, i ^ 1) for i in range(self.size)])

    def fits(self, rows):
        return self.size % 4 == 0 and rows % (16 * self.size) == 0

    def total(self, grad):
        rows, columns = grad.shape
        chips, shard = self.chips, rows // self.size
        halves = grad.reshape(2, chips, shard, columns)
        given = lax.dynamic_index_in_dim(halves, 1 - self.core, 0, False)
        kept = lax.dynamic_index_in_dim(halves, self.core, 0, False)
        held = add_low(kept, self.mate(given))

        def take(offset):
            index = lax.rem(self.place + offset + 2 * chips, chips)
            return lax.dynamic_index_in_dim(held, index, 0, False)

        right, left = take(self.ahead), take(-self.behind)
        for j in range(1, self.ahead + 1):
            right = self.shift(right, 1)
            if j < self.ahead:
                right = add_low(right, take(self.ahead - j))
            if j <= self.behind:
                left = self.shift(left, -1)
                if j < self.behind:
                    left = add_low(left, take(j - self.behind))
        own = (
            take(0).astype(jnp.float32) + right.astype(jnp.float32) + left.astype(jnp.float32)
        ).astype(LOW)
        pieces = {0: own}
        right = left = own
        for j in range(1, self.ahead + 1):
            right = pieces[-j] = self.shift(right, 1)
            if j <= self.behind:
                left = pieces[j] = self.shift(left, -1)
        ordered = jnp.stack([pieces[o] for o in range(-self.ahead, self.behind + 1)])
        return self.place_pieces(ordered, self.mate(ordered))

    def place_pieces(self, mine, theirs):
        chips, shard, columns = mine.shape
        ahead = self.ahead

        def body(where_ref, mine_ref, theirs_ref, out_ref):
            step = pl.program_id(0)

            @pl.when(step < chips)
            def _():
                out_ref[...] = mine_ref[0].astype(jnp.float32)

            @pl.when(step >= chips)
            def _():
                out_ref[...] = theirs_ref[0].astype(jnp.float32)

        def target(i, where):
            core = jnp.where(i < chips, where[0], 1 - where[0])
            return (core * chips + lax.rem(where[1] - ahead + i + chips, chips), 0)

        return pl.pallas_call(
            body,
            grid_spec=pltpu.PrefetchScalarGridSpec(
                num_scalar_prefetch=1,
                grid=(2 * chips,),
                in_specs=[
                    pl.BlockSpec((1, shard, columns), lambda i, w: (jnp.minimum(i, chips - 1), 0, 0)),
                    pl.BlockSpec((1, shard, columns), lambda i, w: (jnp.maximum(i - chips, 0), 0, 0)),
                ],
                out_specs=pl.BlockSpec((shard, columns), target),
            ),
            out_shape=jax.ShapeDtypeStruct((2 * chips * shard, columns), jnp.float32),
            cost_estimate=pl.CostEstimate(
                flops=0, bytes_accessed=16 * chips * shard * columns, transcendentals=0
            ),
            name="place_pieces",
        )(self.place_core, mine, theirs)


def add_low(a, b):
    return (a.astype(jnp.float32) + b.astype(jnp.float32)).astype(LOW)


def dp_total(ring, grad):
    if ring.fits(grad.shape[0]):
        return ring.total(grad.astype(LOW))
    return lax.psum(grad.astype(LOW), "dp").astype(jnp.float32)


def small_total(both, dp_only, size, ranks):
    def fold(value, axis, count):
        if count & (count - 1):
            return lax.psum(value, axis)
        bit = 1
        while bit < count:
            value = value + lax.ppermute(value, axis, [(i, i ^ bit) for i in range(count)])
            bit *= 2
        return value

    lead = both.shape[0]
    both = fold(both, "tensor", ranks)
    total = fold(jnp.concatenate([both, dp_only]), "dp", size)
    return total[:lead], total[lead:]


def layer_norm(rows, gain, shift):
    centre = rows - jnp.mean(rows, -1, keepdims=True)
    inverse = lax.rsqrt(jnp.mean(centre * centre, -1, keepdims=True) + EPS)
    normed = centre * inverse
    return gain * normed + shift, normed, inverse


def norm_back(grad, normed, inverse, gain):
    scaled = grad * gain
    return inverse * (
        scaled
        - jnp.mean(scaled, -1, keepdims=True)
        - normed * jnp.mean(scaled * normed, -1, keepdims=True)
    )


def gelu_parts(values):
    tanh_val = jnp.tanh(GELU_C * (values + 0.044715 * values * values * values))
    output = 0.5 * values * (1.0 + tanh_val)
    slope = 0.5 * (1.0 + tanh_val) + 0.5 * values * (1.0 - tanh_val * tanh_val) * GELU_C * (
        1.0 + 3.0 * 0.044715 * values * values
    )
    return output, slope


def dot(a, b):
    return jnp.dot(a, b, preferred_element_type=jnp.float32)


def dot_nt(a, b):
    return dot_on(a, b, 1, 1)


def dot_tn(a, b):
    return dot_on(a, b, 0, 0)


def local(
    dp_size,
    ranks,
    hidden_in,
    query_w,
    key_w,
    value_w,
    query_b,
    value_b,
    out_w,
    out_b,
    gain_attn,
    shift_attn,
    up_w,
    up_b,
    down_w,
    down_b,
    gain_ffn,
    shift_ffn,
    random_blocks,
    cotangent,
):
    own_rows, seqs_here, width = hidden_in.shape
    channels = query_w.shape[1]
    length = own_rows * ranks
    chunks = CHUNKS
    piece = own_rows // chunks
    ring = Ring(dp_size)
    first = (lax.axis_index("tensor") * (own_rows // BLOCK)).reshape(1).astype(jnp.int32)
    random_ids = random_blocks.reshape(random_blocks.shape[0], -1)
    rows_in = hidden_in.reshape(own_rows, width)
    grad_out = cotangent.reshape(own_rows, width)

    flat = jnp.concatenate(fetch(rows_in, ranks), 0)
    qkv_w = jnp.concatenate([query_w, key_w, value_w], 1)
    qkv_b = jnp.concatenate([query_b, jnp.zeros_like(query_b), value_b])
    qkv = (dot(flat, qkv_w) + qkv_b).astype(LOW)

    contexts, lses = [], []
    for c in range(chunks):
        context, lse = attend(qkv, random_ids, first, c, chunks, ranks)
        contexts.append(context)
        lses.append(lse)

    state = []
    for c in range(chunks):
        span = slice(c * piece, (c + 1) * piece)
        parts = [contexts[c][j * piece : (j + 1) * piece] for j in range(ranks)]
        attn_out = share_sum(lambda x: dot(x, out_w), parts, ranks)
        resid = rows_in[span].astype(jnp.float32) + attn_out + out_b
        hidden, normed, inverse = layer_norm(resid, gain_attn, shift_attn)
        state.append(
            dict(span=span, attn_out=attn_out, resid=resid, hidden=hidden, n1=normed, i1=inverse)
        )
    for s in state:
        s["x"] = fetch(s["hidden"].astype(LOW), ranks)
    for s in state:
        ups = [dot(x, up_w) + up_b for x in s["x"]]
        both = [gelu_parts(u) for u in ups]
        s["act"] = [b[0].astype(LOW) for b in both]
        s["slope"] = [b[1] for b in both]
        s["mlp_out"] = share_sum(lambda x: dot(x, down_w), s["act"], ranks)
    for s in state:
        resid2 = s["hidden"] + s["mlp_out"] + down_b
        layer_out, n2, i2 = layer_norm(resid2, gain_ffn, shift_ffn)
        s["layer_out"] = layer_out.astype(LOW)
        g = grad_out[s["span"]].astype(jnp.float32)
        s["dresid2"] = norm_back(g, n2, i2, gain_ffn)
        s["sums2"] = [
            jnp.sum(s["dresid2"], 0),
            jnp.sum(g * n2, 0),
            jnp.sum(g, 0),
        ]
        s["dmlp"] = fetch(s["dresid2"].astype(LOW), ranks)
    for s in state:
        s["dup"] = [
            (dot_nt(d, down_w) * slope).astype(LOW) for d, slope in zip(s["dmlp"], s["slope"])
        ]
        part = share_sum(lambda x: dot_nt(x, up_w), s["dup"], ranks)
        s["dhidden"] = part + s["dresid2"]
    for s in state:
        s["dresid"] = norm_back(s["dhidden"], s["n1"], s["i1"], gain_attn)
        s["sums1"] = [
            jnp.sum(s["dresid"], 0),
            jnp.sum(s["dhidden"] * s["n1"], 0),
            jnp.sum(s["dhidden"], 0),
        ]
        s["dattn"] = fetch(s["dresid"].astype(LOW), ranks)

    def joined(name):
        return jnp.concatenate([x for s in state for x in s[name]], 0)

    dmlp_all, x_all, dattn_all = joined("dmlp"), joined("x"), joined("dattn")
    act_all, dup_all = joined("act"), joined("dup")
    grad_down_w = dp_total(ring, dot_tn(act_all, dmlp_all))
    grad_up_w = dp_total(ring, dot_tn(x_all, dup_all))
    grad_out_w = dp_total(ring, dot_tn(jnp.concatenate(contexts, 0), dattn_all))
    grad_up_b = jnp.sum(dup_all.astype(jnp.float32), 0)

    dq_parts, sums = [], []
    for c, s in enumerate(state):
        dcontext = jnp.concatenate([dot_nt(d, out_w).astype(LOW) for d in s["dattn"]], 0)
        dq, dk, dv = attend_back(
            qkv, dcontext, lses[c], random_ids, first, sums, c, chunks, ranks
        )
        dq_parts.append(dq)
        sums = [dk, dv]
    dq = jnp.concatenate(
        [dq_parts[c][j * piece : (j + 1) * piece] for j in range(ranks) for c in range(chunks)], 0
    )
    dqkv = jnp.concatenate([dq] + sums, 1)
    grad_qkv = dp_total(ring, dot_tn(flat, dqkv))
    grad_qkv_b = jnp.sum(dqkv.astype(jnp.float32), 0)
    dinput = share_sum(
        lambda x: dot_nt(x, qkv_w),
        [dqkv[j * own_rows : (j + 1) * own_rows] for j in range(ranks)],
        ranks,
    )
    grad_input = (dinput + jnp.concatenate([s["dresid"] for s in state], 0)).astype(LOW)

    def summed(name, n):
        return functools.reduce(jnp.add, [s[name][n] for s in state])

    squares = [
        functools.reduce(jnp.add, [jnp.sum(s[name] * s[name]) for s in state])
        for name in ("resid", "attn_out", "mlp_out")
    ]
    scalars = jnp.pad(jnp.stack(squares), (0, 125))
    both, dp_only = small_total(
        jnp.concatenate([summed(n, i) for n in ("sums1", "sums2") for i in range(3)] + [scalars]),
        jnp.concatenate([grad_qkv_b[:channels], grad_qkv_b[2 * channels :], grad_up_b]),
        dp_size,
        ranks,
    )
    vectors = [both[i * width : (i + 1) * width] for i in range(6)]
    entries = float(own_rows * ranks * dp_size * seqs_here * width)
    rms_stats = jnp.sqrt(both[6 * width : 6 * width + 3] / entries)
    layer_out = jnp.concatenate([s["layer_out"] for s in state], 0)
    shape = hidden_in.shape
    return (
        layer_out.reshape(shape),
        grad_input.reshape(shape),
        grad_qkv[:, :channels],
        grad_qkv[:, channels : 2 * channels],
        grad_qkv[:, 2 * channels :],
        dp_only[:channels],
        dp_only[channels : 2 * channels],
        grad_out_w,
        vectors[0],
        vectors[1],
        vectors[2],
        grad_up_w,
        dp_only[2 * channels :],
        grad_down_w,
        vectors[3],
        vectors[4],
        vectors[5],
        rms_stats,
    )


def solution(mesh):
    rows = P("tensor", "dp", None)
    columns, split, whole = P(None, "tensor"), P("tensor"), P()
    first = P("tensor", None)
    return jax.shard_map(
        functools.partial(local, mesh.shape["dp"], mesh.shape["tensor"]),
        mesh=mesh,
        in_specs=(
            rows,
            columns,
            columns,
            columns,
            split,
            split,
            first,
            whole,
            whole,
            whole,
            columns,
            split,
            first,
            whole,
            whole,
            whole,
            P("tensor", None, None),
            rows,
        ),
        out_specs=(
            rows,
            rows,
            columns,
            columns,
            columns,
            split,
            split,
            first,
            whole,
            whole,
            whole,
            columns,
            split,
            first,
            whole,
            whole,
            whole,
            whole,
        ),
        check_vma=False,
    )
```

```python
import functools
import math

import jax
import jax.numpy as jnp
from jax import lax
from jax.experimental import pallas as pl
from jax.experimental.pallas import tpu as pltpu
from jax.sharding import PartitionSpec as P

HD = 64
BLOCK = 64
NEG = -1e30
EPS = 1e-12
GELU_C = math.sqrt(2.0 / math.pi)
CHUNKS = 2
LOW = jnp.bfloat16
FIRST, CORE, MATE, PLACE = range(4)
COST = pl.CostEstimate(flops=1024, bytes_accessed=1024, transcendentals=0)


def dot_on(left, right, left_dim, right_dim):
    return lax.dot_general(
        left,
        right,
        (((left_dim,), (right_dim,)), ((), ())),
        preferred_element_type=jnp.float32,
    )


def lane_masks(width, value):
    lane = lax.broadcasted_iota(jnp.int32, (1, width), 1) // HD
    return [jnp.where(lane == h, value, 0.0).astype(LOW) for h in range(width // HD)]


def stack_heads(rows, masks):
    return jnp.concatenate([rows * m for m in masks], 0)


def unstack_heads(stacked, heads):
    lane = lax.broadcasted_iota(jnp.int32, (1, stacked.shape[1]), 1) // HD
    out = stacked[:BLOCK]
    for h in range(1, heads):
        out = jnp.where(lane == h, stacked[h * BLOCK : (h + 1) * BLOCK], out)
    return out


def block_at(index):
    return pl.ds(pl.multiple_of(index * BLOCK, BLOCK), BLOCK)


class Plan:
    def __init__(self, chunk, chunks, ranks, length, rand, heads):
        self.blocks = length // BLOCK
        self.rank_blocks = self.blocks // ranks
        self.chunk_blocks = self.rank_blocks // chunks
        self.chunk = chunk
        self.rand = rand
        self.heads = heads
        taken = [
            j * self.rank_blocks + chunk * self.chunk_blocks + r
            for j in range(ranks)
            for r in range(self.chunk_blocks)
        ]
        self.ends = [b for b in taken if b in (0, self.blocks - 1)]
        middles = [b for b in taken if b not in self.ends]
        self.ranges = []
        for b in middles:
            if self.ranges and self.ranges[-1][1] == b:
                self.ranges[-1][1] = b + 1
            else:
                self.ranges.append([b, b + 1])

    def local(self, block, first):
        return lax.rem(block - first + self.blocks, self.blocks)

    def inner(self, local):
        part = lax.div(local, self.rank_blocks)
        rest = local - part * self.rank_blocks
        return part * self.chunk_blocks + rest - self.chunk * self.chunk_blocks

    def fixed(self, block, first):
        wanted = (jnp.int32(0), jnp.int32(self.blocks - 1), block - 1, block, block + 1)
        return [self.local(w, first) for w in wanted]

    def random(self, rb_ref, group, block, first):
        return [
            [
                self.local(rb_ref[group * self.heads + h, (block - 1) * self.rand + r], first)
                for h in range(self.heads)
            ]
            for r in range(self.rand)
        ]

    def run(self, one, unroll):
        for low, high in self.ranges:
            count = high - low
            main = count - count % unroll
            if main > unroll:

                @pl.loop(0, main // unroll)
                def _(step, low=low):
                    for u in range(unroll):
                        one(low + step * unroll + u)
            else:
                main = 0
            for x in range(main, count):
                one(jnp.int32(low + x))


def pick_tiles(ref, fixed, rands):
    width = ref.shape[1]
    column = min(128, width)
    per = column // HD
    lane = lax.broadcasted_iota(jnp.int32, (1, column), 1) // HD
    parts = [ref[block_at(f), :] for f in fixed]
    for per_head in rands:
        columns = []
        for c in range(width // column):
            tile = None
            for p in range(per):
                x = ref[block_at(per_head[c * per + p]), c * column : (c + 1) * column]
                tile = x if tile is None else jnp.where(lane == p, x, tile)
            columns.append(tile)
        parts.append(jnp.concatenate(columns, 1) if len(columns) > 1 else columns[0])
    return jnp.concatenate(parts, 0)


def attend_kernel(plan, unroll, table_ref, rb_ref, q_ref, k_ref, v_ref, o_ref, lse_ref):
    group = pl.program_id(0)
    first = table_ref[FIRST]
    heads = plan.heads
    masks = lane_masks(q_ref.shape[1], HD**-0.5)

    def finish(scores, values, place):
        top = jnp.max(scores, 1, keepdims=True)
        weights = jnp.exp(scores - top)
        total = jnp.sum(weights, 1, keepdims=True)
        out = dot_on(weights.astype(LOW), values, 1, 0) * (1.0 / total)
        o_ref[block_at(place), :] = unstack_heads(out, heads).astype(LOW)
        wide = jnp.broadcast_to(top + jnp.log(total), (heads * BLOCK, 128))
        lse_ref[0, pl.ds(place, 1), :] = jnp.transpose(wide)[0:1, :]

    def one(block):
        fixed = plan.fixed(block, first)
        rands = plan.random(rb_ref, group, block, first)
        queries = stack_heads(q_ref[block_at(fixed[3]), :], masks)
        scores = dot_on(queries, pick_tiles(k_ref, fixed, rands), 1, 1)
        lane = lax.broadcasted_iota(jnp.int32, (1, 2 * BLOCK), 1)
        drop = ((block == 1) & (lane < BLOCK)) | (
            (block == plan.blocks - 2) & (lane >= BLOCK)
        )
        scores = jnp.concatenate(
            [jnp.where(drop, NEG, scores[:, : 2 * BLOCK]), scores[:, 2 * BLOCK :]], 1
        )
        finish(scores, pick_tiles(v_ref, fixed, rands), plan.inner(fixed[3]))

    plan.run(one, unroll)
    for b in plan.ends:
        local = plan.local(jnp.int32(b), first)
        queries = stack_heads(q_ref[block_at(local), :], masks)
        finish(dot_on(queries, k_ref[...], 1, 1), v_ref[...], plan.inner(local))


def attend_back_kernel(plan, unroll, earlier, last, table_ref, rb_ref, q_ref, k_ref, v_ref, *refs):
    do_ref, lse_ref, *refs = refs
    dq_in, refs = refs[:earlier], refs[earlier:]
    if earlier:
        dk_in, dv_in, *refs = refs
    if last:
        all_ref, bias_ref, dq_ref, dk_acc, dv_acc = refs
    else:
        dq_ref, dk_acc, dv_acc = refs
    group = pl.program_id(0)
    first = table_ref[FIRST]
    heads = plan.heads
    width = q_ref.shape[1]
    query_masks, out_masks = lane_masks(width, HD**-0.5), lane_masks(width, 1.0)
    column = min(128, width)
    per = column // HD
    lane = lax.broadcasted_iota(jnp.int32, (1, column), 1) // HD
    if earlier:
        dk_acc[...] = dk_in[...]
        dv_acc[...] = dv_in[...]
    else:
        dk_acc[...] = jnp.zeros_like(dk_acc)
        dv_acc[...] = jnp.zeros_like(dv_acc)

    def core(scores, keys, values, queries, douts, place):
        probs = jnp.exp(scores - lse_ref[0, pl.ds(place, 1), :])
        dprobs = dot_on(values, douts, 1, 1)
        row_dot = jnp.sum(probs * dprobs, 0, keepdims=True)
        dscores = (probs * (dprobs - row_dot)).astype(LOW)
        dv = dot_on(probs.astype(LOW), douts, 1, 0)
        dk = dot_on(dscores, queries, 1, 0)
        dq = unstack_heads(dot_on(dscores, keys, 0, 0), heads) * (HD**-0.5)
        dq_ref[block_at(place), :] = dq.astype(LOW)
        return dk, dv

    def add_tiles(acc, value, fixed, rands):
        for n, f in enumerate(fixed):
            acc[block_at(f), :] += value[n * BLOCK : (n + 1) * BLOCK]
        for r, per_head in enumerate(rands):
            tile = value[(5 + r) * BLOCK : (6 + r) * BLOCK]
            for h in range(heads):
                c = h // per
                cut = slice(c * column, (c + 1) * column)
                acc[block_at(per_head[h]), cut] += jnp.where(lane == h % per, tile[:, cut], 0.0)

    def one(block):
        fixed = plan.fixed(block, first)
        rands = plan.random(rb_ref, group, block, first)
        place = plan.inner(fixed[3])
        queries = stack_heads(q_ref[block_at(fixed[3]), :], query_masks)
        douts = stack_heads(do_ref[block_at(place), :], out_masks)
        keys = pick_tiles(k_ref, fixed, rands)
        values = pick_tiles(v_ref, fixed, rands)
        scores = dot_on(keys, queries, 1, 1)
        scores = jnp.concatenate(
            [
                jnp.where(block == 1, NEG, scores[:BLOCK]),
                jnp.where(block == plan.blocks - 2, NEG, scores[BLOCK : 2 * BLOCK]),
                scores[2 * BLOCK :],
            ],
            0,
        )
        dk, dv = core(scores, keys, values, queries, douts, place)
        add_tiles(dk_acc, dk, fixed, rands)
        add_tiles(dv_acc, dv, fixed, rands)

    for b in plan.ends:
        local = plan.local(jnp.int32(b), first)
        place = plan.inner(local)
        queries = stack_heads(q_ref[block_at(local), :], query_masks)
        douts = stack_heads(do_ref[block_at(place), :], out_masks)
        scores = dot_on(k_ref[...], queries, 1, 1)
        dk, dv = core(scores, k_ref[...], v_ref[...], queries, douts, place)
        dk_acc[...] += dk
        dv_acc[...] += dv
    plan.run(one, unroll)
    if last:
        channels = all_ref.shape[1] // 3
        rows = plan.chunk_blocks * BLOCK
        chunks = earlier + 1
        for at in range(0, channels, width):

            @pl.when(group * width == at)
            def _(at=at):
                for c, source in enumerate([*dq_in, dq_ref]):
                    for j in range(plan.blocks // plan.rank_blocks):
                        low = (j * chunks + c) * rows
                        all_ref[low : low + rows, at : at + width] = source[j * rows : (j + 1) * rows]
                for n, acc in ((1, dk_acc), (2, dv_acc)):
                    cut = n * channels + at
                    all_ref[:, cut : cut + width] = acc[...].astype(LOW)
                for n in (0, 2):
                    cut = slice(n * channels + at, n * channels + at + width)
                    total = jnp.sum(all_ref[:, cut].astype(jnp.float32), 0, keepdims=True)
                    cut = slice(n // 2 * channels + at, n // 2 * channels + at + width)
                    bias_ref[:, cut] = jnp.broadcast_to(total, (8, width))


def group_width(channels):
    return min(256, channels)


def packed_specs(length, channels):
    width = group_width(channels)
    groups = channels // width
    return [
        pl.BlockSpec((length, width), lambda g, *_, n=n: (0, n * groups + g)) for n in range(3)
    ]


def attend(qkv, random_ids, table, chunk, chunks, ranks):
    length, channels = qkv.shape[0], qkv.shape[1] // 3
    width = group_width(channels)
    groups, heads = channels // width, width // HD
    plan = Plan(chunk, chunks, ranks, length, random_ids.shape[1] // (length // BLOCK - 2), heads)
    rows = length // chunks
    return pl.pallas_call(
        functools.partial(attend_kernel, plan, 4),
        grid_spec=pltpu.PrefetchScalarGridSpec(
            num_scalar_prefetch=2,
            grid=(groups,),
            in_specs=packed_specs(length, channels),
            out_specs=[
                pl.BlockSpec((rows, width), lambda g, *_: (0, g)),
                pl.BlockSpec((1, rows // BLOCK, width), lambda g, *_: (g, 0, 0)),
            ],
        ),
        out_shape=[
            jax.ShapeDtypeStruct((rows, channels), LOW),
            jax.ShapeDtypeStruct((groups, rows // BLOCK, width), jnp.float32),
        ],
        compiler_params=pltpu.CompilerParams(vmem_limit_bytes=12 << 20),
        cost_estimate=COST,
        name="attend",
    )(table, random_ids, qkv, qkv, qkv)


def attend_back(qkv, dout, lse, random_ids, table, earlier, sums, chunk, chunks, ranks):
    length, channels = qkv.shape[0], qkv.shape[1] // 3
    width = group_width(channels)
    groups, heads = channels // width, width // HD
    plan = Plan(chunk, chunks, ranks, length, random_ids.shape[1] // (length // BLOCK - 2), heads)
    rows = length // chunks
    last = chunk == chunks - 1
    part = pl.BlockSpec((rows, width), lambda g, *_: (0, g))
    full = pl.BlockSpec((length, width), lambda g, *_: (0, g))
    sum_shape = jax.ShapeDtypeStruct((length, channels), jnp.float32)
    if last:
        bias = (8, 2 * channels)
        out_specs = [pl.BlockSpec(shape, lambda g, *_: (0, 0)) for shape in (qkv.shape, bias)]
        out_shape = [
            jax.ShapeDtypeStruct(qkv.shape, LOW),
            jax.ShapeDtypeStruct(bias, jnp.float32),
        ]
        scratch = [pltpu.VMEM((rows, width), LOW)] + [pltpu.VMEM((length, width), jnp.float32)] * 2
    else:
        out_specs = [part, full, full]
        out_shape = [jax.ShapeDtypeStruct((rows, channels), LOW), sum_shape, sum_shape]
        scratch = []
    return pl.pallas_call(
        functools.partial(attend_back_kernel, plan, 3, len(earlier), last),
        grid_spec=pltpu.PrefetchScalarGridSpec(
            num_scalar_prefetch=2,
            grid=(groups,),
            in_specs=packed_specs(length, channels)
            + [part, pl.BlockSpec((1, rows // BLOCK, width), lambda g, *_: (g, 0, 0))]
            + [part] * len(earlier)
            + [full] * len(sums),
            out_specs=out_specs,
            scratch_shapes=scratch,
        ),
        out_shape=out_shape,
        compiler_params=pltpu.CompilerParams(vmem_limit_bytes=(28 if last else 18) << 20),
        cost_estimate=COST,
        name="attend_back",
    )(table, random_ids, qkv, qkv, qkv, dout, lse, *earlier, *sums)


class Order:
    def __init__(self):
        self.token = None

    def tie(self, values):
        if self.token is None:
            return values
        values, self.token = lax.optimization_barrier((values, self.token))
        return values

    def run(self, function, *values):
        out = function(*self.tie(values))
        self.token = min(jax.tree.leaves(out), key=lambda leaf: leaf.size)
        return out


def fetch(rows, ranks):
    return [
        lax.ppermute(rows, "tensor", [((k + s) % ranks, k) for k in range(ranks)])
        for s in range(1, ranks)
    ]


def hand_over(shares, ranks):
    return [
        lax.ppermute(share, "tensor", [(k, (k + s) % ranks) for k in range(ranks)])
        for s, share in enumerate(shares, 1)
    ]


def plus(own, moved):
    for m in moved:
        own = own + m.astype(jnp.float32)
    return own


class Ring:
    def __init__(self, size):
        self.size = size
        self.chips = size // 2
        self.order = list(range(0, self.chips, 2)) + list(range(1, self.chips, 2))[::-1]
        self.ahead = self.chips // 2
        self.behind = self.chips - 1 - self.ahead

    def table(self, own_blocks):
        index = lax.axis_index("dp")
        core, chip = lax.rem(index, 2), lax.div(index, 2)
        half = lax.div(chip, 2)
        place = jnp.where(lax.rem(chip, 2) == 0, half, self.chips - 1 - half)
        first = lax.axis_index("tensor") * own_blocks
        return jnp.stack([first, core, 1 - core, place]).astype(jnp.int32)

    def shift(self, value, by):
        pairs = []
        for q in range(self.chips):
            source, target = self.order[q], self.order[(q + by) % self.chips]
            pairs += [(2 * source + c, 2 * target + c) for c in range(2)]
        return lax.ppermute(value, "dp", pairs)

    def mate(self, value):
        return lax.ppermute(value, "dp", [(i, i ^ 1) for i in range(self.size)])

    def add(self, table, kept, moved, offset, *more):
        chips, rows, columns = kept.shape
        block = rows // 2 if rows % 32 == 0 else rows

        def body(table_ref, kept_ref, moved_ref, *refs):
            *refs, out_ref = refs
            total = kept_ref[0].astype(jnp.float32) + moved_ref[0].astype(jnp.float32)
            for ref in refs:
                total = total + ref[...].astype(jnp.float32)
            out_ref[...] = total.astype(LOW)

        shard = pl.BlockSpec(
            (1, block, columns),
            lambda i, t: (lax.rem(t[PLACE] + offset + 2 * chips, chips), i, 0),
        )
        part = pl.BlockSpec((block, columns), lambda i, t: (i, 0))
        return pl.pallas_call(
            body,
            grid_spec=pltpu.PrefetchScalarGridSpec(
                num_scalar_prefetch=1,
                grid=(rows // block,),
                in_specs=[shard, shard] + [part] * len(more),
                out_specs=part,
            ),
            out_shape=jax.ShapeDtypeStruct((rows, columns), LOW),
            compiler_params=pltpu.CompilerParams(vmem_limit_bytes=8 << 20),
            cost_estimate=COST,
            name="ring_add",
        )(table, kept, moved, *more)

    def steps(self, order, table, kept, moved, results):
        def add(offset, *more):
            return order.run(
                lambda t, k, m, *more: self.add(t, k, m, offset, *more), table, kept, moved, *more
            )

        right = add(self.ahead)
        left = add(-self.behind)
        for j in range(1, self.ahead + 1):
            right = self.shift(right, 1)
            if j <= self.behind:
                left = self.shift(left, -1)
            yield
            if j < self.ahead:
                right = add(self.ahead - j, right)
            if j < self.behind:
                left = add(j - self.behind, left)
        own = add(0, right, left)
        mine, theirs = {0: own}, {0: self.mate(own)}
        right = left = own
        for j in range(1, self.ahead + 1):
            right = self.shift(right, 1)
            if j <= self.behind:
                left = self.shift(left, -1)
            yield
            right, left = order.tie((right, left))
            mine[-j], theirs[-j] = right, self.mate(right)
            if j <= self.behind:
                mine[j], theirs[j] = left, self.mate(left)
        yield
        offsets = range(-self.ahead, self.behind + 1)
        results += [side[o] for side in (mine, theirs) for o in offsets]

    def place_pieces(self, table, pieces, outs):
        shard, columns = pieces[0].shape
        chips, ahead = self.chips, self.ahead

        def body(table_ref, *refs):
            piece_refs, out_refs = refs[: 2 * chips], refs[2 * chips :]

            def put(sources):
                for i, source in enumerate(sources):
                    slot = lax.rem(table_ref[PLACE] - ahead + i + chips, chips)
                    for ref, (_, moves) in zip(out_refs, outs):
                        for own_rows, own_columns, rows, cut in moves:
                            ref[0, slot, own_rows, own_columns] = source[rows, cut].astype(
                                jnp.float32
                            )

            @pl.when(pl.program_id(0) == 0)
            def _():
                put(piece_refs[:chips])

            @pl.when(pl.program_id(0) == 1)
            def _():
                put(piece_refs[chips:])

        def target(i, t):
            return (jnp.where(i == 0, t[CORE], t[MATE]), 0, 0, 0)

        shapes = [(chips, *shape) for shape, _ in outs]
        results = pl.pallas_call(
            body,
            grid_spec=pltpu.PrefetchScalarGridSpec(
                num_scalar_prefetch=1,
                grid=(2,),
                in_specs=[
                    pl.BlockSpec(
                        (shard, columns), lambda i, w: (0, 0), pipeline_mode=pl.Buffered(1)
                    )
                ]
                * (2 * chips),
                out_specs=[pl.BlockSpec((1, *shape), target) for shape in shapes],
            ),
            out_shape=[jax.ShapeDtypeStruct((2, *shape), jnp.float32) for shape in shapes],
            compiler_params=pltpu.CompilerParams(vmem_limit_bytes=44 << 20),
            cost_estimate=COST,
            name="place_pieces",
        )(table, *pieces)
        return [out.reshape(-1, out.shape[-1]) for out in results]


class Share:
    def __init__(self, size, shape, rows, at):
        self.shard = shape[0] // size
        self.columns = shape[1]
        self.moves = []
        if self.shard <= rows:
            wide = self.columns // (rows // self.shard)
            for i in range(rows // self.shard):
                there = slice(i * self.shard, (i + 1) * self.shard)
                cut = slice(i * wide, (i + 1) * wide)
                self.moves.append((slice(0, self.shard), cut, there, slice(at, at + wide)))
            self.end = at + wide
        else:
            for i in range(self.shard // rows):
                low = at + i * self.columns
                here = slice(i * rows, (i + 1) * rows)
                self.moves.append(
                    (here, slice(0, self.columns), slice(0, rows), slice(low, low + self.columns))
                )
            self.end = at + (self.shard // rows) * self.columns


def grad_halves(table, cores, chips, rows, shares, sides):
    columns = shares[-1].end
    halves = [share.shard * chips for share in shares]
    steps = min(halves) // 128
    per = chips // steps
    arrays, where = [], []
    for lefts, rights in sides:
        place = []
        for array, low, count in [*lefts, *rights]:
            known = [n for n, other in enumerate(arrays) if other is array]
            if not known:
                arrays.append(array)
            place.append((known[0] if known else len(arrays) - 1, slice(low, low + count)))
        where.append((place[: len(lefts)], place[len(lefts) :]))

    def body(table_ref, *refs):
        refs, out_refs = refs[: len(arrays)], refs[len(arrays) :]

        @pl.loop(0, len(cores) * steps)
        def _(at):
            n_out = lax.div(at, steps)
            step = lax.rem(at, steps)
            core = table_ref[cores[0]]
            if len(cores) == 2:
                core = jnp.where(n_out == 0, core, table_ref[cores[1]])
            grads = []
            for half, (left, right) in zip(halves, where):
                tile = half // steps
                low = pl.multiple_of((core * steps + step) * tile, tile)
                grad = None
                for (n, n_rows), (m, m_rows) in zip(left, right):
                    term = dot_on(refs[n][n_rows, pl.ds(low, tile)], refs[m][m_rows, :], 0, 0)
                    grad = term if grad is None else grad + term
                grads.append(grad.astype(LOW))

            def put(ref):
                for grad, share in zip(grads, shares):
                    for n in range(per):
                        for own_rows, own_columns, there, cut in share.moves:
                            first = n * share.shard
                            ref[step * per + n, there, cut] = grad[
                                first + own_rows.start : first + own_rows.stop, own_columns
                            ]

            for n, ref in enumerate(out_refs):
                if len(out_refs) == 1:
                    put(ref)
                else:
                    pl.when(n_out == n)(functools.partial(put, ref))

    vmem = pl.BlockSpec(memory_space=pltpu.VMEM)
    return pl.pallas_call(
        body,
        in_specs=[pl.BlockSpec(memory_space=pltpu.SMEM)] + [vmem] * len(arrays),
        out_specs=[vmem] * len(cores),
        out_shape=[jax.ShapeDtypeStruct((chips, rows, columns), LOW)] * len(cores),
        compiler_params=pltpu.CompilerParams(vmem_limit_bytes=32 << 20),
        cost_estimate=COST,
        name="grad_halves",
    )(table, *arrays)


def add_low(a, b):
    return (a.astype(jnp.float32) + b.astype(jnp.float32)).astype(LOW)


def fold_sum(order, value, axis, count):
    bit = 1
    while bit < count:
        moved = lax.ppermute(value, axis, [(i, i ^ bit) for i in range(count)])
        yield
        value = order.run(jnp.add, value, moved)
        bit *= 2
    return value


def small_total(order, both, dp_only, size, ranks, results):
    lead = both.shape[0]
    both = yield from fold_sum(order, both, "tensor", ranks)
    total = yield from fold_sum(order, jnp.concatenate([both, dp_only]), "dp", size)
    results += [total[:lead], total[lead:]]


def dp_sum(order, value, size, results):
    total = yield from fold_sum(order, value, "dp", size)
    results.append(total)


def row_kernel(name, body, rows, arrays, vectors, out_types, sum_rows):
    block = min(128, rows)
    n = len(arrays) + len(vectors)

    def kernel(*refs):
        values, sums = body(*[r[...].astype(jnp.float32) for r in refs[:n]])
        for ref, value in zip(refs[n:-1], values, strict=True):
            ref[...] = value.astype(ref.dtype)
        sums = [jnp.sum(v, 0, keepdims=True) for v in sums]
        sums = jnp.concatenate(sums + [jnp.zeros_like(sums[0])] * (sum_rows - len(sums)), 0)

        @pl.when(pl.program_id(0) == 0)
        def _():
            refs[-1][...] = sums

        @pl.when(pl.program_id(0) > 0)
        def _():
            refs[-1][...] += sums

    width = vectors[0].shape[-1]
    in_specs = [
        pl.BlockSpec((block, a.shape[1]), lambda i, at=low // block: (at + i, 0))
        for a, low in arrays
    ]
    in_specs += [pl.BlockSpec((1, width), lambda i: (0, 0))] * len(vectors)
    out_specs = [pl.BlockSpec((block, w), lambda i: (i, 0)) for w, _ in out_types]
    return pl.pallas_call(
        kernel,
        grid=(rows // block,),
        in_specs=in_specs,
        out_specs=out_specs + [pl.BlockSpec((sum_rows, width), lambda i: (0, 0))],
        out_shape=[jax.ShapeDtypeStruct((rows, w), t) for w, t in out_types]
        + [jax.ShapeDtypeStruct((sum_rows, width), jnp.float32)],
        compiler_params=pltpu.CompilerParams(vmem_limit_bytes=12 << 20),
        cost_estimate=COST,
        name=name,
    )(*[a for a, _ in arrays], *vectors)


def product(x, low, rows, weights, transposed, out_type):
    inner = x.shape[1]
    outer = weights.shape[0 if transposed else 1]
    tile = min(512, outer)

    def body(x_ref, w_ref, out_ref):
        out_ref[...] = dot_on(x_ref[...], w_ref[...], 1, 1 if transposed else 0).astype(out_type)

    if transposed:
        spec = pl.BlockSpec((tile, inner), lambda i: (i, 0))
    else:
        spec = pl.BlockSpec((inner, tile), lambda i: (0, i))
    return pl.pallas_call(
        body,
        grid=(outer // tile,),
        in_specs=[pl.BlockSpec((rows, inner), lambda i: (low // rows, 0)), spec],
        out_specs=pl.BlockSpec((rows, tile), lambda i: (0, i)),
        out_shape=jax.ShapeDtypeStruct((rows, outer), out_type),
        compiler_params=pltpu.CompilerParams(vmem_limit_bytes=10 << 20),
        cost_estimate=COST,
        name="product",
    )(x, weights)


def ffn_forward(x, up_w, up_b, down_w, out_type):
    rows, width = x.shape
    units = up_w.shape[1]
    tile = min(512, units)
    steps = units // tile

    def body(x_ref, up_ref, b_ref, down_ref, act_ref, slope_ref, out_ref, acc_ref):
        step = pl.program_id(0)
        up = dot_on(x_ref[...], up_ref[...], 1, 0) + b_ref[...].astype(jnp.float32)
        act, slope = gelu_parts(up)
        act = act.astype(LOW)
        act_ref[...] = act
        slope_ref[...] = slope.astype(LOW)
        accumulate(step, steps, dot_on(act, down_ref[...], 1, 0), acc_ref, out_ref)

    part = pl.BlockSpec((rows, tile), lambda i: (0, i))
    whole = pl.BlockSpec((rows, width), lambda i: (0, 0))
    return pl.pallas_call(
        body,
        grid=(steps,),
        in_specs=[
            whole,
            pl.BlockSpec((width, tile), lambda i: (0, i)),
            pl.BlockSpec((1, tile), lambda i: (0, i)),
            pl.BlockSpec((tile, width), lambda i: (i, 0)),
        ],
        out_specs=[part, part, whole],
        out_shape=[jax.ShapeDtypeStruct((rows, units), LOW)] * 2
        + [jax.ShapeDtypeStruct((rows, width), out_type)],
        scratch_shapes=[pltpu.VMEM((rows, width), jnp.float32)],
        compiler_params=pltpu.CompilerParams(vmem_limit_bytes=16 << 20),
        cost_estimate=COST,
        name="ffn_forward",
    )(x, up_w, up_b, down_w)


def ffn_back(grad, slope, down_w, up_w, out_type):
    rows, width = grad.shape
    units = up_w.shape[1]
    tile = min(512, units)
    steps = units // tile

    def body(g_ref, slope_ref, down_ref, up_ref, dup_ref, out_ref, acc_ref):
        step = pl.program_id(0)
        dact = dot_on(g_ref[...], down_ref[...], 1, 1)
        dup = (dact * slope_ref[...].astype(jnp.float32)).astype(LOW)
        dup_ref[...] = dup
        accumulate(step, steps, dot_on(dup, up_ref[...], 1, 1), acc_ref, out_ref)

    part = pl.BlockSpec((rows, tile), lambda i: (0, i))
    whole = pl.BlockSpec((rows, width), lambda i: (0, 0))
    return pl.pallas_call(
        body,
        grid=(steps,),
        in_specs=[
            whole,
            part,
            pl.BlockSpec((tile, width), lambda i: (i, 0)),
            pl.BlockSpec((width, tile), lambda i: (0, i)),
        ],
        out_specs=[part, whole],
        out_shape=[
            jax.ShapeDtypeStruct((rows, units), LOW),
            jax.ShapeDtypeStruct((rows, width), out_type),
        ],
        scratch_shapes=[pltpu.VMEM((rows, width), jnp.float32)],
        compiler_params=pltpu.CompilerParams(vmem_limit_bytes=16 << 20),
        cost_estimate=COST,
        name="ffn_back",
    )(grad, slope, down_w, up_w)


def accumulate(step, steps, term, acc_ref, out_ref):
    if steps == 1:
        out_ref[...] = term.astype(out_ref.dtype)
        return

    @pl.when(step == 0)
    def _():
        acc_ref[...] = term

    @pl.when((step > 0) & (step < steps - 1))
    def _():
        acc_ref[...] += term

    @pl.when(step == steps - 1)
    def _():
        out_ref[...] = (acc_ref[...] + term).astype(out_ref.dtype)


def mean(rows):
    return jnp.mean(rows, -1, keepdims=True)


def normalise(rows):
    centre = rows - mean(rows)
    inverse = lax.rsqrt(mean(centre * centre) + EPS)
    return centre * inverse, inverse


def norm_back(grad, normed, inverse, gain):
    scaled = grad * gain
    return inverse * (scaled - mean(scaled) - normed * mean(scaled * normed))


def gelu_parts(values):
    square = values * values
    rate = -2.0 * GELU_C
    gate = 1.0 / (1.0 + jnp.exp(values * (rate + rate * 0.044715 * square)))
    output = values * gate
    slope = gate + output * (1.0 - gate) * (2.0 * GELU_C + 6.0 * GELU_C * 0.044715 * square)
    return output, slope


def dot(a, b):
    return jnp.dot(a, b, preferred_element_type=jnp.float32)


def dot_nt(a, b):
    return dot_on(a, b, 1, 1)


def dot_tn(a, b):
    return dot_on(a, b, 0, 0)


def column_sums(rows):
    ones = jnp.ones((8, rows.shape[0]), LOW)
    return dot(ones, rows)[0]


def local(
    dp_size,
    ranks,
    hidden_in,
    query_w,
    key_w,
    value_w,
    query_b,
    value_b,
    out_w,
    out_b,
    gain_attn,
    shift_attn,
    up_w,
    up_b,
    down_w,
    down_b,
    gain_ffn,
    shift_ffn,
    random_blocks,
    cotangent,
):
    own_rows, seqs_here, width = hidden_in.shape
    channels, hidden_units = query_w.shape[1], up_w.shape[1]
    length = own_rows * ranks
    chunks = CHUNKS
    piece = own_rows // chunks
    every = range(chunks)
    others = range(1, ranks)
    ring = Ring(dp_size)
    rows_in = hidden_in.reshape(own_rows, width)
    grad_out = cotangent.reshape(own_rows, width)
    lows = [c * piece for c in every]
    order = Order()
    run, tie = order.run, order.tie

    far_rows = fetch(rows_in, ranks)

    def project(x, *w):
        return (dot(x, w[0]) + w[1]).astype(LOW)

    def set_up(ids, q_w, k_w, v_w, q_b, v_b, *vectors):
        return (
            ring.table(own_rows // BLOCK),
            ids.reshape(ids.shape[0], -1),
            jnp.concatenate([q_w, k_w, v_w], 1),
            jnp.concatenate([q_b, jnp.zeros_like(q_b), v_b]).astype(jnp.float32),
            [v.reshape(1, -1) for v in vectors],
        )

    table, random_ids, qkv_w, qkv_b, vectors = run(
        set_up,
        random_blocks,
        query_w,
        key_w,
        value_w,
        query_b,
        value_b,
        out_b,
        gain_attn,
        shift_attn,
        up_b,
        down_b,
        gain_ffn,
        shift_ffn,
    )
    out_b, gain_attn, shift_attn, up_b, down_b, gain_ffn, shift_ffn = vectors
    near = run(project, rows_in, qkv_w, qkv_b)
    qkv = run(
        lambda n, w, b, *x: jnp.concatenate([n] + [project(p, w, b) for p in x], 0),
        near,
        qkv_w,
        qkv_b,
        *far_rows,
    )

    contexts, lses, attn_moved, attn_own = [], [], [], []
    for c in every:
        context, lse = run(lambda v: attend(v, random_ids, table, c, chunks, ranks), qkv)
        contexts.append(context)
        lses.append(lse)
        shares = [
            run(lambda x: product(x, j * piece, piece, out_w, False, LOW), context) for j in others
        ]
        attn_moved.append(hand_over(shares, ranks))
    for c in every:
        attn_own.append(
            run(lambda x: product(x, 0, piece, out_w, False, jnp.float32), contexts[c])
        )

    low_rows = (width, LOW)

    def norm_one(low, own, *moved):
        def body(*values):
            *terms, source, bias, gain, shift = values
            attn_out = functools.reduce(jnp.add, terms)
            resid = source + attn_out + bias
            normed, inverse = normalise(resid)
            hidden = gain * normed + shift
            inverse = jnp.broadcast_to(inverse, (inverse.shape[0], 128))
            return [hidden, normed, inverse], [resid * resid, attn_out * attn_out]

        return row_kernel(
            "norm_one",
            body,
            piece,
            [(own, 0)] + [(m, 0) for m in moved] + [(rows_in, low)],
            [out_b, gain_attn, shift_attn],
            [low_rows, low_rows, (128, jnp.float32)],
            8,
        )

    x, n1, i1, squares, acts, slopes, mlp_moved, mlp_own = ([] for _ in range(8))
    for c in every:
        low, n, i, sq = run(functools.partial(norm_one, lows[c]), attn_own[c], *attn_moved[c])
        n1.append(n)
        i1.append(i)
        squares.append(sq)
        x.append([low] + fetch(low, ranks))
        act, slope, own = run(lambda v: ffn_forward(v, up_w, up_b, down_w, jnp.float32), low)
        acts.append([act])
        slopes.append([slope])
        mlp_own.append(own)
    for c in every:
        shares = []
        for j in others:
            act, slope, share = run(lambda v: ffn_forward(v, up_w, up_b, down_w, LOW), x[c][j])
            acts[c].append(act)
            slopes[c].append(slope)
            shares.append(share)
        mlp_moved.append(hand_over(shares, ranks))

    def norm_two(low, own, h, *moved):
        def body(*values):
            *terms, before, g, bias, gain, shift = values
            mlp_out = functools.reduce(jnp.add, terms)
            normed, inverse = normalise(before + mlp_out + bias)
            back = norm_back(g, normed, inverse, gain)
            sums = [back, g * normed, g, mlp_out * mlp_out]
            return [back, gain * normed + shift], sums

        return row_kernel(
            "norm_two",
            body,
            piece,
            [(own, 0)] + [(m, 0) for m in moved] + [(h, 0), (grad_out, low)],
            [down_b, gain_ffn, shift_ffn],
            [low_rows, low_rows],
            8,
        )

    dmlp, layer_out, sums2 = [], [], []
    for c in every:
        low, out, sums = run(
            functools.partial(norm_two, lows[c]), mlp_own[c], x[c][0], *mlp_moved[c]
        )
        layer_out.append(out)
        sums2.append(sums)
        dmlp.append([low] + fetch(low, ranks))

    dups, dhid_moved, dhid_own = [], [], []
    for c in every:
        dup, own = run(
            lambda d, s: ffn_back(d, s, down_w, up_w, jnp.float32), dmlp[c][0], slopes[c][0]
        )
        dups.append([dup])
        dhid_own.append(own)
    for c in every:
        shares = []
        for j in others:
            dup, share = run(
                lambda d, s: ffn_back(d, s, down_w, up_w, LOW), dmlp[c][j], slopes[c][j]
            )
            dups[c].append(dup)
            shares.append(share)
        dhid_moved.append(hand_over(shares, ranks))

    under_way = []

    def advance(*names):
        for name in names or [n for n, _ in under_way]:
            for entry in [e for e in under_way if e[0] == name]:
                if next(entry[1], "end") == "end":
                    under_way.remove(entry)

    def begin(name, rows, shares, sides, between):
        results = []
        leaves, tree = jax.tree.flatten(sides)
        arrays = list({id(x): x for x in leaves if not isinstance(x, int)}.values())

        def halves(*cores):
            def call(*tied):
                known = {id(x): t for x, t in zip(arrays, tied)}
                found = [x if isinstance(x, int) else known[id(x)] for x in leaves]
                sides = jax.tree.unflatten(tree, found)
                return grad_halves(table, cores, ring.chips, rows, shares, sides)

            return run(call, *arrays)

        if between is None:
            given, kept = halves(MATE, CORE)
            moved = ring.mate(given)
        else:
            moved = ring.mate(halves(MATE)[0])
            between()
            (kept,) = halves(CORE)
        under_way.append((name, ring.steps(order, table, kept, moved, results)))
        return results

    def pieces_of(parts):
        return [(p, 0, piece) for part in parts for p in part]

    ffn_rows = hidden_units // dp_size
    down_share = Share(dp_size, (hidden_units, width), ffn_rows, 0)
    up_share = Share(dp_size, (width, hidden_units), ffn_rows, down_share.end)
    ffn = begin(
        "ffn",
        ffn_rows,
        [down_share, up_share],
        [
            (pieces_of(acts), pieces_of(dmlp)),
            (pieces_of(x), pieces_of(dups)),
        ],
        None,
    )

    def norm_one_back(own, d2, n, i, *moved):
        def body(*values):
            *terms, normed, inverse, gain = values
            dhidden = functools.reduce(jnp.add, terms)
            back = norm_back(dhidden, normed, inverse[:, :1], gain)
            return [back], [back, dhidden * normed, dhidden]

        return row_kernel(
            "norm_one_back",
            body,
            piece,
            [(a, 0) for a in (own, *moved, d2, n, i)],
            [gain_attn],
            [low_rows],
            8,
        )

    dattn, sums1, dcontexts = [], [], []
    for c in every:
        low, sums = run(
            norm_one_back, dhid_own[c], dmlp[c][0], n1[c], i1[c], *dhid_moved[c]
        )
        sums1.append(sums)
        dattn.append([low] + fetch(low, ranks))
        advance("ffn")
    for c in every:
        dcontexts.append(run(lambda d: product(d, 0, piece, out_w, True, LOW), dattn[c][0]))
    grad_up_b = run(
        lambda *d: functools.reduce(jnp.add, [column_sums(p) for p in d]),
        *[p for part in dups for p in part],
    )

    def gather_sums(squares, one, two):
        one, two, squares = sum(one), sum(two), sum(squares)
        scalars = jnp.stack([jnp.sum(squares[0]), jnp.sum(squares[1]), jnp.sum(two[3])])
        rows = [one[i] for i in range(3)] + [two[i] for i in range(3)]
        return jnp.concatenate(rows + [jnp.pad(scalars, (0, 125))])

    small = []
    both = run(gather_sums, squares, sums1, sums2)
    under_way.append(("small", small_total(order, both, grad_up_b, dp_size, ranks, small)))

    dq_parts, sums = [], []
    for c in every:
        dcontext = run(
            lambda near, *far: jnp.concatenate(
                [near] + [product(d, 0, piece, out_w, True, LOW) for d in far], 0
            ),
            dcontexts[c],
            *dattn[c][1:],
        )
        advance("ffn", "small")
        dq, *sums = run(
            lambda v, d, l, e, s: jax.tree.leaves(
                attend_back(v, d, l, random_ids, table, e, s, c, chunks, ranks)
            ),
            qkv,
            dcontext,
            lses[c],
            dq_parts,
            sums,
        )
        dq_parts.append(dq)
        if c < chunks - 1:
            advance("ffn", "small")
    dqkv, bias_sums = dq, sums[0]

    attn_rows = width // dp_size
    attn_shares = [Share(dp_size, (width, 3 * channels), attn_rows, 0)]
    attn_sides = [
        (
            [(x, 0, own_rows) for x in [rows_in] + far_rows],
            [(dqkv, j * own_rows, own_rows) for j in range(ranks)],
        )
    ]
    with_out = channels % 256 == 0
    if with_out:
        attn_shares.append(Share(dp_size, (channels, width), attn_rows, attn_shares[0].end))
        attn_sides.append(
            (
                [(contexts[c], j * piece, piece) for c in every for j in range(ranks)],
                [(dattn[c][j], 0, piece) for c in every for j in range(ranks)],
            )
        )
    dinput_moved = []

    def send_dinput():
        shares = [
            run(lambda d: product(d, j * own_rows, own_rows, qkv_w, True, LOW), dqkv)
            for j in others
        ]
        dinput_moved.extend(hand_over(shares, ranks))

    attn = begin("attn", attn_rows, attn_shares, attn_sides, send_dinput)
    qkv_b_sums = []
    advance("attn", "ffn")
    under_way.append(
        ("qkv_b", dp_sum(order, bias_sums[0], dp_size, qkv_b_sums))
    )
    advance("attn")
    dinput_own = run(lambda d: product(d, 0, own_rows, qkv_w, True, jnp.float32), dqkv)
    advance("ffn", "attn", "qkv_b")
    grad_input = run(
        lambda own, d, *m: (plus(own, m) + jnp.concatenate(d, 0)).astype(LOW),
        dinput_own,
        [d[0] for d in dattn],
        *dinput_moved,
    )
    totals = {}
    entries = float(own_rows * ranks * dp_size * seqs_here * width)

    def spread(both):
        vectors = [both[i * width : (i + 1) * width] for i in range(6)]
        return vectors, jnp.sqrt(both[6 * width : 6 * width + 3] / entries)

    ffn_outs = [((g.shard, g.columns), g.moves) for g in (down_share, up_share)]
    while under_way:
        advance()
        names = {n for n, _ in under_way}
        if "ffn" not in names and "ffn" not in totals:
            totals["ffn"] = run(lambda *p: ring.place_pieces(table, p, ffn_outs), *ffn)
        if "small" not in names and "small" not in totals:
            totals["small"] = run(spread, small[0])
    everything = slice(0, attn_rows)
    attn_outs = []
    for i in range(3):
        cut = slice(i * channels, (i + 1) * channels)
        attn_outs.append(
            ((attn_rows, channels), [(everything, slice(0, channels), everything, cut)])
        )
    if with_out:
        attn_outs.append(((attn_shares[1].shard, width), attn_shares[1].moves))
    grad_q, grad_k, grad_v, *rest = run(lambda *p: ring.place_pieces(table, p, attn_outs), *attn)
    if with_out:
        (grad_out_w,) = rest
    else:
        partial = sum(
            dot_tn(contexts[c], jnp.concatenate(dattn[c], 0)) for c in every
        )
        grad_out_w = lax.psum(partial.astype(LOW), "dp").astype(jnp.float32)
    grad_down_w, grad_up_w = totals["ffn"]
    vectors, rms_stats = totals["small"]
    biases = [qkv_b_sums[0][:channels], qkv_b_sums[0][channels:], small[1]]
    shape = hidden_in.shape
    return (
        jnp.concatenate(layer_out, 0).reshape(shape),
        grad_input.reshape(shape),
        grad_q,
        grad_k,
        grad_v,
        biases[0],
        biases[1],
        grad_out_w,
        vectors[0],
        vectors[1],
        vectors[2],
        grad_up_w,
        biases[2],
        grad_down_w,
        vectors[3],
        vectors[4],
        vectors[5],
        rms_stats,
    )


def solution(mesh):
    rows = P("tensor", "dp", None)
    columns, split, whole = P(None, "tensor"), P("tensor"), P()
    first = P("tensor", None)
    return jax.shard_map(
        functools.partial(local, mesh.shape["dp"], mesh.shape["tensor"]),
        mesh=mesh,
        in_specs=(
            rows,
            columns,
            columns,
            columns,
            split,
            split,
            first,
            whole,
            whole,
            whole,
            columns,
            split,
            first,
            whole,
            whole,
            whole,
            P("tensor", None, None),
            rows,
        ),
        out_specs=(
            rows,
            rows,
            columns,
            columns,
            columns,
            split,
            split,
            first,
            whole,
            whole,
            whole,
            columns,
            split,
            first,
            whole,
            whole,
            whole,
            whole,
        ),
        check_vma=False,
    )
```

```python
import functools
import math

import jax
import jax.numpy as jnp
from jax import lax
from jax.experimental import pallas as pl
from jax.experimental.pallas import tpu as pltpu
from jax.sharding import PartitionSpec as P

HD = 64
BLOCK = 64
NEG = -1e30
EPS = 1e-12
GELU_C = math.sqrt(2.0 / math.pi)
CHUNKS = 2
LOW = jnp.bfloat16
FIRST, CORE, MATE, PLACE = range(4)
COST = pl.CostEstimate(flops=1024, bytes_accessed=1024, transcendentals=0)


def dot_on(left, right, left_dim, right_dim):
    return lax.dot_general(
        left,
        right,
        (((left_dim,), (right_dim,)), ((), ())),
        preferred_element_type=jnp.float32,
    )


def lane_masks(width, value):
    lane = lax.broadcasted_iota(jnp.int32, (1, width), 1) // HD
    return [jnp.where(lane == h, value, 0.0).astype(LOW) for h in range(width // HD)]


def stack_heads(rows, masks):
    return jnp.concatenate([rows * m for m in masks], 0)


def unstack_heads(stacked, heads):
    lane = lax.broadcasted_iota(jnp.int32, (1, stacked.shape[1]), 1) // HD
    out = stacked[:BLOCK]
    for h in range(1, heads):
        out = jnp.where(lane == h, stacked[h * BLOCK : (h + 1) * BLOCK], out)
    return out


def block_at(index):
    return pl.ds(pl.multiple_of(index * BLOCK, BLOCK), BLOCK)


class Plan:
    def __init__(self, chunk, chunks, ranks, length, rand, heads):
        self.blocks = length // BLOCK
        self.rank_blocks = self.blocks // ranks
        self.chunk_blocks = self.rank_blocks // chunks
        self.chunk = chunk
        self.rand = rand
        self.heads = heads
        taken = [
            j * self.rank_blocks + chunk * self.chunk_blocks + r
            for j in range(ranks)
            for r in range(self.chunk_blocks)
        ]
        self.ends = [b for b in taken if b in (0, self.blocks - 1)]
        middles = [b for b in taken if b not in self.ends]
        self.ranges = []
        for b in middles:
            if self.ranges and self.ranges[-1][1] == b:
                self.ranges[-1][1] = b + 1
            else:
                self.ranges.append([b, b + 1])

    def local(self, block, first):
        return lax.rem(block - first + self.blocks, self.blocks)

    def inner(self, local):
        part = lax.div(local, self.rank_blocks)
        rest = local - part * self.rank_blocks
        return part * self.chunk_blocks + rest - self.chunk * self.chunk_blocks

    def fixed(self, block, first):
        wanted = (jnp.int32(0), jnp.int32(self.blocks - 1), block - 1, block, block + 1)
        return [self.local(w, first) for w in wanted]

    def random(self, rb_ref, group, block, first):
        return [
            [
                self.local(rb_ref[group * self.heads + h, (block - 1) * self.rand + r], first)
                for h in range(self.heads)
            ]
            for r in range(self.rand)
        ]

    def run(self, one, unroll):
        for low, high in self.ranges:
            count = high - low
            main = count - count % unroll
            if main > unroll:

                @pl.loop(0, main // unroll)
                def _(step, low=low):
                    for u in range(unroll):
                        one(low + step * unroll + u)
            else:
                main = 0
            for x in range(main, count):
                one(jnp.int32(low + x))


def pick_tiles(ref, fixed, rands):
    width = ref.shape[1]
    column = min(128, width)
    per = column // HD
    lane = lax.broadcasted_iota(jnp.int32, (1, column), 1) // HD
    parts = [ref[block_at(f), :] for f in fixed]
    for per_head in rands:
        columns = []
        for c in range(width // column):
            tile = None
            for p in range(per):
                x = ref[block_at(per_head[c * per + p]), c * column : (c + 1) * column]
                tile = x if tile is None else jnp.where(lane == p, x, tile)
            columns.append(tile)
        parts.append(jnp.concatenate(columns, 1) if len(columns) > 1 else columns[0])
    return jnp.concatenate(parts, 0)


def attend_kernel(plan, unroll, table_ref, rb_ref, q_ref, k_ref, v_ref, o_ref, lse_ref):
    group = pl.program_id(0)
    first = table_ref[FIRST]
    heads = plan.heads
    masks = lane_masks(q_ref.shape[1], HD**-0.5)

    def finish(scores, values, place):
        top = jnp.max(scores, 1, keepdims=True)
        weights = jnp.exp(scores - top)
        total = jnp.sum(weights, 1, keepdims=True)
        out = dot_on(weights.astype(LOW), values, 1, 0) * (1.0 / total)
        o_ref[block_at(place), :] = unstack_heads(out, heads).astype(LOW)
        wide = jnp.broadcast_to(top + jnp.log(total), (heads * BLOCK, 128))
        lse_ref[0, pl.ds(place, 1), :] = jnp.transpose(wide)[0:1, :]

    def one(block):
        fixed = plan.fixed(block, first)
        rands = plan.random(rb_ref, group, block, first)
        queries = stack_heads(q_ref[block_at(fixed[3]), :], masks)
        scores = dot_on(queries, pick_tiles(k_ref, fixed, rands), 1, 1)
        lane = lax.broadcasted_iota(jnp.int32, (1, 2 * BLOCK), 1)
        drop = ((block == 1) & (lane < BLOCK)) | (
            (block == plan.blocks - 2) & (lane >= BLOCK)
        )
        scores = jnp.concatenate(
            [jnp.where(drop, NEG, scores[:, : 2 * BLOCK]), scores[:, 2 * BLOCK :]], 1
        )
        finish(scores, pick_tiles(v_ref, fixed, rands), plan.inner(fixed[3]))

    plan.run(one, unroll)
    for b in plan.ends:
        local = plan.local(jnp.int32(b), first)
        queries = stack_heads(q_ref[block_at(local), :], masks)
        finish(dot_on(queries, k_ref[...], 1, 1), v_ref[...], plan.inner(local))


def attend_back_kernel(plan, unroll, earlier, last, table_ref, rb_ref, q_ref, k_ref, v_ref, *refs):
    do_ref, lse_ref, *refs = refs
    dq_in, refs = refs[:earlier], refs[earlier:]
    if earlier:
        dk_in, dv_in, *refs = refs
    if last:
        all_ref, bias_ref, dq_ref, dk_acc, dv_acc = refs
    else:
        dq_ref, dk_acc, dv_acc = refs
    group = pl.program_id(0)
    first = table_ref[FIRST]
    heads = plan.heads
    width = q_ref.shape[1]
    query_masks, out_masks = lane_masks(width, HD**-0.5), lane_masks(width, 1.0)
    column = min(128, width)
    per = column // HD
    lane = lax.broadcasted_iota(jnp.int32, (1, column), 1) // HD
    if earlier:
        dk_acc[...] = dk_in[...]
        dv_acc[...] = dv_in[...]
    else:
        dk_acc[...] = jnp.zeros_like(dk_acc)
        dv_acc[...] = jnp.zeros_like(dv_acc)

    def core(scores, keys, values, queries, douts, place):
        probs = jnp.exp(scores - lse_ref[0, pl.ds(place, 1), :])
        dprobs = dot_on(values, douts, 1, 1)
        row_dot = jnp.sum(probs * dprobs, 0, keepdims=True)
        dscores = (probs * (dprobs - row_dot)).astype(LOW)
        dv = dot_on(probs.astype(LOW), douts, 1, 0)
        dk = dot_on(dscores, queries, 1, 0)
        dq = unstack_heads(dot_on(dscores, keys, 0, 0), heads) * (HD**-0.5)
        dq_ref[block_at(place), :] = dq.astype(LOW)
        return dk, dv

    def add_tiles(acc, value, fixed, rands):
        for n, f in enumerate(fixed):
            acc[block_at(f), :] += value[n * BLOCK : (n + 1) * BLOCK]
        for r, per_head in enumerate(rands):
            tile = value[(5 + r) * BLOCK : (6 + r) * BLOCK]
            for h in range(heads):
                c = h // per
                cut = slice(c * column, (c + 1) * column)
                acc[block_at(per_head[h]), cut] += jnp.where(lane == h % per, tile[:, cut], 0.0)

    def one(block):
        fixed = plan.fixed(block, first)
        rands = plan.random(rb_ref, group, block, first)
        place = plan.inner(fixed[3])
        queries = stack_heads(q_ref[block_at(fixed[3]), :], query_masks)
        douts = stack_heads(do_ref[block_at(place), :], out_masks)
        keys = pick_tiles(k_ref, fixed, rands)
        values = pick_tiles(v_ref, fixed, rands)
        scores = dot_on(keys, queries, 1, 1)
        scores = jnp.concatenate(
            [
                jnp.where(block == 1, NEG, scores[:BLOCK]),
                jnp.where(block == plan.blocks - 2, NEG, scores[BLOCK : 2 * BLOCK]),
                scores[2 * BLOCK :],
            ],
            0,
        )
        dk, dv = core(scores, keys, values, queries, douts, place)
        add_tiles(dk_acc, dk, fixed, rands)
        add_tiles(dv_acc, dv, fixed, rands)

    for b in plan.ends:
        local = plan.local(jnp.int32(b), first)
        place = plan.inner(local)
        queries = stack_heads(q_ref[block_at(local), :], query_masks)
        douts = stack_heads(do_ref[block_at(place), :], out_masks)
        scores = dot_on(k_ref[...], queries, 1, 1)
        dk, dv = core(scores, k_ref[...], v_ref[...], queries, douts, place)
        dk_acc[...] += dk
        dv_acc[...] += dv
    plan.run(one, unroll)
    if last:
        channels = all_ref.shape[1] // 3
        rows = plan.chunk_blocks * BLOCK
        chunks = earlier + 1
        for at in range(0, channels, width):

            @pl.when(group * width == at)
            def _(at=at):
                for c, source in enumerate([*dq_in, dq_ref]):
                    for j in range(plan.blocks // plan.rank_blocks):
                        low = (j * chunks + c) * rows
                        all_ref[low : low + rows, at : at + width] = source[j * rows : (j + 1) * rows]
                for n, acc in ((1, dk_acc), (2, dv_acc)):
                    cut = n * channels + at
                    all_ref[:, cut : cut + width] = acc[...].astype(LOW)
                for n in (0, 2):
                    cut = slice(n * channels + at, n * channels + at + width)
                    total = jnp.sum(all_ref[:, cut].astype(jnp.float32), 0, keepdims=True)
                    cut = slice(n // 2 * channels + at, n // 2 * channels + at + width)
                    bias_ref[:, cut] = jnp.broadcast_to(total, (8, width))


def group_width(channels):
    return min(256, channels)


def packed_specs(length, channels):
    width = group_width(channels)
    groups = channels // width
    return [
        pl.BlockSpec((length, width), lambda g, *_, n=n: (0, n * groups + g)) for n in range(3)
    ]


def attend(qkv, random_ids, table, chunk, chunks, ranks):
    length, channels = qkv.shape[0], qkv.shape[1] // 3
    width = group_width(channels)
    groups, heads = channels // width, width // HD
    plan = Plan(chunk, chunks, ranks, length, random_ids.shape[1] // (length // BLOCK - 2), heads)
    rows = length // chunks
    return pl.pallas_call(
        functools.partial(attend_kernel, plan, 4),
        grid_spec=pltpu.PrefetchScalarGridSpec(
            num_scalar_prefetch=2,
            grid=(groups,),
            in_specs=packed_specs(length, channels),
            out_specs=[
                pl.BlockSpec((rows, width), lambda g, *_: (0, g)),
                pl.BlockSpec((1, rows // BLOCK, width), lambda g, *_: (g, 0, 0)),
            ],
        ),
        out_shape=[
            jax.ShapeDtypeStruct((rows, channels), LOW),
            jax.ShapeDtypeStruct((groups, rows // BLOCK, width), jnp.float32),
        ],
        compiler_params=pltpu.CompilerParams(vmem_limit_bytes=12 << 20),
        cost_estimate=COST,
        name="attend",
    )(table, random_ids, qkv, qkv, qkv)


def attend_back(qkv, dout, lse, random_ids, table, earlier, sums, chunk, chunks, ranks):
    length, channels = qkv.shape[0], qkv.shape[1] // 3
    width = group_width(channels)
    groups, heads = channels // width, width // HD
    plan = Plan(chunk, chunks, ranks, length, random_ids.shape[1] // (length // BLOCK - 2), heads)
    rows = length // chunks
    last = chunk == chunks - 1
    part = pl.BlockSpec((rows, width), lambda g, *_: (0, g))
    full = pl.BlockSpec((length, width), lambda g, *_: (0, g))
    sum_shape = jax.ShapeDtypeStruct((length, channels), jnp.float32)
    if last:
        bias = (8, 2 * channels)
        out_specs = [pl.BlockSpec(shape, lambda g, *_: (0, 0)) for shape in (qkv.shape, bias)]
        out_shape = [
            jax.ShapeDtypeStruct(qkv.shape, LOW),
            jax.ShapeDtypeStruct(bias, jnp.float32),
        ]
        scratch = [pltpu.VMEM((rows, width), LOW)] + [pltpu.VMEM((length, width), jnp.float32)] * 2
    else:
        out_specs = [part, full, full]
        out_shape = [jax.ShapeDtypeStruct((rows, channels), LOW), sum_shape, sum_shape]
        scratch = []
    return pl.pallas_call(
        functools.partial(attend_back_kernel, plan, 3, len(earlier), last),
        grid_spec=pltpu.PrefetchScalarGridSpec(
            num_scalar_prefetch=2,
            grid=(groups,),
            in_specs=packed_specs(length, channels)
            + [part, pl.BlockSpec((1, rows // BLOCK, width), lambda g, *_: (g, 0, 0))]
            + [part] * len(earlier)
            + [full] * len(sums),
            out_specs=out_specs,
            scratch_shapes=scratch,
        ),
        out_shape=out_shape,
        compiler_params=pltpu.CompilerParams(vmem_limit_bytes=(28 if last else 18) << 20),
        cost_estimate=COST,
        name="attend_back",
    )(table, random_ids, qkv, qkv, qkv, dout, lse, *earlier, *sums)


class Order:
    def __init__(self):
        self.token = None

    def tie(self, values):
        if self.token is None:
            return values
        values, self.token = lax.optimization_barrier((values, self.token))
        return values

    def run(self, function, *values):
        out = function(*self.tie(values))
        self.token = min(jax.tree.leaves(out), key=lambda leaf: leaf.size)
        return out


def fetch(rows, ranks):
    return [
        lax.ppermute(rows, "tensor", [((k + s) % ranks, k) for k in range(ranks)])
        for s in range(1, ranks)
    ]


def hand_over(shares, ranks):
    return [
        lax.ppermute(share, "tensor", [(k, (k + s) % ranks) for k in range(ranks)])
        for s, share in enumerate(shares, 1)
    ]


def plus(own, moved):
    for m in moved:
        own = own + m.astype(jnp.float32)
    return own


class Ring:
    def __init__(self, size):
        self.size = size
        self.chips = size // 2
        self.order = list(range(0, self.chips, 2)) + list(range(1, self.chips, 2))[::-1]
        self.ahead = self.chips // 2
        self.behind = self.chips - 1 - self.ahead

    def table(self, own_blocks):
        index = lax.axis_index("dp")
        core, chip = lax.rem(index, 2), lax.div(index, 2)
        half = lax.div(chip, 2)
        place = jnp.where(lax.rem(chip, 2) == 0, half, self.chips - 1 - half)
        first = lax.axis_index("tensor") * own_blocks
        return jnp.stack([first, core, 1 - core, place]).astype(jnp.int32)

    def shift(self, value, by):
        pairs = []
        for q in range(self.chips):
            source, target = self.order[q], self.order[(q + by) % self.chips]
            pairs += [(2 * source + c, 2 * target + c) for c in range(2)]
        return lax.ppermute(value, "dp", pairs)

    def mate(self, value):
        return lax.ppermute(value, "dp", [(i, i ^ 1) for i in range(self.size)])

    def add(self, table, kept, moved, offset, part, pair, *more):
        chips, rows, columns = kept.shape
        block = rows // 2 if rows % 32 == 0 else rows
        steps = rows // block if part is None else 1

        def body(table_ref, kept_ref, moved_ref, *refs):
            *refs, out_ref = refs
            total = kept_ref[0].astype(jnp.float32) + moved_ref[0].astype(jnp.float32)
            for ref, (array, half) in zip(refs, more):
                term = ref[...].astype(jnp.float32)
                if array.shape[0] < rows and part is None:
                    term = jnp.where(pl.program_id(0) == half, term, 0.0)
                total = total + term
            out_ref[...] = total.astype(LOW)
            if pair is not None and part != 1:

                @pl.when(pl.program_id(0) == 0)
                def _():
                    out_ref[0:16, pair:] = two_parts(total[0:8, pair:] + total[8:16, pair:])

        shard = pl.BlockSpec(
            (1, block, columns),
            lambda i, t: (lax.rem(t[PLACE] + offset + 2 * chips, chips), i + (part or 0), 0),
        )
        each = pl.BlockSpec((block, columns), lambda i, t: (i, 0))
        fixed = pl.BlockSpec((block, columns), lambda i, t: (0, 0))
        return pl.pallas_call(
            body,
            grid_spec=pltpu.PrefetchScalarGridSpec(
                num_scalar_prefetch=1,
                grid=(steps,),
                in_specs=[shard, shard] + [fixed if a.shape[0] < rows else each for a, _ in more],
                out_specs=each,
            ),
            out_shape=jax.ShapeDtypeStruct((block * steps, columns), LOW),
            compiler_params=pltpu.CompilerParams(vmem_limit_bytes=8 << 20),
            cost_estimate=COST,
            name="ring_add",
        )(table, kept, moved, *[a for a, _ in more])

    def steps(self, order, table, kept, moved, results, pair=None):
        ahead = self.ahead
        rows = kept.shape[1]
        split = rows % 32 == 0

        def add(offset, part, *more):
            halves = [h for _, h in more]
            return order.run(
                lambda t, k, m, *more: self.add(t, k, m, offset, part, pair, *zip(more, halves)),
                table,
                kept,
                moved,
                *[a for a, _ in more],
            )

        right = add(ahead, 0 if split else None)
        left = add(-ahead, 1) if split else None
        for j in range(1, ahead + 1):
            right = self.shift(right, 1)
            left = None if left is None else self.shift(left, -1)
            yield
            if j < ahead:
                right = add(ahead - j, None, (right, 0))
                left = add(j - ahead, None, *([] if left is None else [(left, 1)]))
        own = add(0, None, (right, 0), (left, 0))
        mine, theirs = {0: own}, {0: order.tie(self.mate(own))}
        right = left = own
        for j in range(1, ahead + 1):
            if j == ahead and split:
                half = rows // 2
                right, left = order.run(lambda r, l: (r[:half], l[half:]), right, left)
            right = self.shift(right, 1)
            left = self.shift(left, -1) if j < ahead or split else None
            yield
            right, left = order.tie((right, left))
            mine[-j], mine[j] = right, left
            theirs[-j] = self.mate(right)
            theirs[j] = None if left is None else self.mate(left)
        offsets = range(-ahead, ahead + 1)
        results += [[side[o] for o in offsets] for side in (mine, theirs)]

    def place_pieces(self, table, pieces, outs):
        chips, ahead = self.chips, self.ahead
        size = pieces[0][ahead].shape[0]
        arrays, places = [], []
        for side in pieces:
            entries = []
            for offset, array in zip(range(-ahead, ahead + 1), side):
                if array is not None:
                    first = size - array.shape[0] if offset == ahead else 0
                    entries.append((offset, len(arrays), first, array.shape[0]))
                    arrays.append(array)
            places.append(entries)

        def body(table_ref, *refs):
            piece_refs, out_refs = refs[: len(arrays)], refs[len(arrays) :]

            def put(entries):
                for offset, at, first, count in entries:
                    slot = lax.rem(table_ref[PLACE] + offset + chips, chips)
                    for ref, (_, moves) in zip(out_refs, outs):
                        for own_rows, own_columns, rows, cut in moves:
                            if isinstance(rows, tuple):
                                if first == 0:
                                    both = [piece_refs[at][r, cut].astype(jnp.float32) for r in rows]
                                    ref[0, slot, own_rows, own_columns] = both[0] + both[1]
                                continue
                            low, high = max(rows.start, first), min(rows.stop, first + count)
                            if low >= high:
                                continue
                            there = slice(
                                own_rows.start + low - rows.start,
                                own_rows.start + high - rows.start,
                            )
                            value = piece_refs[at][low - first : high - first, cut]
                            ref[0, slot, there, own_columns] = value.astype(jnp.float32)

            for i, entries in enumerate(places):
                pl.when(pl.program_id(0) == i)(functools.partial(put, entries))

        def target(i, t):
            return (jnp.where(i == 0, t[CORE], t[MATE]), 0, 0, 0)

        shapes = [(chips, *shape) for shape, _ in outs]
        results = pl.pallas_call(
            body,
            grid_spec=pltpu.PrefetchScalarGridSpec(
                num_scalar_prefetch=1,
                grid=(2,),
                in_specs=[
                    pl.BlockSpec(a.shape, lambda i, w: (0, 0), pipeline_mode=pl.Buffered(1))
                    for a in arrays
                ],
                out_specs=[pl.BlockSpec((1, *shape), target) for shape in shapes],
            ),
            out_shape=[jax.ShapeDtypeStruct((2, *shape), jnp.float32) for shape in shapes],
            compiler_params=pltpu.CompilerParams(vmem_limit_bytes=40 << 20),
            cost_estimate=COST,
            name="place_pieces",
        )(table, *arrays)
        return [out.reshape(-1, out.shape[-1]) for out in results]


class Share:
    def __init__(self, size, shape, rows, at):
        self.array = 0
        self.shard = shape[0] // size
        self.columns = shape[1]
        self.moves = []
        if self.shard <= rows:
            wide = self.columns // (rows // self.shard)
            for i in range(rows // self.shard):
                there = slice(i * self.shard, (i + 1) * self.shard)
                cut = slice(i * wide, (i + 1) * wide)
                self.moves.append((slice(0, self.shard), cut, there, slice(at, at + wide)))
            self.end = at + wide
        else:
            for i in range(self.shard // rows):
                low = at + i * self.columns
                here = slice(i * rows, (i + 1) * rows)
                self.moves.append(
                    (here, slice(0, self.columns), slice(0, rows), slice(low, low + self.columns))
                )
            self.end = at + (self.shard // rows) * self.columns


def two_parts(values):
    high = values.astype(LOW)
    low = (values - high.astype(jnp.float32)).astype(LOW)
    return jnp.concatenate([high, low], 0)


def grad_halves(table, cores, chips, rows, shares, sides, extra=None):
    count = max(share.array for share in shares) + 1
    columns = [max(share.end for share in shares if share.array == n) for n in range(count)]
    halves = [share.shard * chips for share in shares]
    steps = min(halves) // 128
    per = chips // steps
    arrays, where = [] if extra is None else [extra], []
    at = columns[0]
    if extra is not None:
        columns[0] += 128
    for lefts, rights in sides:
        place = []
        for array, low, size in [*lefts, *rights]:
            known = [n for n, other in enumerate(arrays) if other is array]
            if not known:
                arrays.append(array)
            place.append((known[0] if known else len(arrays) - 1, slice(low, low + size)))
        where.append((place[: len(lefts)], place[len(lefts) :]))

    def body(table_ref, *refs):
        refs, out_refs = refs[: len(arrays)], refs[len(arrays) :]

        @pl.loop(0, len(cores) * steps)
        def _(turn):
            n_out = lax.div(turn, steps)
            step = lax.rem(turn, steps)
            core = table_ref[cores[0]]
            if len(cores) == 2:
                core = jnp.where(n_out == 0, core, table_ref[cores[1]])
            grads = []
            for half, (left, right) in zip(halves, where):
                tile = half // steps
                low = pl.multiple_of((core * steps + step) * tile, tile)
                grad = None
                for (n, n_rows), (m, m_rows) in zip(left, right):
                    term = dot_on(refs[n][n_rows, pl.ds(low, tile)], refs[m][m_rows, :], 0, 0)
                    grad = term if grad is None else grad + term
                grads.append(grad.astype(LOW))

            def put(core_refs):
                for n in range(per if extra is not None else 0):
                    row = refs[0][pl.ds(core * chips + step * per + n, 1), :]
                    lines = [row[:, k * 128 : (k + 1) * 128] for k in range(row.shape[1] // 128)]
                    block = two_parts(jnp.concatenate(lines, 0))
                    if rows > 16:
                        fill = jnp.zeros((rows - 16, 128), LOW)
                        block = jnp.concatenate([block, fill], 0)
                    core_refs[0][step * per + n, :, at : at + 128] = block
                for grad, share in zip(grads, shares):
                    ref = core_refs[share.array]
                    for n in range(per):
                        for own_rows, own_columns, there, cut in share.moves:
                            first = n * share.shard
                            ref[step * per + n, there, cut] = grad[
                                first + own_rows.start : first + own_rows.stop, own_columns
                            ]

            for n in range(len(cores)):
                core_refs = out_refs[n * count : (n + 1) * count]
                if len(cores) == 1:
                    put(core_refs)
                else:
                    pl.when(n_out == n)(functools.partial(put, core_refs))

    vmem = pl.BlockSpec(memory_space=pltpu.VMEM)
    outs = pl.pallas_call(
        body,
        in_specs=[pl.BlockSpec(memory_space=pltpu.SMEM)] + [vmem] * len(arrays),
        out_specs=[vmem] * (len(cores) * count),
        out_shape=[jax.ShapeDtypeStruct((chips, rows, c), LOW) for c in columns] * len(cores),
        compiler_params=pltpu.CompilerParams(vmem_limit_bytes=16 << 20),
        cost_estimate=COST,
        name="grad_halves",
    )(table, *arrays)
    return [outs[n] for n in range(len(cores))]


def row_kernel(name, body, rows, arrays, vectors, out_types, sum_rows):
    block = min(128, rows)
    n = len(arrays) + len(vectors)

    def kernel(*refs):
        values, sums = body(*[r[...].astype(jnp.float32) for r in refs[:n]])
        for ref, value in zip(refs[n:-1], values, strict=True):
            ref[...] = value.astype(ref.dtype)
        sums = [jnp.sum(v, 0, keepdims=True) for v in sums]
        sums = jnp.concatenate(sums + [jnp.zeros_like(sums[0])] * (sum_rows - len(sums)), 0)

        @pl.when(pl.program_id(0) == 0)
        def _():
            refs[-1][...] = sums

        @pl.when(pl.program_id(0) > 0)
        def _():
            refs[-1][...] += sums

    width = vectors[0].shape[-1]
    in_specs = [
        pl.BlockSpec((block, a.shape[1]), lambda i, at=low // block: (at + i, 0))
        for a, low in arrays
    ]
    in_specs += [pl.BlockSpec((1, width), lambda i: (0, 0))] * len(vectors)
    out_specs = [pl.BlockSpec((block, w), lambda i: (i, 0)) for w, _ in out_types]
    return pl.pallas_call(
        kernel,
        grid=(rows // block,),
        in_specs=in_specs,
        out_specs=out_specs + [pl.BlockSpec((sum_rows, width), lambda i: (0, 0))],
        out_shape=[jax.ShapeDtypeStruct((rows, w), t) for w, t in out_types]
        + [jax.ShapeDtypeStruct((sum_rows, width), jnp.float32)],
        compiler_params=pltpu.CompilerParams(vmem_limit_bytes=12 << 20),
        cost_estimate=COST,
        name=name,
    )(*[a for a, _ in arrays], *vectors)


def product(x, low, rows, weights, transposed, out_type, into=None, parts=1, part=0):
    inner = x.shape[1]
    outer = weights.shape[0 if transposed else 1]
    tile = min(512, outer)

    def body(x_ref, w_ref, *refs):
        refs[-1][...] = dot_on(x_ref[...], w_ref[...], 1, 1 if transposed else 0).astype(out_type)

    if transposed:
        spec = pl.BlockSpec((tile, inner), lambda i: (i, 0))
    else:
        spec = pl.BlockSpec((inner, tile), lambda i: (0, i))
    more = [] if into is None else [into]
    return pl.pallas_call(
        body,
        grid=(outer // tile,),
        in_specs=[pl.BlockSpec((rows, inner), lambda i: (low // rows, 0)), spec]
        + [pl.BlockSpec(memory_space=pl.ANY)] * len(more),
        out_specs=pl.BlockSpec((rows, tile), lambda i: (part, i)),
        out_shape=jax.ShapeDtypeStruct((rows * parts, outer), out_type),
        input_output_aliases={2: 0} if more else {},
        compiler_params=pltpu.CompilerParams(vmem_limit_bytes=10 << 20),
        cost_estimate=COST,
        name="product",
    )(x, weights, *more)


def sum_kernel(one, two, squares):
    flat = [*one, *two, *squares]
    width = one[0].shape[1]

    def body(*refs):
        *refs, out_ref = refs

        def total(count):
            nonlocal refs
            mine, refs = refs[:count], refs[count:]
            return functools.reduce(jnp.add, [r[...] for r in mine])

        first, second, third = (total(len(g)) for g in (one, two, squares))
        lane = lax.broadcasted_iota(jnp.int32, (1, width), 1)
        row = jnp.zeros((1, width), jnp.float32)
        for n, source in enumerate((third[0:1], third[1:2], second[3:4])):
            row = jnp.where(lane == n, jnp.sum(source, 1, keepdims=True), row)
        out_ref[...] = jnp.concatenate([first[0:3], second[0:3], row, jnp.zeros_like(row)], 0)

    vmem = pl.BlockSpec(memory_space=pltpu.VMEM)
    return pl.pallas_call(
        body,
        in_specs=[vmem] * len(flat),
        out_specs=vmem,
        out_shape=jax.ShapeDtypeStruct((8, width), jnp.float32),
        compiler_params=pltpu.CompilerParams(vmem_limit_bytes=4 << 20),
        cost_estimate=COST,
        name="sum_kernel",
    )(*flat)


def row_values(size, norms, up_sums, biases):
    width = norms[0].shape[1]
    up_rows = -(-up_sums[0].shape[1] // width)
    flat = [*norms, *up_sums, biases]

    def body(*refs):
        *refs, out_ref = refs
        out_ref[...] = jnp.zeros_like(out_ref)
        out_ref[0:8, :] = functools.reduce(jnp.add, [r[...] for r in refs[: len(norms)]])
        ups = functools.reduce(jnp.add, [r[...] for r in refs[len(norms) : -1]])
        for n in range(up_rows):
            part = ups[:, n * width : (n + 1) * width]
            out_ref[8 + n : 9 + n, 0 : part.shape[1]] = part
        bias = refs[-1][0:1]
        out_ref[8 + up_rows : 9 + up_rows, 0 : bias.shape[1]] = bias

    vmem = pl.BlockSpec(memory_space=pltpu.VMEM)
    return pl.pallas_call(
        body,
        in_specs=[vmem] * len(flat),
        out_specs=vmem,
        out_shape=jax.ShapeDtypeStruct((size, width), jnp.float32),
        compiler_params=pltpu.CompilerParams(vmem_limit_bytes=4 << 20),
        cost_estimate=COST,
        name="row_values",
    )(*flat)


def ffn_forward(x, up_w, up_b, down_w, out_type):
    rows, width = x.shape
    units = up_w.shape[1]
    tile = min(512, units)
    steps = units // tile

    def body(x_ref, up_ref, b_ref, down_ref, act_ref, slope_ref, out_ref, acc_ref):
        step = pl.program_id(0)
        up = dot_on(x_ref[...], up_ref[...], 1, 0) + b_ref[...].astype(jnp.float32)
        act, slope = gelu_parts(up)
        act = act.astype(LOW)
        act_ref[...] = act
        slope_ref[...] = slope.astype(LOW)
        accumulate(step, steps, dot_on(act, down_ref[...], 1, 0), acc_ref, out_ref)

    part = pl.BlockSpec((rows, tile), lambda i: (0, i))
    whole = pl.BlockSpec((rows, width), lambda i: (0, 0))
    return pl.pallas_call(
        body,
        grid=(steps,),
        in_specs=[
            whole,
            pl.BlockSpec((width, tile), lambda i: (0, i)),
            pl.BlockSpec((1, tile), lambda i: (0, i)),
            pl.BlockSpec((tile, width), lambda i: (i, 0)),
        ],
        out_specs=[part, part, whole],
        out_shape=[jax.ShapeDtypeStruct((rows, units), LOW)] * 2
        + [jax.ShapeDtypeStruct((rows, width), out_type)],
        scratch_shapes=[pltpu.VMEM((rows, width), jnp.float32)],
        compiler_params=pltpu.CompilerParams(vmem_limit_bytes=16 << 20),
        cost_estimate=COST,
        name="ffn_forward",
    )(x, up_w, up_b, down_w)


def ffn_back(grad, slope, down_w, up_w, out_type):
    rows, width = grad.shape
    units = up_w.shape[1]
    tile = min(512, units)
    steps = units // tile

    def body(g_ref, slope_ref, down_ref, up_ref, dup_ref, sum_ref, out_ref, acc_ref):
        step = pl.program_id(0)
        dact = dot_on(g_ref[...], down_ref[...], 1, 1)
        dup = (dact * slope_ref[...].astype(jnp.float32)).astype(LOW)
        dup_ref[...] = dup
        sum_ref[...] = jnp.sum(dup.astype(jnp.float32), 0, keepdims=True)
        accumulate(step, steps, dot_on(dup, up_ref[...], 1, 1), acc_ref, out_ref)

    part = pl.BlockSpec((rows, tile), lambda i: (0, i))
    whole = pl.BlockSpec((rows, width), lambda i: (0, 0))
    return pl.pallas_call(
        body,
        grid=(steps,),
        in_specs=[
            whole,
            part,
            pl.BlockSpec((tile, width), lambda i: (i, 0)),
            pl.BlockSpec((width, tile), lambda i: (0, i)),
        ],
        out_specs=[part, pl.BlockSpec((1, tile), lambda i: (0, i)), whole],
        out_shape=[
            jax.ShapeDtypeStruct((rows, units), LOW),
            jax.ShapeDtypeStruct((1, units), jnp.float32),
            jax.ShapeDtypeStruct((rows, width), out_type),
        ],
        scratch_shapes=[pltpu.VMEM((rows, width), jnp.float32)],
        compiler_params=pltpu.CompilerParams(vmem_limit_bytes=16 << 20),
        cost_estimate=COST,
        name="ffn_back",
    )(grad, slope, down_w, up_w)


def accumulate(step, steps, term, acc_ref, out_ref):
    if steps == 1:
        out_ref[...] = term.astype(out_ref.dtype)
        return

    @pl.when(step == 0)
    def _():
        acc_ref[...] = term

    @pl.when((step > 0) & (step < steps - 1))
    def _():
        acc_ref[...] += term

    @pl.when(step == steps - 1)
    def _():
        out_ref[...] = (acc_ref[...] + term).astype(out_ref.dtype)


def mean(rows):
    return jnp.mean(rows, -1, keepdims=True)


def normalise(rows):
    centre = rows - mean(rows)
    inverse = lax.rsqrt(mean(centre * centre) + EPS)
    return centre * inverse, inverse


def norm_back(grad, normed, inverse, gain):
    scaled = grad * gain
    return inverse * (scaled - mean(scaled) - normed * mean(scaled * normed))


def gelu_parts(values):
    square = values * values
    rate = -2.0 * GELU_C
    gate = 1.0 / (1.0 + jnp.exp(values * (rate + rate * 0.044715 * square)))
    output = values * gate
    slope = gate + output * (1.0 - gate) * (2.0 * GELU_C + 6.0 * GELU_C * 0.044715 * square)
    return output, slope


def dot(a, b):
    return jnp.dot(a, b, preferred_element_type=jnp.float32)


def dot_nt(a, b):
    return dot_on(a, b, 1, 1)


def dot_tn(a, b):
    return dot_on(a, b, 0, 0)


def column_sums(rows):
    ones = jnp.ones((8, rows.shape[0]), LOW)
    return dot(ones, rows)[0]


def local(
    dp_size,
    ranks,
    hidden_in,
    query_w,
    key_w,
    value_w,
    query_b,
    value_b,
    out_w,
    out_b,
    gain_attn,
    shift_attn,
    up_w,
    up_b,
    down_w,
    down_b,
    gain_ffn,
    shift_ffn,
    random_blocks,
    cotangent,
):
    own_rows, seqs_here, width = hidden_in.shape
    channels, hidden_units = query_w.shape[1], up_w.shape[1]
    length = own_rows * ranks
    chunks = CHUNKS
    piece = own_rows // chunks
    every = range(chunks)
    others = range(1, ranks)
    ring = Ring(dp_size)
    rows_in = hidden_in.reshape(own_rows, width)
    grad_out = cotangent.reshape(own_rows, width)
    lows = [c * piece for c in every]
    order = Order()
    run, tie = order.run, order.tie

    far_rows = fetch(rows_in, ranks)

    def project(x, *w):
        return (dot(x, w[0]) + w[1]).astype(LOW)

    def set_up(ids, q_w, k_w, v_w, q_b, v_b, *vectors):
        return (
            ring.table(own_rows // BLOCK),
            ids.reshape(ids.shape[0], -1),
            jnp.concatenate([q_w, k_w, v_w], 1),
            jnp.concatenate([q_b, jnp.zeros_like(q_b), v_b]).astype(jnp.float32),
            [v.reshape(1, -1) for v in vectors],
        )

    table, random_ids, qkv_w, qkv_b, vectors = run(
        set_up,
        random_blocks,
        query_w,
        key_w,
        value_w,
        query_b,
        value_b,
        out_b,
        gain_attn,
        shift_attn,
        up_b,
        down_b,
        gain_ffn,
        shift_ffn,
    )
    out_b, gain_attn, shift_attn, up_b, down_b, gain_ffn, shift_ffn = vectors
    near = run(project, rows_in, qkv_w, qkv_b)
    qkv = run(
        lambda n, w, b, *x: jnp.concatenate([n] + [project(p, w, b) for p in x], 0),
        near,
        qkv_w,
        qkv_b,
        *far_rows,
    )

    contexts, lses, attn_moved, attn_own = [], [], [], []
    for c in every:
        context, lse = run(lambda v: attend(v, random_ids, table, c, chunks, ranks), qkv)
        contexts.append(context)
        lses.append(lse)
        shares = [
            run(lambda x: product(x, j * piece, piece, out_w, False, LOW), context) for j in others
        ]
        attn_moved.append(hand_over(shares, ranks))
    for c in every:
        attn_own.append(
            run(lambda x: product(x, 0, piece, out_w, False, jnp.float32), contexts[c])
        )

    low_rows = (width, LOW)

    def norm_one(low, own, *moved):
        def body(*values):
            *terms, source, bias, gain, shift = values
            attn_out = functools.reduce(jnp.add, terms)
            resid = source + attn_out + bias
            normed, inverse = normalise(resid)
            hidden = gain * normed + shift
            inverse = jnp.broadcast_to(inverse, (inverse.shape[0], 128))
            return [hidden, normed, inverse], [resid * resid, attn_out * attn_out]

        return row_kernel(
            "norm_one",
            body,
            piece,
            [(own, 0)] + [(m, 0) for m in moved] + [(rows_in, low)],
            [out_b, gain_attn, shift_attn],
            [low_rows, low_rows, (128, jnp.float32)],
            8,
        )

    x, n1, i1, squares, acts, slopes, mlp_moved, mlp_own = ([] for _ in range(8))
    for c in every:
        low, n, i, sq = run(functools.partial(norm_one, lows[c]), attn_own[c], *attn_moved[c])
        n1.append(n)
        i1.append(i)
        squares.append(sq)
        x.append([low] + fetch(low, ranks))
        act, slope, own = run(lambda v: ffn_forward(v, up_w, up_b, down_w, jnp.float32), low)
        acts.append([act])
        slopes.append([slope])
        mlp_own.append(own)
    for c in every:
        shares = []
        for j in others:
            act, slope, share = run(lambda v: ffn_forward(v, up_w, up_b, down_w, LOW), x[c][j])
            acts[c].append(act)
            slopes[c].append(slope)
            shares.append(share)
        mlp_moved.append(hand_over(shares, ranks))

    def norm_two(low, own, h, *moved):
        def body(*values):
            *terms, before, g, bias, gain, shift = values
            mlp_out = functools.reduce(jnp.add, terms)
            normed, inverse = normalise(before + mlp_out + bias)
            back = norm_back(g, normed, inverse, gain)
            sums = [back, g * normed, g, mlp_out * mlp_out]
            return [back, gain * normed + shift], sums

        return row_kernel(
            "norm_two",
            body,
            piece,
            [(own, 0)] + [(m, 0) for m in moved] + [(h, 0), (grad_out, low)],
            [down_b, gain_ffn, shift_ffn],
            [low_rows, low_rows],
            8,
        )

    dmlp, layer_out, sums2 = [], [], []
    for c in every:
        low, out, sums = run(
            functools.partial(norm_two, lows[c]), mlp_own[c], x[c][0], *mlp_moved[c]
        )
        layer_out.append(out)
        sums2.append(sums)
        dmlp.append([low] + fetch(low, ranks))

    dups, dhid_moved, dhid_own, up_sums = [], [], [], []
    for c in every:
        dup, total, own = run(
            lambda d, s: ffn_back(d, s, down_w, up_w, jnp.float32), dmlp[c][0], slopes[c][0]
        )
        dups.append([dup])
        up_sums.append(total)
        dhid_own.append(own)
    for c in every:
        shares = []
        for j in others:
            dup, total, share = run(
                lambda d, s: ffn_back(d, s, down_w, up_w, LOW), dmlp[c][j], slopes[c][j]
            )
            dups[c].append(dup)
            up_sums.append(total)
            shares.append(share)
        dhid_moved.append(hand_over(shares, ranks))

    under_way = []

    def advance(*names):
        for name in names or [n for n, _ in under_way]:
            for entry in [e for e in under_way if e[0] == name]:
                if next(entry[1], "end") == "end":
                    under_way.remove(entry)

    class Grads:
        def __init__(self, rows, shares, sides, extra=None):
            self.rows, self.shares, self.extra = rows, shares, extra
            self.leaves, self.tree = jax.tree.flatten(sides)
            leaves = [x for x in self.leaves if not isinstance(x, int)]
            self.arrays = list({id(x): x for x in leaves}.values())
            self.results = []

        def halves(self, *cores):
            def call(t, extra, *tied):
                known = {id(x): v for x, v in zip(self.arrays, tied)}
                found = [x if isinstance(x, int) else known[id(x)] for x in self.leaves]
                sides = jax.tree.unflatten(self.tree, found)
                return grad_halves(t, cores, ring.chips, self.rows, self.shares, sides, extra)

            return run(call, table, self.extra, *self.arrays)

        def ring(self, name, kept, moved, pair=None):
            under_way.append((name, ring.steps(order, table, kept, moved, self.results, pair)))

    def pieces_of(parts):
        return [(p, 0, piece) for part in parts for p in part]

    ffn_rows = hidden_units // dp_size
    down_share = Share(dp_size, (hidden_units, width), ffn_rows, 0)
    up_share = Share(dp_size, (width, hidden_units), ffn_rows, down_share.end)
    ffn = Grads(
        ffn_rows,
        [down_share, up_share],
        [(pieces_of(acts), pieces_of(dmlp)), (pieces_of(x), pieces_of(dups))],
    )
    ffn_given, ffn_kept = ffn.halves(MATE, CORE)

    def norm_one_back(own, d2, n, i, *moved):
        def body(*values):
            *terms, normed, inverse, gain = values
            dhidden = functools.reduce(jnp.add, terms)
            back = norm_back(dhidden, normed, inverse[:, :1], gain)
            return [back], [back, dhidden * normed, dhidden]

        return row_kernel(
            "norm_one_back",
            body,
            piece,
            [(a, 0) for a in (own, *moved, d2, n, i)],
            [gain_attn],
            [low_rows],
            8,
        )

    dattn, sums1, dcontexts = [], [], []
    for c in every:
        low, sums = run(
            norm_one_back, dhid_own[c], dmlp[c][0], n1[c], i1[c], *dhid_moved[c]
        )
        sums1.append(sums)
        dattn.append([low] + fetch(low, ranks))
    ffn_moved = ring.mate(tie(ffn_given))
    for c in every:
        dcontexts.append(
            run(lambda d: product(d, 0, piece, out_w, True, LOW, None, ranks, 0), dattn[c][0])
        )
    norms = run(sum_kernel, sums1, sums2, squares)
    norms = [norms] + fetch(norms, ranks)
    ffn.ring("ffn", ffn_kept, ffn_moved)
    advance("ffn")

    dq_parts, sums = [], []
    for c in every:
        dcontext = dcontexts[c]
        for j in others:
            dcontext = run(
                lambda d, whole: product(d, 0, piece, out_w, True, LOW, whole, ranks, j),
                dattn[c][j],
                dcontext,
            )
        advance("ffn")
        dq, *sums = run(
            lambda v, d, l, e, s: jax.tree.leaves(
                attend_back(v, d, l, random_ids, table, e, s, c, chunks, ranks)
            ),
            qkv,
            dcontext,
            lses[c],
            dq_parts,
            sums,
        )
        dq_parts.append(dq)
    dqkv, bias_sums = dq, sums[0]

    attn_rows = width // dp_size
    attn_shares = [Share(dp_size, (width, 3 * channels), attn_rows, 0)]
    attn_sides = [
        (
            [(x, 0, own_rows) for x in [rows_in] + far_rows],
            [(dqkv, j * own_rows, own_rows) for j in range(ranks)],
        )
    ]
    with_out = channels % 256 == 0
    if with_out:
        attn_shares.append(Share(dp_size, (channels, width), attn_rows, attn_shares[0].end))
        attn_sides.append(
            (
                [(contexts[c], j * piece, piece) for c in every for j in range(ranks)],
                [(dattn[c][j], 0, piece) for c in every for j in range(ranks)],
            )
        )
    values = run(functools.partial(row_values, dp_size), norms, up_sums, bias_sums)
    pair = attn_shares[-1].end
    attn = Grads(attn_rows, attn_shares, attn_sides, values)
    (given,) = attn.halves(MATE)
    advance("ffn")
    moved = ring.mate(tie(given))
    shares = [
        run(lambda d: product(d, j * own_rows, own_rows, qkv_w, True, LOW), dqkv) for j in others
    ]
    dinput_moved = hand_over(shares, ranks)
    (kept,) = attn.halves(CORE)
    attn.ring("attn", kept, moved, pair)
    advance("attn")
    dinput_own = run(lambda d: product(d, 0, own_rows, qkv_w, True, jnp.float32), dqkv)
    advance("ffn", "attn")
    grad_input = run(
        lambda own, d, *m: (plus(own, m) + jnp.concatenate(d, 0)).astype(LOW),
        dinput_own,
        [d[0] for d in dattn],
        *dinput_moved,
    )
    totals = {}
    entries = float(own_rows * ranks * dp_size * seqs_here * width)
    ffn_outs = [((g.shard, g.columns), g.moves) for g in (down_share, up_share)]
    up_rows = -(-hidden_units // width)

    def spread(value):
        value = value.reshape(dp_size, width)
        return (
            [value[i] for i in range(6)],
            jnp.sqrt(value[6, :3] / entries),
            value[8 + up_rows, :channels],
            value[8 + up_rows, channels : 2 * channels],
            value[8 : 8 + up_rows].reshape(-1)[:hidden_units],
        )

    while under_way:
        advance()
        names = {n for n, _ in under_way}
        if "ffn" not in names and "ffn" not in totals:
            totals["ffn"] = run(lambda *p: ring.place_pieces(table, p, ffn_outs), *ffn.results)
    everything = slice(0, attn_rows)
    attn_outs = []
    for i in range(3):
        cut = slice(i * channels, (i + 1) * channels)
        attn_outs.append(
            ((attn_rows, channels), [(everything, slice(0, channels), everything, cut)])
        )
    lines = slice(0, 8)
    attn_outs.append(
        ((8, 128), [(lines, slice(0, 128), (lines, slice(8, 16)), slice(pair, pair + 128))])
    )
    if with_out:
        attn_outs.append(((attn_shares[1].shard, width), attn_shares[1].moves))
    grad_q, grad_k, grad_v, value, *rest = run(lambda *p: ring.place_pieces(table, p, attn_outs), *attn.results)
    if with_out:
        (grad_out_w,) = rest
    else:
        partial = sum(
            dot_tn(contexts[c], jnp.concatenate(dattn[c], 0)) for c in every
        )
        grad_out_w = lax.psum(partial.astype(LOW), "dp").astype(jnp.float32)
    grad_down_w, grad_up_w = totals["ffn"]
    vectors, rms_stats, *biases = spread(value)
    shape = hidden_in.shape
    return (
        jnp.concatenate(layer_out, 0).reshape(shape),
        grad_input.reshape(shape),
        grad_q,
        grad_k,
        grad_v,
        biases[0],
        biases[1],
        grad_out_w,
        vectors[0],
        vectors[1],
        vectors[2],
        grad_up_w,
        biases[2],
        grad_down_w,
        vectors[3],
        vectors[4],
        vectors[5],
        rms_stats,
    )


def solution(mesh):
    rows = P("tensor", "dp", None)
    columns, split, whole = P(None, "tensor"), P("tensor"), P()
    first = P("tensor", None)
    return jax.shard_map(
        functools.partial(local, mesh.shape["dp"], mesh.shape["tensor"]),
        mesh=mesh,
        in_specs=(
            rows,
            columns,
            columns,
            columns,
            split,
            split,
            first,
            whole,
            whole,
            whole,
            columns,
            split,
            first,
            whole,
            whole,
            whole,
            P("tensor", None, None),
            rows,
        ),
        out_specs=(
            rows,
            rows,
            columns,
            columns,
            columns,
            split,
            split,
            first,
            whole,
            whole,
            whole,
            columns,
            split,
            first,
            whole,
            whole,
            whole,
            whole,
        ),
        check_vma=False,
    )
```

```python
import functools
import math

import jax
import jax.numpy as jnp
from jax import lax
from jax.experimental import pallas as pl
from jax.experimental.pallas import tpu as pltpu
from jax.sharding import PartitionSpec as P

HD = 64
BLOCK = 64
NEG = -1e30
EPS = 1e-12
GELU_C = math.sqrt(2.0 / math.pi)
CHUNKS = 2
LOW = jnp.bfloat16
FIRST, CORE, MATE, PLACE = range(4)
COST = pl.CostEstimate(flops=1024, bytes_accessed=1024, transcendentals=0)


def dot_on(left, right, left_dim, right_dim):
    return lax.dot_general(
        left,
        right,
        (((left_dim,), (right_dim,)), ((), ())),
        preferred_element_type=jnp.float32,
    )


def lane_masks(width, value):
    lane = lax.broadcasted_iota(jnp.int32, (1, width), 1) // HD
    return [jnp.where(lane == h, value, 0.0).astype(LOW) for h in range(width // HD)]


def stack_heads(rows, masks):
    return jnp.concatenate([rows * m for m in masks], 0)


def unstack_heads(stacked, heads):
    lane = lax.broadcasted_iota(jnp.int32, (1, stacked.shape[1]), 1) // HD
    out = stacked[:BLOCK]
    for h in range(1, heads):
        out = jnp.where(lane == h, stacked[h * BLOCK : (h + 1) * BLOCK], out)
    return out


def block_at(index):
    return pl.ds(pl.multiple_of(index * BLOCK, BLOCK), BLOCK)


class Plan:
    def __init__(self, chunk, chunks, ranks, length, rand, heads):
        self.blocks = length // BLOCK
        self.rank_blocks = self.blocks // ranks
        self.chunk_blocks = self.rank_blocks // chunks
        self.chunk = chunk
        self.rand = rand
        self.heads = heads
        taken = [
            j * self.rank_blocks + chunk * self.chunk_blocks + r
            for j in range(ranks)
            for r in range(self.chunk_blocks)
        ]
        self.ends = [b for b in taken if b in (0, self.blocks - 1)]
        middles = [b for b in taken if b not in self.ends]
        self.ranges = []
        for b in middles:
            if self.ranges and self.ranges[-1][1] == b:
                self.ranges[-1][1] = b + 1
            else:
                self.ranges.append([b, b + 1])

    def local(self, block, first):
        return lax.rem(block - first + self.blocks, self.blocks)

    def inner(self, local):
        part = lax.div(local, self.rank_blocks)
        rest = local - part * self.rank_blocks
        return part * self.chunk_blocks + rest - self.chunk * self.chunk_blocks

    def fixed(self, block, first):
        wanted = (jnp.int32(0), jnp.int32(self.blocks - 1), block - 1, block, block + 1)
        return [self.local(w, first) for w in wanted]

    def random(self, rb_ref, group, block, first):
        return [
            [
                self.local(rb_ref[group * self.heads + h, (block - 1) * self.rand + r], first)
                for h in range(self.heads)
            ]
            for r in range(self.rand)
        ]

    def run(self, one, unroll):
        for low, high in self.ranges:
            count = high - low
            main = count - count % unroll
            if main > unroll:

                @pl.loop(0, main // unroll)
                def _(step, low=low):
                    for u in range(unroll):
                        one(low + step * unroll + u)
            else:
                main = 0
            for x in range(main, count):
                one(jnp.int32(low + x))


def pick_tiles(ref, fixed, rands):
    width = ref.shape[1]
    column = min(128, width)
    per = column // HD
    lane = lax.broadcasted_iota(jnp.int32, (1, column), 1) // HD
    parts = [ref[block_at(f), :] for f in fixed]
    for per_head in rands:
        columns = []
        for c in range(width // column):
            tile = None
            for p in range(per):
                x = ref[block_at(per_head[c * per + p]), c * column : (c + 1) * column]
                tile = x if tile is None else jnp.where(lane == p, x, tile)
            columns.append(tile)
        parts.append(jnp.concatenate(columns, 1) if len(columns) > 1 else columns[0])
    return jnp.concatenate(parts, 0)


def attend_kernel(plan, unroll, table_ref, rb_ref, q_ref, k_ref, v_ref, o_ref, lse_ref):
    group = pl.program_id(0)
    first = table_ref[FIRST]
    heads = plan.heads
    masks = lane_masks(q_ref.shape[1], HD**-0.5)

    def finish(scores, values, place):
        top = jnp.max(scores, 1, keepdims=True)
        weights = jnp.exp(scores - top)
        total = jnp.sum(weights, 1, keepdims=True)
        out = dot_on(weights.astype(LOW), values, 1, 0) * (1.0 / total)
        o_ref[block_at(place), :] = unstack_heads(out, heads).astype(LOW)
        wide = jnp.broadcast_to(top + jnp.log(total), (heads * BLOCK, 128))
        lse_ref[0, pl.ds(place, 1), :] = jnp.transpose(wide)[0:1, :]

    def one(block):
        fixed = plan.fixed(block, first)
        rands = plan.random(rb_ref, group, block, first)
        queries = stack_heads(q_ref[block_at(fixed[3]), :], masks)
        scores = dot_on(queries, pick_tiles(k_ref, fixed, rands), 1, 1)
        lane = lax.broadcasted_iota(jnp.int32, (1, 2 * BLOCK), 1)
        drop = ((block == 1) & (lane < BLOCK)) | (
            (block == plan.blocks - 2) & (lane >= BLOCK)
        )
        scores = jnp.concatenate(
            [jnp.where(drop, NEG, scores[:, : 2 * BLOCK]), scores[:, 2 * BLOCK :]], 1
        )
        finish(scores, pick_tiles(v_ref, fixed, rands), plan.inner(fixed[3]))

    plan.run(one, unroll)
    for b in plan.ends:
        local = plan.local(jnp.int32(b), first)
        queries = stack_heads(q_ref[block_at(local), :], masks)
        finish(dot_on(queries, k_ref[...], 1, 1), v_ref[...], plan.inner(local))


def attend_back_kernel(plan, unroll, earlier, last, table_ref, rb_ref, q_ref, k_ref, v_ref, *refs):
    do_ref, lse_ref, *refs = refs
    dq_in, refs = refs[:earlier], refs[earlier:]
    if earlier:
        dk_in, dv_in, *refs = refs
    if last:
        all_ref, bias_ref, dq_ref, dk_acc, dv_acc = refs
    else:
        dq_ref, dk_acc, dv_acc = refs
    group = pl.program_id(0)
    first = table_ref[FIRST]
    heads = plan.heads
    width = q_ref.shape[1]
    query_masks, out_masks = lane_masks(width, HD**-0.5), lane_masks(width, 1.0)
    column = min(128, width)
    per = column // HD
    lane = lax.broadcasted_iota(jnp.int32, (1, column), 1) // HD
    if earlier:
        dk_acc[...] = dk_in[...]
        dv_acc[...] = dv_in[...]
    else:
        dk_acc[...] = jnp.zeros_like(dk_acc)
        dv_acc[...] = jnp.zeros_like(dv_acc)

    def core(scores, keys, values, queries, douts, place):
        probs = jnp.exp(scores - lse_ref[0, pl.ds(place, 1), :])
        dprobs = dot_on(values, douts, 1, 1)
        row_dot = jnp.sum(probs * dprobs, 0, keepdims=True)
        dscores = (probs * (dprobs - row_dot)).astype(LOW)
        dv = dot_on(probs.astype(LOW), douts, 1, 0)
        dk = dot_on(dscores, queries, 1, 0)
        dq = unstack_heads(dot_on(dscores, keys, 0, 0), heads) * (HD**-0.5)
        dq_ref[block_at(place), :] = dq.astype(LOW)
        return dk, dv

    def add_tiles(acc, value, fixed, rands):
        for n, f in enumerate(fixed):
            acc[block_at(f), :] += value[n * BLOCK : (n + 1) * BLOCK]
        for r, per_head in enumerate(rands):
            tile = value[(5 + r) * BLOCK : (6 + r) * BLOCK]
            for h in range(heads):
                c = h // per
                cut = slice(c * column, (c + 1) * column)
                acc[block_at(per_head[h]), cut] += jnp.where(lane == h % per, tile[:, cut], 0.0)

    def one(block):
        fixed = plan.fixed(block, first)
        rands = plan.random(rb_ref, group, block, first)
        place = plan.inner(fixed[3])
        queries = stack_heads(q_ref[block_at(fixed[3]), :], query_masks)
        douts = stack_heads(do_ref[block_at(place), :], out_masks)
        keys = pick_tiles(k_ref, fixed, rands)
        values = pick_tiles(v_ref, fixed, rands)
        scores = dot_on(keys, queries, 1, 1)
        scores = jnp.concatenate(
            [
                jnp.where(block == 1, NEG, scores[:BLOCK]),
                jnp.where(block == plan.blocks - 2, NEG, scores[BLOCK : 2 * BLOCK]),
                scores[2 * BLOCK :],
            ],
            0,
        )
        dk, dv = core(scores, keys, values, queries, douts, place)
        add_tiles(dk_acc, dk, fixed, rands)
        add_tiles(dv_acc, dv, fixed, rands)

    for b in plan.ends:
        local = plan.local(jnp.int32(b), first)
        place = plan.inner(local)
        queries = stack_heads(q_ref[block_at(local), :], query_masks)
        douts = stack_heads(do_ref[block_at(place), :], out_masks)
        scores = dot_on(k_ref[...], queries, 1, 1)
        dk, dv = core(scores, k_ref[...], v_ref[...], queries, douts, place)
        dk_acc[...] += dk
        dv_acc[...] += dv
    plan.run(one, unroll)
    if last:
        channels = all_ref.shape[1] // 3
        rows = plan.chunk_blocks * BLOCK
        chunks = earlier + 1
        for at in range(0, channels, width):

            @pl.when(group * width == at)
            def _(at=at):
                for c, source in enumerate([*dq_in, dq_ref]):
                    for j in range(plan.blocks // plan.rank_blocks):
                        low = (j * chunks + c) * rows
                        all_ref[low : low + rows, at : at + width] = source[j * rows : (j + 1) * rows]
                for n, acc in ((1, dk_acc), (2, dv_acc)):
                    cut = n * channels + at
                    all_ref[:, cut : cut + width] = acc[...].astype(LOW)
                for n in (0, 2):
                    cut = slice(n * channels + at, n * channels + at + width)
                    total = jnp.sum(all_ref[:, cut].astype(jnp.float32), 0, keepdims=True)
                    cut = slice(n // 2 * channels + at, n // 2 * channels + at + width)
                    bias_ref[:, cut] = jnp.broadcast_to(total, (8, width))


def group_width(channels):
    return min(256, channels)


def packed_specs(length, channels):
    width = group_width(channels)
    groups = channels // width
    return [
        pl.BlockSpec((length, width), lambda g, *_, n=n: (0, n * groups + g)) for n in range(3)
    ]


def attend(qkv, random_ids, table, chunk, chunks, ranks):
    length, channels = qkv.shape[0], qkv.shape[1] // 3
    width = group_width(channels)
    groups, heads = channels // width, width // HD
    plan = Plan(chunk, chunks, ranks, length, random_ids.shape[1] // (length // BLOCK - 2), heads)
    rows = length // chunks
    return pl.pallas_call(
        functools.partial(attend_kernel, plan, 4),
        grid_spec=pltpu.PrefetchScalarGridSpec(
            num_scalar_prefetch=2,
            grid=(groups,),
            in_specs=packed_specs(length, channels),
            out_specs=[
                pl.BlockSpec((rows, width), lambda g, *_: (0, g)),
                pl.BlockSpec((1, rows // BLOCK, width), lambda g, *_: (g, 0, 0)),
            ],
        ),
        out_shape=[
            jax.ShapeDtypeStruct((rows, channels), LOW),
            jax.ShapeDtypeStruct((groups, rows // BLOCK, width), jnp.float32),
        ],
        compiler_params=pltpu.CompilerParams(vmem_limit_bytes=12 << 20),
        cost_estimate=COST,
        name="attend",
    )(table, random_ids, qkv, qkv, qkv)


def attend_back(qkv, dout, lse, random_ids, table, earlier, sums, chunk, chunks, ranks):
    length, channels = qkv.shape[0], qkv.shape[1] // 3
    width = group_width(channels)
    groups, heads = channels // width, width // HD
    plan = Plan(chunk, chunks, ranks, length, random_ids.shape[1] // (length // BLOCK - 2), heads)
    rows = length // chunks
    last = chunk == chunks - 1
    part = pl.BlockSpec((rows, width), lambda g, *_: (0, g))
    full = pl.BlockSpec((length, width), lambda g, *_: (0, g))
    sum_shape = jax.ShapeDtypeStruct((length, channels), jnp.float32)
    if last:
        bias = (8, 2 * channels)
        out_specs = [pl.BlockSpec(shape, lambda g, *_: (0, 0)) for shape in (qkv.shape, bias)]
        out_shape = [
            jax.ShapeDtypeStruct(qkv.shape, LOW),
            jax.ShapeDtypeStruct(bias, jnp.float32),
        ]
        scratch = [pltpu.VMEM((rows, width), LOW)] + [pltpu.VMEM((length, width), jnp.float32)] * 2
    else:
        out_specs = [part, full, full]
        out_shape = [jax.ShapeDtypeStruct((rows, channels), LOW), sum_shape, sum_shape]
        scratch = []
    return pl.pallas_call(
        functools.partial(attend_back_kernel, plan, 3, len(earlier), last),
        grid_spec=pltpu.PrefetchScalarGridSpec(
            num_scalar_prefetch=2,
            grid=(groups,),
            in_specs=packed_specs(length, channels)
            + [part, pl.BlockSpec((1, rows // BLOCK, width), lambda g, *_: (g, 0, 0))]
            + [part] * len(earlier)
            + [full] * len(sums),
            out_specs=out_specs,
            scratch_shapes=scratch,
        ),
        out_shape=out_shape,
        compiler_params=pltpu.CompilerParams(vmem_limit_bytes=(28 if last else 18) << 20),
        cost_estimate=COST,
        name="attend_back",
    )(table, random_ids, qkv, qkv, qkv, dout, lse, *earlier, *sums)


class Order:
    def __init__(self):
        self.token = None

    def tie(self, values):
        if self.token is None:
            return values
        values, self.token = lax.optimization_barrier((values, self.token))
        return values

    def run(self, function, *values):
        out = function(*self.tie(values))
        self.token = min(jax.tree.leaves(out), key=lambda leaf: leaf.size)
        return out


def fetch(rows, ranks):
    return [
        lax.ppermute(rows, "tensor", [((k + s) % ranks, k) for k in range(ranks)])
        for s in range(1, ranks)
    ]


def hand_over(shares, ranks):
    return [
        lax.ppermute(share, "tensor", [(k, (k + s) % ranks) for k in range(ranks)])
        for s, share in enumerate(shares, 1)
    ]


def plus(own, moved):
    for m in moved:
        own = own + m.astype(jnp.float32)
    return own


class Ring:
    def __init__(self, size):
        self.size = size
        self.chips = size // 2
        self.order = list(range(0, self.chips, 2)) + list(range(1, self.chips, 2))[::-1]
        self.ahead = self.chips // 2
        self.behind = self.chips - 1 - self.ahead

    def table(self, own_blocks):
        index = lax.axis_index("dp")
        core, chip = lax.rem(index, 2), lax.div(index, 2)
        half = lax.div(chip, 2)
        place = jnp.where(lax.rem(chip, 2) == 0, half, self.chips - 1 - half)
        first = lax.axis_index("tensor") * own_blocks
        return jnp.stack([first, core, 1 - core, place]).astype(jnp.int32)

    def shift(self, value, by):
        pairs = []
        for q in range(self.chips):
            source, target = self.order[q], self.order[(q + by) % self.chips]
            pairs += [(2 * source + c, 2 * target + c) for c in range(2)]
        return lax.ppermute(value, "dp", pairs)

    def mate(self, value):
        return lax.ppermute(value, "dp", [(i, i ^ 1) for i in range(self.size)])

    def add(self, table, kept, moved, offset, part, pair, *more):
        chips, rows, columns = kept.shape
        block = rows // 2 if rows % 32 == 0 else rows
        steps = rows // block if part is None else 1

        def body(table_ref, kept_ref, moved_ref, *refs):
            *refs, out_ref = refs
            total = kept_ref[0].astype(jnp.float32) + moved_ref[0].astype(jnp.float32)
            for ref, (array, half) in zip(refs, more):
                term = ref[...].astype(jnp.float32)
                if array.shape[0] < rows and part is None:
                    term = jnp.where(pl.program_id(0) == half, term, 0.0)
                total = total + term
            out_ref[...] = total.astype(LOW)
            if pair is not None and part != 1:

                @pl.when(pl.program_id(0) == 0)
                def _():
                    out_ref[0:16, pair:] = two_parts(total[0:8, pair:] + total[8:16, pair:])

        shard = pl.BlockSpec(
            (1, block, columns),
            lambda i, t: (lax.rem(t[PLACE] + offset + 2 * chips, chips), i + (part or 0), 0),
        )
        each = pl.BlockSpec((block, columns), lambda i, t: (i, 0))
        fixed = pl.BlockSpec((block, columns), lambda i, t: (0, 0))
        return pl.pallas_call(
            body,
            grid_spec=pltpu.PrefetchScalarGridSpec(
                num_scalar_prefetch=1,
                grid=(steps,),
                in_specs=[shard, shard] + [fixed if a.shape[0] < rows else each for a, _ in more],
                out_specs=each,
            ),
            out_shape=jax.ShapeDtypeStruct((block * steps, columns), LOW),
            compiler_params=pltpu.CompilerParams(vmem_limit_bytes=8 << 20),
            cost_estimate=COST,
            name="ring_add",
        )(table, kept, moved, *[a for a, _ in more])

    def steps(self, order, table, kept, moved, results, pair=None):
        ahead = self.ahead
        rows = kept.shape[1]
        split = rows % 32 == 0

        def add(offset, part, *more):
            halves = [h for _, h in more]
            return order.run(
                lambda t, k, m, *more: self.add(t, k, m, offset, part, pair, *zip(more, halves)),
                table,
                kept,
                moved,
                *[a for a, _ in more],
            )

        right = add(ahead, 0 if split else None)
        left = add(-ahead, 1) if split else None
        for j in range(1, ahead + 1):
            right = self.shift(right, 1)
            left = None if left is None else self.shift(left, -1)
            yield
            if j < ahead:
                right = add(ahead - j, None, (right, 0))
                left = add(j - ahead, None, *([] if left is None else [(left, 1)]))
        own = add(0, None, (right, 0), (left, 0))
        mine, theirs = {0: own}, {0: order.tie(self.mate(own))}
        right = left = own
        for j in range(1, ahead + 1):
            if j == ahead and split:
                half = rows // 2
                right, left = order.run(lambda r, l: (r[:half], l[half:]), right, left)
            right = self.shift(right, 1)
            left = self.shift(left, -1) if j < ahead or split else None
            yield
            right, left = order.tie((right, left))
            mine[-j], mine[j] = right, left
            theirs[-j] = self.mate(right)
            theirs[j] = None if left is None else self.mate(left)
        offsets = range(-ahead, ahead + 1)
        results += [[side[o] for o in offsets] for side in (mine, theirs)]

    def place_pieces(self, table, pieces, outs):
        chips, ahead = self.chips, self.ahead
        size = pieces[0][ahead].shape[0]
        cuts = [move[3] for _, moves in outs for move in moves]
        first_lane = min(cut.start for cut in cuts)
        wide = max(cut.stop for cut in cuts) - first_lane
        arrays, places = [], []
        for side in pieces:
            entries = []
            for offset, array in zip(range(-ahead, ahead + 1), side):
                if array is not None:
                    first = size - array.shape[0] if offset == ahead else 0
                    entries.append((offset, len(arrays), first, array.shape[0]))
                    arrays.append(array)
            places.append(entries)

        def body(table_ref, *refs):
            piece_refs, out_refs = refs[: len(arrays)], refs[len(arrays) :]

            def put(entries):
                for offset, at, first, count in entries:
                    slot = lax.rem(table_ref[PLACE] + offset + chips, chips)
                    for ref, (_, moves) in zip(out_refs, outs):
                        for own_rows, own_columns, rows, cut in moves:
                            lanes = slice(cut.start - first_lane, cut.stop - first_lane)
                            if isinstance(rows, tuple):
                                if first == 0:
                                    both = [piece_refs[at][r, lanes].astype(jnp.float32) for r in rows]
                                    ref[0, slot, own_rows, own_columns] = both[0] + both[1]
                                continue
                            low, high = max(rows.start, first), min(rows.stop, first + count)
                            if low >= high:
                                continue
                            there = slice(
                                own_rows.start + low - rows.start,
                                own_rows.start + high - rows.start,
                            )
                            value = piece_refs[at][low - first : high - first, lanes]
                            ref[0, slot, there, own_columns] = value.astype(jnp.float32)

            for i, entries in enumerate(places):
                pl.when(pl.program_id(0) == i)(functools.partial(put, entries))

        def target(i, t):
            return (jnp.where(i == 0, t[CORE], t[MATE]), 0, 0, 0)

        shapes = [(chips, *shape) for shape, _ in outs]
        results = pl.pallas_call(
            body,
            grid_spec=pltpu.PrefetchScalarGridSpec(
                num_scalar_prefetch=1,
                grid=(2,),
                in_specs=[
                    pl.BlockSpec(
                        (a.shape[0], wide),
                        lambda i, w: (0, first_lane // wide),
                        pipeline_mode=pl.Buffered(1),
                    )
                    for a in arrays
                ],
                out_specs=[pl.BlockSpec((1, *shape), target) for shape in shapes],
            ),
            out_shape=[jax.ShapeDtypeStruct((2, *shape), jnp.float32) for shape in shapes],
            compiler_params=pltpu.CompilerParams(vmem_limit_bytes=40 << 20),
            cost_estimate=COST,
            name="place_pieces",
        )(table, *arrays)
        return [out.reshape(-1, out.shape[-1]) for out in results]


class Share:
    def __init__(self, size, shape, rows, at):
        self.array = 0
        self.shard = shape[0] // size
        self.columns = shape[1]
        self.moves = []
        if self.shard <= rows:
            wide = self.columns // (rows // self.shard)
            for i in range(rows // self.shard):
                there = slice(i * self.shard, (i + 1) * self.shard)
                cut = slice(i * wide, (i + 1) * wide)
                self.moves.append((slice(0, self.shard), cut, there, slice(at, at + wide)))
            self.end = at + wide
        else:
            for i in range(self.shard // rows):
                low = at + i * self.columns
                here = slice(i * rows, (i + 1) * rows)
                self.moves.append(
                    (here, slice(0, self.columns), slice(0, rows), slice(low, low + self.columns))
                )
            self.end = at + (self.shard // rows) * self.columns


def two_parts(values):
    high = values.astype(LOW)
    low = (values - high.astype(jnp.float32)).astype(LOW)
    return jnp.concatenate([high, low], 0)


def grad_halves(table, cores, chips, rows, shares, sides, extra=None):
    count = max(share.array for share in shares) + 1
    columns = [max(share.end for share in shares if share.array == n) for n in range(count)]
    halves = [share.shard * chips for share in shares]
    steps = min(halves) // 128
    per = chips // steps
    arrays, where = [] if extra is None else [extra], []
    at = columns[0]
    if extra is not None:
        columns[0] += 128
    for lefts, rights in sides:
        place = []
        for array, low, size in [*lefts, *rights]:
            known = [n for n, other in enumerate(arrays) if other is array]
            if not known:
                arrays.append(array)
            place.append((known[0] if known else len(arrays) - 1, slice(low, low + size)))
        where.append((place[: len(lefts)], place[len(lefts) :]))

    def body(table_ref, *refs):
        refs, out_refs = refs[: len(arrays)], refs[len(arrays) :]

        @pl.loop(0, len(cores) * steps)
        def _(turn):
            n_out = lax.div(turn, steps)
            step = lax.rem(turn, steps)
            core = table_ref[cores[0]]
            if len(cores) == 2:
                core = jnp.where(n_out == 0, core, table_ref[cores[1]])
            grads = []
            for half, (left, right) in zip(halves, where):
                tile = half // steps
                low = pl.multiple_of((core * steps + step) * tile, tile)
                grad = None
                for (n, n_rows), (m, m_rows) in zip(left, right):
                    term = dot_on(refs[n][n_rows, pl.ds(low, tile)], refs[m][m_rows, :], 0, 0)
                    grad = term if grad is None else grad + term
                grads.append(grad.astype(LOW))

            def put(core_refs):
                for n in range(per if extra is not None else 0):
                    row = refs[0][pl.ds(core * chips + step * per + n, 1), :]
                    lines = [row[:, k * 128 : (k + 1) * 128] for k in range(row.shape[1] // 128)]
                    block = two_parts(jnp.concatenate(lines, 0))
                    if rows > 16:
                        fill = jnp.zeros((rows - 16, 128), LOW)
                        block = jnp.concatenate([block, fill], 0)
                    core_refs[0][step * per + n, :, at : at + 128] = block
                for grad, share in zip(grads, shares):
                    ref = core_refs[share.array]
                    for n in range(per):
                        for own_rows, own_columns, there, cut in share.moves:
                            first = n * share.shard
                            ref[step * per + n, there, cut] = grad[
                                first + own_rows.start : first + own_rows.stop, own_columns
                            ]

            for n in range(len(cores)):
                core_refs = out_refs[n * count : (n + 1) * count]
                if len(cores) == 1:
                    put(core_refs)
                else:
                    pl.when(n_out == n)(functools.partial(put, core_refs))

    vmem = pl.BlockSpec(memory_space=pltpu.VMEM)
    outs = pl.pallas_call(
        body,
        in_specs=[pl.BlockSpec(memory_space=pltpu.SMEM)] + [vmem] * len(arrays),
        out_specs=[vmem] * (len(cores) * count),
        out_shape=[jax.ShapeDtypeStruct((chips, rows, c), LOW) for c in columns] * len(cores),
        compiler_params=pltpu.CompilerParams(vmem_limit_bytes=16 << 20),
        cost_estimate=COST,
        name="grad_halves",
    )(table, *arrays)
    return [outs[n] for n in range(len(cores))]


def row_kernel(name, body, rows, arrays, vectors, out_types, sum_rows):
    block = min(128, rows)
    n = len(arrays) + len(vectors)

    def kernel(*refs):
        values, sums = body(*[r[...].astype(jnp.float32) for r in refs[:n]])
        for ref, value in zip(refs[n:-1], values, strict=True):
            ref[...] = value.astype(ref.dtype)
        sums = [jnp.sum(v, 0, keepdims=True) for v in sums]
        sums = jnp.concatenate(sums + [jnp.zeros_like(sums[0])] * (sum_rows - len(sums)), 0)

        @pl.when(pl.program_id(0) == 0)
        def _():
            refs[-1][...] = sums

        @pl.when(pl.program_id(0) > 0)
        def _():
            refs[-1][...] += sums

    width = vectors[0].shape[-1]
    in_specs = [
        pl.BlockSpec((block, a.shape[1]), lambda i, at=low // block: (at + i, 0))
        for a, low in arrays
    ]
    in_specs += [pl.BlockSpec((1, width), lambda i: (0, 0))] * len(vectors)
    out_specs = [pl.BlockSpec((block, w), lambda i: (i, 0)) for w, _ in out_types]
    return pl.pallas_call(
        kernel,
        grid=(rows // block,),
        in_specs=in_specs,
        out_specs=out_specs + [pl.BlockSpec((sum_rows, width), lambda i: (0, 0))],
        out_shape=[jax.ShapeDtypeStruct((rows, w), t) for w, t in out_types]
        + [jax.ShapeDtypeStruct((sum_rows, width), jnp.float32)],
        compiler_params=pltpu.CompilerParams(vmem_limit_bytes=12 << 20),
        cost_estimate=COST,
        name=name,
    )(*[a for a, _ in arrays], *vectors)


def product(x, low, rows, weights, transposed, out_type, into=None, parts=1, part=0):
    inner = x.shape[1]
    outer = weights.shape[0 if transposed else 1]
    tile = min(512, outer)

    def body(x_ref, w_ref, *refs):
        refs[-1][...] = dot_on(x_ref[...], w_ref[...], 1, 1 if transposed else 0).astype(out_type)

    if transposed:
        spec = pl.BlockSpec((tile, inner), lambda i: (i, 0))
    else:
        spec = pl.BlockSpec((inner, tile), lambda i: (0, i))
    more = [] if into is None else [into]
    return pl.pallas_call(
        body,
        grid=(outer // tile,),
        in_specs=[pl.BlockSpec((rows, inner), lambda i: (low // rows, 0)), spec]
        + [pl.BlockSpec(memory_space=pl.ANY)] * len(more),
        out_specs=pl.BlockSpec((rows, tile), lambda i: (part, i)),
        out_shape=jax.ShapeDtypeStruct((rows * parts, outer), out_type),
        input_output_aliases={2: 0} if more else {},
        compiler_params=pltpu.CompilerParams(vmem_limit_bytes=10 << 20),
        cost_estimate=COST,
        name="product",
    )(x, weights, *more)


def sum_kernel(one, two, squares):
    flat = [*one, *two, *squares]
    width = one[0].shape[1]

    def body(*refs):
        *refs, out_ref = refs

        def total(count):
            nonlocal refs
            mine, refs = refs[:count], refs[count:]
            return functools.reduce(jnp.add, [r[...] for r in mine])

        first, second, third = (total(len(g)) for g in (one, two, squares))
        lane = lax.broadcasted_iota(jnp.int32, (1, width), 1)
        row = jnp.zeros((1, width), jnp.float32)
        for n, source in enumerate((third[0:1], third[1:2], second[3:4])):
            row = jnp.where(lane == n, jnp.sum(source, 1, keepdims=True), row)
        out_ref[...] = jnp.concatenate([first[0:3], second[0:3], row, jnp.zeros_like(row)], 0)

    vmem = pl.BlockSpec(memory_space=pltpu.VMEM)
    return pl.pallas_call(
        body,
        in_specs=[vmem] * len(flat),
        out_specs=vmem,
        out_shape=jax.ShapeDtypeStruct((8, width), jnp.float32),
        compiler_params=pltpu.CompilerParams(vmem_limit_bytes=4 << 20),
        cost_estimate=COST,
        name="sum_kernel",
    )(*flat)


def row_values(size, norms, up_sums, biases):
    width = norms[0].shape[1]
    up_rows = -(-up_sums[0].shape[1] // width)
    flat = [*norms, *up_sums, biases]

    def body(*refs):
        *refs, out_ref = refs
        out_ref[...] = jnp.zeros_like(out_ref)
        out_ref[0:8, :] = functools.reduce(jnp.add, [r[...] for r in refs[: len(norms)]])
        ups = functools.reduce(jnp.add, [r[...] for r in refs[len(norms) : -1]])
        for n in range(up_rows):
            part = ups[:, n * width : (n + 1) * width]
            out_ref[8 + n : 9 + n, 0 : part.shape[1]] = part
        bias = refs[-1][0:1]
        out_ref[8 + up_rows : 9 + up_rows, 0 : bias.shape[1]] = bias

    vmem = pl.BlockSpec(memory_space=pltpu.VMEM)
    return pl.pallas_call(
        body,
        in_specs=[vmem] * len(flat),
        out_specs=vmem,
        out_shape=jax.ShapeDtypeStruct((size, width), jnp.float32),
        compiler_params=pltpu.CompilerParams(vmem_limit_bytes=4 << 20),
        cost_estimate=COST,
        name="row_values",
    )(*flat)


def ffn_forward(x, up_w, up_b, down_w, out_type):
    rows, width = x.shape
    units = up_w.shape[1]
    tile = min(512, units)
    steps = units // tile

    def body(x_ref, up_ref, b_ref, down_ref, act_ref, slope_ref, out_ref, acc_ref):
        step = pl.program_id(0)
        up = dot_on(x_ref[...], up_ref[...], 1, 0) + b_ref[...].astype(jnp.float32)
        act, slope = gelu_parts(up)
        act = act.astype(LOW)
        act_ref[...] = act
        slope_ref[...] = slope.astype(LOW)
        accumulate(step, steps, dot_on(act, down_ref[...], 1, 0), acc_ref, out_ref)

    part = pl.BlockSpec((rows, tile), lambda i: (0, i))
    whole = pl.BlockSpec((rows, width), lambda i: (0, 0))
    return pl.pallas_call(
        body,
        grid=(steps,),
        in_specs=[
            whole,
            pl.BlockSpec((width, tile), lambda i: (0, i)),
            pl.BlockSpec((1, tile), lambda i: (0, i)),
            pl.BlockSpec((tile, width), lambda i: (i, 0)),
        ],
        out_specs=[part, part, whole],
        out_shape=[jax.ShapeDtypeStruct((rows, units), LOW)] * 2
        + [jax.ShapeDtypeStruct((rows, width), out_type)],
        scratch_shapes=[pltpu.VMEM((rows, width), jnp.float32)],
        compiler_params=pltpu.CompilerParams(vmem_limit_bytes=16 << 20),
        cost_estimate=COST,
        name="ffn_forward",
    )(x, up_w, up_b, down_w)


def ffn_back(grad, slope, down_w, up_w, out_type):
    rows, width = grad.shape
    units = up_w.shape[1]
    tile = min(512, units)
    steps = units // tile

    def body(g_ref, slope_ref, down_ref, up_ref, dup_ref, sum_ref, out_ref, acc_ref):
        step = pl.program_id(0)
        dact = dot_on(g_ref[...], down_ref[...], 1, 1)
        dup = (dact * slope_ref[...].astype(jnp.float32)).astype(LOW)
        dup_ref[...] = dup
        sum_ref[...] = jnp.sum(dup.astype(jnp.float32), 0, keepdims=True)
        accumulate(step, steps, dot_on(dup, up_ref[...], 1, 1), acc_ref, out_ref)

    part = pl.BlockSpec((rows, tile), lambda i: (0, i))
    whole = pl.BlockSpec((rows, width), lambda i: (0, 0))
    return pl.pallas_call(
        body,
        grid=(steps,),
        in_specs=[
            whole,
            part,
            pl.BlockSpec((tile, width), lambda i: (i, 0)),
            pl.BlockSpec((width, tile), lambda i: (0, i)),
        ],
        out_specs=[part, pl.BlockSpec((1, tile), lambda i: (0, i)), whole],
        out_shape=[
            jax.ShapeDtypeStruct((rows, units), LOW),
            jax.ShapeDtypeStruct((1, units), jnp.float32),
            jax.ShapeDtypeStruct((rows, width), out_type),
        ],
        scratch_shapes=[pltpu.VMEM((rows, width), jnp.float32)],
        compiler_params=pltpu.CompilerParams(vmem_limit_bytes=16 << 20),
        cost_estimate=COST,
        name="ffn_back",
    )(grad, slope, down_w, up_w)


def accumulate(step, steps, term, acc_ref, out_ref):
    if steps == 1:
        out_ref[...] = term.astype(out_ref.dtype)
        return

    @pl.when(step == 0)
    def _():
        acc_ref[...] = term

    @pl.when((step > 0) & (step < steps - 1))
    def _():
        acc_ref[...] += term

    @pl.when(step == steps - 1)
    def _():
        out_ref[...] = (acc_ref[...] + term).astype(out_ref.dtype)


def mean(rows):
    return jnp.mean(rows, -1, keepdims=True)


def normalise(rows):
    centre = rows - mean(rows)
    inverse = lax.rsqrt(mean(centre * centre) + EPS)
    return centre * inverse, inverse


def norm_back(grad, normed, inverse, gain):
    scaled = grad * gain
    return inverse * (scaled - mean(scaled) - normed * mean(scaled * normed))


def gelu_parts(values):
    square = values * values
    rate = -2.0 * GELU_C
    gate = 1.0 / (1.0 + jnp.exp(values * (rate + rate * 0.044715 * square)))
    output = values * gate
    slope = gate + output * (1.0 - gate) * (2.0 * GELU_C + 6.0 * GELU_C * 0.044715 * square)
    return output, slope


def dot(a, b):
    return jnp.dot(a, b, preferred_element_type=jnp.float32)


def dot_nt(a, b):
    return dot_on(a, b, 1, 1)


def dot_tn(a, b):
    return dot_on(a, b, 0, 0)


def column_sums(rows):
    ones = jnp.ones((8, rows.shape[0]), LOW)
    return dot(ones, rows)[0]


def local(
    dp_size,
    ranks,
    hidden_in,
    query_w,
    key_w,
    value_w,
    query_b,
    value_b,
    out_w,
    out_b,
    gain_attn,
    shift_attn,
    up_w,
    up_b,
    down_w,
    down_b,
    gain_ffn,
    shift_ffn,
    random_blocks,
    cotangent,
):
    own_rows, seqs_here, width = hidden_in.shape
    channels, hidden_units = query_w.shape[1], up_w.shape[1]
    length = own_rows * ranks
    chunks = CHUNKS
    piece = own_rows // chunks
    every = range(chunks)
    others = range(1, ranks)
    ring = Ring(dp_size)
    rows_in = hidden_in.reshape(own_rows, width)
    grad_out = cotangent.reshape(own_rows, width)
    lows = [c * piece for c in every]
    order = Order()
    run, tie = order.run, order.tie

    far_rows = fetch(rows_in, ranks)

    def project(x, *w):
        return (dot(x, w[0]) + w[1]).astype(LOW)

    def set_up(ids, q_w, k_w, v_w, q_b, v_b, *vectors):
        return (
            ring.table(own_rows // BLOCK),
            ids.reshape(ids.shape[0], -1),
            jnp.concatenate([q_w, k_w, v_w], 1),
            jnp.concatenate([q_b, jnp.zeros_like(q_b), v_b]).astype(jnp.float32),
            [v.reshape(1, -1) for v in vectors],
        )

    table, random_ids, qkv_w, qkv_b, vectors = run(
        set_up,
        random_blocks,
        query_w,
        key_w,
        value_w,
        query_b,
        value_b,
        out_b,
        gain_attn,
        shift_attn,
        up_b,
        down_b,
        gain_ffn,
        shift_ffn,
    )
    out_b, gain_attn, shift_attn, up_b, down_b, gain_ffn, shift_ffn = vectors
    near = run(project, rows_in, qkv_w, qkv_b)
    qkv = run(
        lambda n, w, b, *x: jnp.concatenate([n] + [project(p, w, b) for p in x], 0),
        near,
        qkv_w,
        qkv_b,
        *far_rows,
    )

    contexts, lses, attn_moved, attn_own = [], [], [], []
    for c in every:
        context, lse = run(lambda v: attend(v, random_ids, table, c, chunks, ranks), qkv)
        contexts.append(context)
        lses.append(lse)
        shares = [
            run(lambda x: product(x, j * piece, piece, out_w, False, LOW), context) for j in others
        ]
        attn_moved.append(hand_over(shares, ranks))
    for c in every:
        attn_own.append(
            run(lambda x: product(x, 0, piece, out_w, False, jnp.float32), contexts[c])
        )

    low_rows = (width, LOW)

    def norm_one(low, own, *moved):
        def body(*values):
            *terms, source, bias, gain, shift = values
            attn_out = functools.reduce(jnp.add, terms)
            resid = source + attn_out + bias
            normed, inverse = normalise(resid)
            hidden = gain * normed + shift
            inverse = jnp.broadcast_to(inverse, (inverse.shape[0], 128))
            return [hidden, normed, inverse], [resid * resid, attn_out * attn_out]

        return row_kernel(
            "norm_one",
            body,
            piece,
            [(own, 0)] + [(m, 0) for m in moved] + [(rows_in, low)],
            [out_b, gain_attn, shift_attn],
            [low_rows, low_rows, (128, jnp.float32)],
            8,
        )

    x, n1, i1, squares, acts, slopes, mlp_moved, mlp_own = ([] for _ in range(8))
    for c in every:
        low, n, i, sq = run(functools.partial(norm_one, lows[c]), attn_own[c], *attn_moved[c])
        n1.append(n)
        i1.append(i)
        squares.append(sq)
        x.append([low] + fetch(low, ranks))
        act, slope, own = run(lambda v: ffn_forward(v, up_w, up_b, down_w, jnp.float32), low)
        acts.append([act])
        slopes.append([slope])
        mlp_own.append(own)
    for c in every:
        shares = []
        for j in others:
            act, slope, share = run(lambda v: ffn_forward(v, up_w, up_b, down_w, LOW), x[c][j])
            acts[c].append(act)
            slopes[c].append(slope)
            shares.append(share)
        mlp_moved.append(hand_over(shares, ranks))

    def norm_two(low, own, h, *moved):
        def body(*values):
            *terms, before, g, bias, gain, shift = values
            mlp_out = functools.reduce(jnp.add, terms)
            normed, inverse = normalise(before + mlp_out + bias)
            back = norm_back(g, normed, inverse, gain)
            sums = [back, g * normed, g, mlp_out * mlp_out]
            return [back, gain * normed + shift], sums

        return row_kernel(
            "norm_two",
            body,
            piece,
            [(own, 0)] + [(m, 0) for m in moved] + [(h, 0), (grad_out, low)],
            [down_b, gain_ffn, shift_ffn],
            [low_rows, low_rows],
            8,
        )

    dmlp, layer_out, sums2 = [], [], []
    for c in every:
        low, out, sums = run(
            functools.partial(norm_two, lows[c]), mlp_own[c], x[c][0], *mlp_moved[c]
        )
        layer_out.append(out)
        sums2.append(sums)
        dmlp.append([low] + fetch(low, ranks))

    dups, dhid_moved, dhid_own, up_sums = [], [], [], []
    for c in every:
        dup, total, own = run(
            lambda d, s: ffn_back(d, s, down_w, up_w, jnp.float32), dmlp[c][0], slopes[c][0]
        )
        dups.append([dup])
        up_sums.append(total)
        dhid_own.append(own)
    for c in every:
        shares = []
        for j in others:
            dup, total, share = run(
                lambda d, s: ffn_back(d, s, down_w, up_w, LOW), dmlp[c][j], slopes[c][j]
            )
            dups[c].append(dup)
            up_sums.append(total)
            shares.append(share)
        dhid_moved.append(hand_over(shares, ranks))

    under_way = []

    def advance(*names):
        for name in names or [n for n, _ in under_way]:
            for entry in [e for e in under_way if e[0] == name]:
                if next(entry[1], "end") == "end":
                    under_way.remove(entry)

    class Grads:
        def __init__(self, rows, shares, sides, extra=None):
            self.rows, self.shares, self.extra = rows, shares, extra
            self.leaves, self.tree = jax.tree.flatten(sides)
            leaves = [x for x in self.leaves if not isinstance(x, int)]
            self.arrays = list({id(x): x for x in leaves}.values())
            self.results = []

        def halves(self, *cores):
            def call(t, extra, *tied):
                known = {id(x): v for x, v in zip(self.arrays, tied)}
                found = [x if isinstance(x, int) else known[id(x)] for x in self.leaves]
                sides = jax.tree.unflatten(self.tree, found)
                return grad_halves(t, cores, ring.chips, self.rows, self.shares, sides, extra)

            return run(call, table, self.extra, *self.arrays)

        def ring(self, name, kept, moved, pair=None):
            under_way.append((name, ring.steps(order, table, kept, moved, self.results, pair)))

    def pieces_of(parts):
        return [(p, 0, piece) for part in parts for p in part]

    ffn_rows = hidden_units // dp_size
    down_share = Share(dp_size, (hidden_units, width), ffn_rows, 0)
    up_share = Share(dp_size, (width, hidden_units), ffn_rows, down_share.end)
    ffn = Grads(
        ffn_rows,
        [down_share, up_share],
        [(pieces_of(acts), pieces_of(dmlp)), (pieces_of(x), pieces_of(dups))],
    )
    ffn_given, ffn_kept = ffn.halves(MATE, CORE)

    def norm_one_back(own, d2, n, i, *moved):
        def body(*values):
            *terms, normed, inverse, gain = values
            dhidden = functools.reduce(jnp.add, terms)
            back = norm_back(dhidden, normed, inverse[:, :1], gain)
            return [back], [back, dhidden * normed, dhidden]

        return row_kernel(
            "norm_one_back",
            body,
            piece,
            [(a, 0) for a in (own, *moved, d2, n, i)],
            [gain_attn],
            [low_rows],
            8,
        )

    dattn, sums1, dcontexts = [], [], []
    for c in every:
        low, sums = run(
            norm_one_back, dhid_own[c], dmlp[c][0], n1[c], i1[c], *dhid_moved[c]
        )
        sums1.append(sums)
        dattn.append([low] + fetch(low, ranks))
    ffn_moved = ring.mate(tie(ffn_given))
    for c in every:
        dcontexts.append(
            run(lambda d: product(d, 0, piece, out_w, True, LOW, None, ranks, 0), dattn[c][0])
        )
    norms = run(sum_kernel, sums1, sums2, squares)
    norms = [norms] + fetch(norms, ranks)
    ffn.ring("ffn", ffn_kept, ffn_moved)
    advance("ffn")

    dq_parts, sums = [], []
    for c in every:
        dcontext = dcontexts[c]
        for j in others:
            dcontext = run(
                lambda d, whole: product(d, 0, piece, out_w, True, LOW, whole, ranks, j),
                dattn[c][j],
                dcontext,
            )
        advance("ffn")
        dq, *sums = run(
            lambda v, d, l, e, s: jax.tree.leaves(
                attend_back(v, d, l, random_ids, table, e, s, c, chunks, ranks)
            ),
            qkv,
            dcontext,
            lses[c],
            dq_parts,
            sums,
        )
        dq_parts.append(dq)
    dqkv, bias_sums = dq, sums[0]

    attn_rows = width // dp_size
    attn_shares = [Share(dp_size, (width, 3 * channels), attn_rows, 0)]
    attn_sides = [
        (
            [(x, 0, own_rows) for x in [rows_in] + far_rows],
            [(dqkv, j * own_rows, own_rows) for j in range(ranks)],
        )
    ]
    with_out = channels % 256 == 0
    if with_out:
        attn_shares.append(Share(dp_size, (channels, width), attn_rows, attn_shares[0].end))
        attn_sides.append(
            (
                [(contexts[c], j * piece, piece) for c in every for j in range(ranks)],
                [(dattn[c][j], 0, piece) for c in every for j in range(ranks)],
            )
        )
    values = run(functools.partial(row_values, dp_size), norms, up_sums, bias_sums)
    pair = attn_shares[-1].end
    attn = Grads(attn_rows, attn_shares, attn_sides, values)
    (given,) = attn.halves(MATE)
    advance("ffn")
    moved = ring.mate(tie(given))
    shares = [
        run(lambda d: product(d, j * own_rows, own_rows, qkv_w, True, LOW), dqkv) for j in others
    ]
    dinput_moved = hand_over(shares, ranks)
    (kept,) = attn.halves(CORE)
    attn.ring("attn", kept, moved, pair)
    advance("attn")
    dinput_own = run(lambda d: product(d, 0, own_rows, qkv_w, True, jnp.float32), dqkv)
    advance("ffn", "attn")
    grad_input = run(
        lambda own, d, *m: (plus(own, m) + jnp.concatenate(d, 0)).astype(LOW),
        dinput_own,
        [d[0] for d in dattn],
        *dinput_moved,
    )
    totals = {}
    entries = float(own_rows * ranks * dp_size * seqs_here * width)
    ffn_outs = [((g.shard, g.columns), g.moves) for g in (down_share, up_share)]
    up_rows = -(-hidden_units // width)

    def spread(value):
        value = value.reshape(dp_size, width)
        return (
            [value[i] for i in range(6)],
            jnp.sqrt(value[6, :3] / entries),
            value[8 + up_rows, :channels],
            value[8 + up_rows, channels : 2 * channels],
            value[8 : 8 + up_rows].reshape(-1)[:hidden_units],
        )

    while under_way:
        advance()
        for n, name in enumerate(("down", "up")):
            if ffn.results and name not in totals:
                (totals[name],) = run(
                    lambda *p: ring.place_pieces(table, p, [ffn_outs[n]]), *ffn.results
                )
                break
    everything = slice(0, attn_rows)
    attn_outs = []
    for i in range(3):
        cut = slice(i * channels, (i + 1) * channels)
        attn_outs.append(
            ((attn_rows, channels), [(everything, slice(0, channels), everything, cut)])
        )
    lines = slice(0, 8)
    attn_outs.append(
        ((8, 128), [(lines, slice(0, 128), (lines, slice(8, 16)), slice(pair, pair + 128))])
    )
    if with_out:
        attn_outs.append(((attn_shares[1].shard, width), attn_shares[1].moves))
    grad_q, grad_k, grad_v, value, *rest = run(lambda *p: ring.place_pieces(table, p, attn_outs), *attn.results)
    if with_out:
        (grad_out_w,) = rest
    else:
        partial = sum(
            dot_tn(contexts[c], jnp.concatenate(dattn[c], 0)) for c in every
        )
        grad_out_w = lax.psum(partial.astype(LOW), "dp").astype(jnp.float32)
    grad_down_w, grad_up_w = totals["down"], totals["up"]
    vectors, rms_stats, *biases = spread(value)
    shape = hidden_in.shape
    return (
        jnp.concatenate(layer_out, 0).reshape(shape),
        grad_input.reshape(shape),
        grad_q,
        grad_k,
        grad_v,
        biases[0],
        biases[1],
        grad_out_w,
        vectors[0],
        vectors[1],
        vectors[2],
        grad_up_w,
        biases[2],
        grad_down_w,
        vectors[3],
        vectors[4],
        vectors[5],
        rms_stats,
    )


def solution(mesh):
    rows = P("tensor", "dp", None)
    columns, split, whole = P(None, "tensor"), P("tensor"), P()
    first = P("tensor", None)
    return jax.shard_map(
        functools.partial(local, mesh.shape["dp"], mesh.shape["tensor"]),
        mesh=mesh,
        in_specs=(
            rows,
            columns,
            columns,
            columns,
            split,
            split,
            first,
            whole,
            whole,
            whole,
            columns,
            split,
            first,
            whole,
            whole,
            whole,
            P("tensor", None, None),
            rows,
        ),
        out_specs=(
            rows,
            rows,
            columns,
            columns,
            columns,
            split,
            split,
            first,
            whole,
            whole,
            whole,
            columns,
            split,
            first,
            whole,
            whole,
            whole,
            whole,
        ),
        check_vma=False,
    )
```

```python
import functools
import math

import jax
import jax.numpy as jnp
from jax import lax
from jax.experimental import pallas as pl
from jax.experimental.pallas import tpu as pltpu
from jax.sharding import PartitionSpec as P

HD = 64
BLOCK = 64
NEG = -1e30
EPS = 1e-12
GELU_C = math.sqrt(2.0 / math.pi)
CHUNKS = 2
LOW = jnp.bfloat16
FIRST, CORE, MATE, PLACE = range(4)
COST = pl.CostEstimate(flops=1024, bytes_accessed=1024, transcendentals=0)


def dot_on(left, right, left_dim, right_dim):
    return lax.dot_general(
        left,
        right,
        (((left_dim,), (right_dim,)), ((), ())),
        preferred_element_type=jnp.float32,
    )


def lane_masks(width, value):
    lane = lax.broadcasted_iota(jnp.int32, (1, width), 1) // HD
    return [jnp.where(lane == h, value, 0.0).astype(LOW) for h in range(width // HD)]


def stack_heads(rows, masks):
    return jnp.concatenate([rows * m for m in masks], 0)


def unstack_heads(stacked, heads):
    lane = lax.broadcasted_iota(jnp.int32, (1, stacked.shape[1]), 1) // HD
    out = stacked[:BLOCK]
    for h in range(1, heads):
        out = jnp.where(lane == h, stacked[h * BLOCK : (h + 1) * BLOCK], out)
    return out


def block_at(index):
    return pl.ds(pl.multiple_of(index * BLOCK, BLOCK), BLOCK)


class Plan:
    def __init__(self, chunk, chunks, ranks, length, rand, heads):
        self.blocks = length // BLOCK
        self.rank_blocks = self.blocks // ranks
        self.chunk_blocks = self.rank_blocks // chunks
        self.chunk = chunk
        self.rand = rand
        self.heads = heads
        taken = [
            j * self.rank_blocks + chunk * self.chunk_blocks + r
            for j in range(ranks)
            for r in range(self.chunk_blocks)
        ]
        self.ends = [b for b in taken if b in (0, self.blocks - 1)]
        middles = [b for b in taken if b not in self.ends]
        self.ranges = []
        for b in middles:
            if self.ranges and self.ranges[-1][1] == b:
                self.ranges[-1][1] = b + 1
            else:
                self.ranges.append([b, b + 1])

    def local(self, block, first):
        return lax.rem(block - first + self.blocks, self.blocks)

    def inner(self, local):
        part = lax.div(local, self.rank_blocks)
        rest = local - part * self.rank_blocks
        return part * self.chunk_blocks + rest - self.chunk * self.chunk_blocks

    def fixed(self, block, first):
        wanted = (jnp.int32(0), jnp.int32(self.blocks - 1), block - 1, block, block + 1)
        return [self.local(w, first) for w in wanted]

    def random(self, rb_ref, group, block, first):
        return [
            [
                self.local(rb_ref[group * self.heads + h, (block - 1) * self.rand + r], first)
                for h in range(self.heads)
            ]
            for r in range(self.rand)
        ]

    def run(self, one, unroll):
        for low, high in self.ranges:
            count = high - low
            main = count - count % unroll
            if main > unroll:

                @pl.loop(0, main // unroll)
                def _(step, low=low):
                    for u in range(unroll):
                        one(low + step * unroll + u)
            else:
                main = 0
            for x in range(main, count):
                one(jnp.int32(low + x))


def pick_tiles(ref, fixed, rands):
    width = ref.shape[1]
    column = min(128, width)
    per = column // HD
    lane = lax.broadcasted_iota(jnp.int32, (1, column), 1) // HD
    parts = [ref[block_at(f), :] for f in fixed]
    for per_head in rands:
        columns = []
        for c in range(width // column):
            tile = None
            for p in range(per):
                x = ref[block_at(per_head[c * per + p]), c * column : (c + 1) * column]
                tile = x if tile is None else jnp.where(lane == p, x, tile)
            columns.append(tile)
        parts.append(jnp.concatenate(columns, 1) if len(columns) > 1 else columns[0])
    return jnp.concatenate(parts, 0)


def attend_kernel(plan, unroll, table_ref, rb_ref, q_ref, k_ref, v_ref, o_ref, lse_ref):
    group = pl.program_id(0)
    first = table_ref[FIRST]
    heads = plan.heads
    masks = lane_masks(q_ref.shape[1], HD**-0.5)

    def finish(scores, values, place):
        top = jnp.max(scores, 1, keepdims=True)
        weights = jnp.exp(scores - top)
        total = jnp.sum(weights, 1, keepdims=True)
        out = dot_on(weights.astype(LOW), values, 1, 0) * (1.0 / total)
        o_ref[block_at(place), :] = unstack_heads(out, heads).astype(LOW)
        wide = jnp.broadcast_to(top + jnp.log(total), (heads * BLOCK, 128))
        lse_ref[0, pl.ds(place, 1), :] = jnp.transpose(wide)[0:1, :]

    def one(block):
        fixed = plan.fixed(block, first)
        rands = plan.random(rb_ref, group, block, first)
        queries = stack_heads(q_ref[block_at(fixed[3]), :], masks)
        scores = dot_on(queries, pick_tiles(k_ref, fixed, rands), 1, 1)
        lane = lax.broadcasted_iota(jnp.int32, (1, 2 * BLOCK), 1)
        drop = ((block == 1) & (lane < BLOCK)) | (
            (block == plan.blocks - 2) & (lane >= BLOCK)
        )
        scores = jnp.concatenate(
            [jnp.where(drop, NEG, scores[:, : 2 * BLOCK]), scores[:, 2 * BLOCK :]], 1
        )
        finish(scores, pick_tiles(v_ref, fixed, rands), plan.inner(fixed[3]))

    plan.run(one, unroll)
    for b in plan.ends:
        local = plan.local(jnp.int32(b), first)
        queries = stack_heads(q_ref[block_at(local), :], masks)
        finish(dot_on(queries, k_ref[...], 1, 1), v_ref[...], plan.inner(local))


def attend_back_kernel(plan, unroll, earlier, last, table_ref, rb_ref, q_ref, k_ref, v_ref, *refs):
    do_ref, lse_ref, *refs = refs
    dq_in, refs = refs[:earlier], refs[earlier:]
    if earlier:
        dk_in, dv_in, *refs = refs
    if last:
        all_ref, bias_ref, dq_ref, dk_acc, dv_acc = refs
    else:
        dq_ref, dk_acc, dv_acc = refs
    group = pl.program_id(0)
    first = table_ref[FIRST]
    heads = plan.heads
    width = q_ref.shape[1]
    query_masks, out_masks = lane_masks(width, HD**-0.5), lane_masks(width, 1.0)
    column = min(128, width)
    per = column // HD
    lane = lax.broadcasted_iota(jnp.int32, (1, column), 1) // HD
    if earlier:
        dk_acc[...] = dk_in[...]
        dv_acc[...] = dv_in[...]
    else:
        dk_acc[...] = jnp.zeros_like(dk_acc)
        dv_acc[...] = jnp.zeros_like(dv_acc)

    def core(scores, keys, values, queries, douts, place):
        probs = jnp.exp(scores - lse_ref[0, pl.ds(place, 1), :])
        dprobs = dot_on(values, douts, 1, 1)
        row_dot = jnp.sum(probs * dprobs, 0, keepdims=True)
        dscores = (probs * (dprobs - row_dot)).astype(LOW)
        dv = dot_on(probs.astype(LOW), douts, 1, 0)
        dk = dot_on(dscores, queries, 1, 0)
        dq = unstack_heads(dot_on(dscores, keys, 0, 0), heads) * (HD**-0.5)
        dq_ref[block_at(place), :] = dq.astype(LOW)
        return dk, dv

    def add_tiles(acc, value, fixed, rands):
        for n, f in enumerate(fixed):
            acc[block_at(f), :] += value[n * BLOCK : (n + 1) * BLOCK]
        for r, per_head in enumerate(rands):
            tile = value[(5 + r) * BLOCK : (6 + r) * BLOCK]
            for h in range(heads):
                c = h // per
                cut = slice(c * column, (c + 1) * column)
                acc[block_at(per_head[h]), cut] += jnp.where(lane == h % per, tile[:, cut], 0.0)

    def one(block):
        fixed = plan.fixed(block, first)
        rands = plan.random(rb_ref, group, block, first)
        place = plan.inner(fixed[3])
        queries = stack_heads(q_ref[block_at(fixed[3]), :], query_masks)
        douts = stack_heads(do_ref[block_at(place), :], out_masks)
        keys = pick_tiles(k_ref, fixed, rands)
        values = pick_tiles(v_ref, fixed, rands)
        scores = dot_on(keys, queries, 1, 1)
        scores = jnp.concatenate(
            [
                jnp.where(block == 1, NEG, scores[:BLOCK]),
                jnp.where(block == plan.blocks - 2, NEG, scores[BLOCK : 2 * BLOCK]),
                scores[2 * BLOCK :],
            ],
            0,
        )
        dk, dv = core(scores, keys, values, queries, douts, place)
        add_tiles(dk_acc, dk, fixed, rands)
        add_tiles(dv_acc, dv, fixed, rands)

    for b in plan.ends:
        local = plan.local(jnp.int32(b), first)
        place = plan.inner(local)
        queries = stack_heads(q_ref[block_at(local), :], query_masks)
        douts = stack_heads(do_ref[block_at(place), :], out_masks)
        scores = dot_on(k_ref[...], queries, 1, 1)
        dk, dv = core(scores, k_ref[...], v_ref[...], queries, douts, place)
        dk_acc[...] += dk
        dv_acc[...] += dv
    plan.run(one, unroll)
    if last:
        channels = all_ref.shape[1] // 3
        rows = plan.chunk_blocks * BLOCK
        chunks = earlier + 1
        for at in range(0, channels, width):

            @pl.when(group * width == at)
            def _(at=at):
                for c, source in enumerate([*dq_in, dq_ref]):
                    for j in range(plan.blocks // plan.rank_blocks):
                        low = (j * chunks + c) * rows
                        all_ref[low : low + rows, at : at + width] = source[j * rows : (j + 1) * rows]
                for n, acc in ((1, dk_acc), (2, dv_acc)):
                    cut = n * channels + at
                    all_ref[:, cut : cut + width] = acc[...].astype(LOW)
                for n in (0, 2):
                    cut = slice(n * channels + at, n * channels + at + width)
                    total = jnp.sum(all_ref[:, cut].astype(jnp.float32), 0, keepdims=True)
                    cut = slice(n // 2 * channels + at, n // 2 * channels + at + width)
                    bias_ref[:, cut] = jnp.broadcast_to(total, (8, width))


def group_width(channels):
    return min(256, channels)


def packed_specs(length, channels):
    width = group_width(channels)
    groups = channels // width
    return [
        pl.BlockSpec((length, width), lambda g, *_, n=n: (0, n * groups + g)) for n in range(3)
    ]


def attend(qkv, random_ids, table, chunk, chunks, ranks):
    length, channels = qkv.shape[0], qkv.shape[1] // 3
    width = group_width(channels)
    groups, heads = channels // width, width // HD
    plan = Plan(chunk, chunks, ranks, length, random_ids.shape[1] // (length // BLOCK - 2), heads)
    rows = length // chunks
    return pl.pallas_call(
        functools.partial(attend_kernel, plan, 4),
        grid_spec=pltpu.PrefetchScalarGridSpec(
            num_scalar_prefetch=2,
            grid=(groups,),
            in_specs=packed_specs(length, channels),
            out_specs=[
                pl.BlockSpec((rows, width), lambda g, *_: (0, g)),
                pl.BlockSpec((1, rows // BLOCK, width), lambda g, *_: (g, 0, 0)),
            ],
        ),
        out_shape=[
            jax.ShapeDtypeStruct((rows, channels), LOW),
            jax.ShapeDtypeStruct((groups, rows // BLOCK, width), jnp.float32),
        ],
        compiler_params=pltpu.CompilerParams(vmem_limit_bytes=12 << 20),
        cost_estimate=COST,
        name="attend",
    )(table, random_ids, qkv, qkv, qkv)


def attend_back(qkv, dout, lse, random_ids, table, earlier, sums, chunk, chunks, ranks):
    length, channels = qkv.shape[0], qkv.shape[1] // 3
    width = group_width(channels)
    groups, heads = channels // width, width // HD
    plan = Plan(chunk, chunks, ranks, length, random_ids.shape[1] // (length // BLOCK - 2), heads)
    rows = length // chunks
    last = chunk == chunks - 1
    part = pl.BlockSpec((rows, width), lambda g, *_: (0, g))
    full = pl.BlockSpec((length, width), lambda g, *_: (0, g))
    sum_shape = jax.ShapeDtypeStruct((length, channels), jnp.float32)
    if last:
        bias = (8, 2 * channels)
        out_specs = [pl.BlockSpec(shape, lambda g, *_: (0, 0)) for shape in (qkv.shape, bias)]
        out_shape = [
            jax.ShapeDtypeStruct(qkv.shape, LOW),
            jax.ShapeDtypeStruct(bias, jnp.float32),
        ]
        scratch = [pltpu.VMEM((rows, width), LOW)] + [pltpu.VMEM((length, width), jnp.float32)] * 2
    else:
        out_specs = [part, full, full]
        out_shape = [jax.ShapeDtypeStruct((rows, channels), LOW), sum_shape, sum_shape]
        scratch = []
    return pl.pallas_call(
        functools.partial(attend_back_kernel, plan, 3, len(earlier), last),
        grid_spec=pltpu.PrefetchScalarGridSpec(
            num_scalar_prefetch=2,
            grid=(groups,),
            in_specs=packed_specs(length, channels)
            + [part, pl.BlockSpec((1, rows // BLOCK, width), lambda g, *_: (g, 0, 0))]
            + [part] * len(earlier)
            + [full] * len(sums),
            out_specs=out_specs,
            scratch_shapes=scratch,
        ),
        out_shape=out_shape,
        compiler_params=pltpu.CompilerParams(vmem_limit_bytes=(28 if last else 18) << 20),
        cost_estimate=COST,
        name="attend_back",
    )(table, random_ids, qkv, qkv, qkv, dout, lse, *earlier, *sums)


class Order:
    def __init__(self):
        self.token = None

    def tie(self, values):
        if self.token is None:
            return values
        values, self.token = lax.optimization_barrier((values, self.token))
        return values

    def run(self, function, *values):
        out = function(*self.tie(values))
        self.token = min(jax.tree.leaves(out), key=lambda leaf: leaf.size)
        return out


def fetch(rows, ranks):
    return [
        lax.ppermute(rows, "tensor", [((k + s) % ranks, k) for k in range(ranks)])
        for s in range(1, ranks)
    ]


def hand_over(shares, ranks):
    return [
        lax.ppermute(share, "tensor", [(k, (k + s) % ranks) for k in range(ranks)])
        for s, share in enumerate(shares, 1)
    ]


def plus(own, moved):
    for m in moved:
        own = own + m.astype(jnp.float32)
    return own


class Ring:
    def __init__(self, size):
        self.size = size
        self.chips = size // 2
        self.order = list(range(0, self.chips, 2)) + list(range(1, self.chips, 2))[::-1]
        self.ahead = self.chips // 2
        self.behind = self.chips - 1 - self.ahead

    def table(self, own_blocks):
        index = lax.axis_index("dp")
        core, chip = lax.rem(index, 2), lax.div(index, 2)
        half = lax.div(chip, 2)
        place = jnp.where(lax.rem(chip, 2) == 0, half, self.chips - 1 - half)
        first = lax.axis_index("tensor") * own_blocks
        return jnp.stack([first, core, 1 - core, place]).astype(jnp.int32)

    def shift(self, value, by):
        pairs = []
        for q in range(self.chips):
            source, target = self.order[q], self.order[(q + by) % self.chips]
            pairs += [(2 * source + c, 2 * target + c) for c in range(2)]
        return lax.ppermute(value, "dp", pairs)

    def mate(self, value):
        return lax.ppermute(value, "dp", [(i, i ^ 1) for i in range(self.size)])

    def add(self, table, kept, moved, offset, part, pair, *more):
        chips, rows, columns = kept.shape
        block = rows // 2 if rows % 32 == 0 else rows
        steps = rows // block if part is None else 1

        def body(table_ref, kept_ref, moved_ref, *refs):
            *refs, out_ref = refs
            total = kept_ref[0].astype(jnp.float32) + moved_ref[0].astype(jnp.float32)
            for ref, (array, half) in zip(refs, more):
                term = ref[...].astype(jnp.float32)
                if array.shape[0] < rows and part is None:
                    term = jnp.where(pl.program_id(0) == half, term, 0.0)
                total = total + term
            out_ref[...] = total.astype(LOW)
            if pair is not None and part != 1:

                @pl.when(pl.program_id(0) == 0)
                def _():
                    out_ref[0:16, pair:] = two_parts(total[0:8, pair:] + total[8:16, pair:])

        shard = pl.BlockSpec(
            (1, block, columns),
            lambda i, t: (lax.rem(t[PLACE] + offset + 2 * chips, chips), i + (part or 0), 0),
        )
        each = pl.BlockSpec((block, columns), lambda i, t: (i, 0))
        fixed = pl.BlockSpec((block, columns), lambda i, t: (0, 0))
        return pl.pallas_call(
            body,
            grid_spec=pltpu.PrefetchScalarGridSpec(
                num_scalar_prefetch=1,
                grid=(steps,),
                in_specs=[shard, shard] + [fixed if a.shape[0] < rows else each for a, _ in more],
                out_specs=each,
            ),
            out_shape=jax.ShapeDtypeStruct((block * steps, columns), LOW),
            compiler_params=pltpu.CompilerParams(vmem_limit_bytes=8 << 20),
            cost_estimate=COST,
            name="ring_add",
        )(table, kept, moved, *[a for a, _ in more])

    def steps(self, order, table, kept, moved, results, pair=None):
        ahead = self.ahead
        rows = kept.shape[1]
        split = rows % 32 == 0

        def add(offset, part, *more):
            halves = [h for _, h in more]
            return order.run(
                lambda t, k, m, *more: self.add(t, k, m, offset, part, pair, *zip(more, halves)),
                table,
                kept,
                moved,
                *[a for a, _ in more],
            )

        right = add(ahead, 0 if split else None)
        left = add(-ahead, 1) if split else None
        for j in range(1, ahead + 1):
            right = self.shift(right, 1)
            left = None if left is None else self.shift(left, -1)
            yield
            if j < ahead:
                right = add(ahead - j, None, (right, 0))
                left = add(j - ahead, None, *([] if left is None else [(left, 1)]))
        own = add(0, None, (right, 0), (left, 0))
        mine, theirs = {0: own}, {0: order.tie(self.mate(own))}
        right = left = own
        for j in range(1, ahead + 1):
            if j == ahead and split:
                half = rows // 2
                right, left = order.run(lambda r, l: (r[:half], l[half:]), right, left)
            right = self.shift(right, 1)
            left = self.shift(left, -1) if j < ahead or split else None
            yield
            right, left = order.tie((right, left))
            mine[-j], mine[j] = right, left
            theirs[-j] = self.mate(right)
            theirs[j] = None if left is None else self.mate(left)
        offsets = range(-ahead, ahead + 1)
        results += [[side[o] for o in offsets] for side in (mine, theirs)]

    def place_pieces(self, table, pieces, outs):
        chips, ahead = self.chips, self.ahead
        size = pieces[0][ahead].shape[0]
        cuts = [move[3] for _, moves in outs for move in moves]
        first_lane = min(cut.start for cut in cuts)
        wide = max(cut.stop for cut in cuts) - first_lane
        arrays, places = [], []
        for side in pieces:
            entries = []
            for offset, array in zip(range(-ahead, ahead + 1), side):
                if array is not None:
                    first = size - array.shape[0] if offset == ahead else 0
                    entries.append((offset, len(arrays), first, array.shape[0]))
                    arrays.append(array)
            places.append(entries)

        def body(table_ref, *refs):
            piece_refs, out_refs = refs[: len(arrays)], refs[len(arrays) :]

            def put(entries):
                for offset, at, first, count in entries:
                    slot = lax.rem(table_ref[PLACE] + offset + chips, chips)
                    for ref, (_, moves) in zip(out_refs, outs):
                        for own_rows, own_columns, rows, cut in moves:
                            lanes = slice(cut.start - first_lane, cut.stop - first_lane)
                            if isinstance(rows, tuple):
                                if first == 0:
                                    both = [piece_refs[at][r, lanes].astype(jnp.float32) for r in rows]
                                    ref[0, slot, own_rows, own_columns] = both[0] + both[1]
                                continue
                            low, high = max(rows.start, first), min(rows.stop, first + count)
                            if low >= high:
                                continue
                            there = slice(
                                own_rows.start + low - rows.start,
                                own_rows.start + high - rows.start,
                            )
                            value = piece_refs[at][low - first : high - first, lanes]
                            ref[0, slot, there, own_columns] = value.astype(jnp.float32)

            for i, entries in enumerate(places):
                pl.when(pl.program_id(0) == i)(functools.partial(put, entries))

        def target(i, t):
            return (jnp.where(i == 0, t[CORE], t[MATE]), 0, 0, 0)

        shapes = [(chips, *shape) for shape, _ in outs]
        results = pl.pallas_call(
            body,
            grid_spec=pltpu.PrefetchScalarGridSpec(
                num_scalar_prefetch=1,
                grid=(2,),
                in_specs=[
                    pl.BlockSpec(
                        (a.shape[0], wide),
                        lambda i, w: (0, first_lane // wide),
                        pipeline_mode=pl.Buffered(1),
                    )
                    for a in arrays
                ],
                out_specs=[pl.BlockSpec((1, *shape), target) for shape in shapes],
            ),
            out_shape=[jax.ShapeDtypeStruct((2, *shape), jnp.float32) for shape in shapes],
            compiler_params=pltpu.CompilerParams(vmem_limit_bytes=40 << 20),
            cost_estimate=COST,
            name="place_pieces",
        )(table, *arrays)
        return [out.reshape(-1, out.shape[-1]) for out in results]


class Share:
    def __init__(self, size, shape, rows, at):
        self.array = 0
        self.shard = shape[0] // size
        self.columns = shape[1]
        self.moves = []
        if self.shard <= rows:
            wide = self.columns // (rows // self.shard)
            for i in range(rows // self.shard):
                there = slice(i * self.shard, (i + 1) * self.shard)
                cut = slice(i * wide, (i + 1) * wide)
                self.moves.append((slice(0, self.shard), cut, there, slice(at, at + wide)))
            self.end = at + wide
        else:
            for i in range(self.shard // rows):
                low = at + i * self.columns
                here = slice(i * rows, (i + 1) * rows)
                self.moves.append(
                    (here, slice(0, self.columns), slice(0, rows), slice(low, low + self.columns))
                )
            self.end = at + (self.shard // rows) * self.columns


def two_parts(values):
    high = values.astype(LOW)
    low = (values - high.astype(jnp.float32)).astype(LOW)
    return jnp.concatenate([high, low], 0)


def grad_halves(table, cores, chips, rows, shares, sides, extra=None):
    count = max(share.array for share in shares) + 1
    columns = [max(share.end for share in shares if share.array == n) for n in range(count)]
    halves = [share.shard * chips for share in shares]
    steps = min(halves) // 128
    per = chips // steps
    arrays, where = [] if extra is None else [extra], []
    at = columns[0]
    if extra is not None:
        columns[0] += 128
    for lefts, rights in sides:
        place = []
        for array, low, size in [*lefts, *rights]:
            known = [n for n, other in enumerate(arrays) if other is array]
            if not known:
                arrays.append(array)
            place.append((known[0] if known else len(arrays) - 1, slice(low, low + size)))
        where.append((place[: len(lefts)], place[len(lefts) :]))

    def body(table_ref, *refs):
        refs, out_refs = refs[: len(arrays)], refs[len(arrays) :]

        @pl.loop(0, len(cores) * steps)
        def _(turn):
            n_out = lax.div(turn, steps)
            step = lax.rem(turn, steps)
            core = table_ref[cores[0]]
            if len(cores) == 2:
                core = jnp.where(n_out == 0, core, table_ref[cores[1]])
            grads = []
            for half, (left, right) in zip(halves, where):
                tile = half // steps
                low = pl.multiple_of((core * steps + step) * tile, tile)
                grad = None
                for (n, n_rows), (m, m_rows) in zip(left, right):
                    term = dot_on(refs[n][n_rows, pl.ds(low, tile)], refs[m][m_rows, :], 0, 0)
                    grad = term if grad is None else grad + term
                grads.append(grad.astype(LOW))

            def put(core_refs):
                for n in range(per if extra is not None else 0):
                    row = refs[0][pl.ds(core * chips + step * per + n, 1), :]
                    lines = [row[:, k * 128 : (k + 1) * 128] for k in range(row.shape[1] // 128)]
                    block = two_parts(jnp.concatenate(lines, 0))
                    if rows > 16:
                        fill = jnp.zeros((rows - 16, 128), LOW)
                        block = jnp.concatenate([block, fill], 0)
                    core_refs[0][step * per + n, :, at : at + 128] = block
                for grad, share in zip(grads, shares):
                    ref = core_refs[share.array]
                    for n in range(per):
                        for own_rows, own_columns, there, cut in share.moves:
                            first = n * share.shard
                            ref[step * per + n, there, cut] = grad[
                                first + own_rows.start : first + own_rows.stop, own_columns
                            ]

            for n in range(len(cores)):
                core_refs = out_refs[n * count : (n + 1) * count]
                if len(cores) == 1:
                    put(core_refs)
                else:
                    pl.when(n_out == n)(functools.partial(put, core_refs))

    vmem = pl.BlockSpec(memory_space=pltpu.VMEM)
    outs = pl.pallas_call(
        body,
        in_specs=[pl.BlockSpec(memory_space=pltpu.SMEM)] + [vmem] * len(arrays),
        out_specs=[vmem] * (len(cores) * count),
        out_shape=[jax.ShapeDtypeStruct((chips, rows, c), LOW) for c in columns] * len(cores),
        compiler_params=pltpu.CompilerParams(vmem_limit_bytes=16 << 20),
        cost_estimate=COST,
        name="grad_halves",
    )(table, *arrays)
    return [outs[n] for n in range(len(cores))]


def row_kernel(name, body, rows, arrays, vectors, out_types, sum_rows):
    block = min(128, rows)
    n = len(arrays) + len(vectors)

    def kernel(*refs):
        values, sums = body(*[r[...].astype(jnp.float32) for r in refs[:n]])
        for ref, value in zip(refs[n:-1], values, strict=True):
            ref[...] = value.astype(ref.dtype)
        sums = [jnp.sum(v, 0, keepdims=True) for v in sums]
        sums = jnp.concatenate(sums + [jnp.zeros_like(sums[0])] * (sum_rows - len(sums)), 0)

        @pl.when(pl.program_id(0) == 0)
        def _():
            refs[-1][...] = sums

        @pl.when(pl.program_id(0) > 0)
        def _():
            refs[-1][...] += sums

    width = vectors[0].shape[-1]
    in_specs = [
        pl.BlockSpec((block, a.shape[1]), lambda i, at=low // block: (at + i, 0))
        for a, low in arrays
    ]
    in_specs += [pl.BlockSpec((1, width), lambda i: (0, 0))] * len(vectors)
    out_specs = [pl.BlockSpec((block, w), lambda i: (i, 0)) for w, _ in out_types]
    return pl.pallas_call(
        kernel,
        grid=(rows // block,),
        in_specs=in_specs,
        out_specs=out_specs + [pl.BlockSpec((sum_rows, width), lambda i: (0, 0))],
        out_shape=[jax.ShapeDtypeStruct((rows, w), t) for w, t in out_types]
        + [jax.ShapeDtypeStruct((sum_rows, width), jnp.float32)],
        compiler_params=pltpu.CompilerParams(vmem_limit_bytes=12 << 20),
        cost_estimate=COST,
        name=name,
    )(*[a for a, _ in arrays], *vectors)


def product(x, low, rows, weights, transposed, out_type, into=None, parts=1, part=0):
    inner = x.shape[1]
    outer = weights.shape[0 if transposed else 1]
    tile = min(512, outer)

    def body(x_ref, w_ref, *refs):
        refs[-1][...] = dot_on(x_ref[...], w_ref[...], 1, 1 if transposed else 0).astype(out_type)

    if transposed:
        spec = pl.BlockSpec((tile, inner), lambda i: (i, 0))
    else:
        spec = pl.BlockSpec((inner, tile), lambda i: (0, i))
    more = [] if into is None else [into]
    return pl.pallas_call(
        body,
        grid=(outer // tile,),
        in_specs=[pl.BlockSpec((rows, inner), lambda i: (low // rows, 0)), spec]
        + [pl.BlockSpec(memory_space=pl.ANY)] * len(more),
        out_specs=pl.BlockSpec((rows, tile), lambda i: (part, i)),
        out_shape=jax.ShapeDtypeStruct((rows * parts, outer), out_type),
        input_output_aliases={2: 0} if more else {},
        compiler_params=pltpu.CompilerParams(vmem_limit_bytes=10 << 20),
        cost_estimate=COST,
        name="product",
    )(x, weights, *more)


def sum_kernel(one, two, squares):
    flat = [*one, *two, *squares]
    width = one[0].shape[1]

    def body(*refs):
        *refs, out_ref = refs

        def total(count):
            nonlocal refs
            mine, refs = refs[:count], refs[count:]
            return functools.reduce(jnp.add, [r[...] for r in mine])

        first, second, third = (total(len(g)) for g in (one, two, squares))
        lane = lax.broadcasted_iota(jnp.int32, (1, width), 1)
        row = jnp.zeros((1, width), jnp.float32)
        for n, source in enumerate((third[0:1], third[1:2], second[3:4])):
            row = jnp.where(lane == n, jnp.sum(source, 1, keepdims=True), row)
        out_ref[...] = jnp.concatenate([first[0:3], second[0:3], row, jnp.zeros_like(row)], 0)

    vmem = pl.BlockSpec(memory_space=pltpu.VMEM)
    return pl.pallas_call(
        body,
        in_specs=[vmem] * len(flat),
        out_specs=vmem,
        out_shape=jax.ShapeDtypeStruct((8, width), jnp.float32),
        compiler_params=pltpu.CompilerParams(vmem_limit_bytes=4 << 20),
        cost_estimate=COST,
        name="sum_kernel",
    )(*flat)


def row_values(size, norms, up_sums, biases):
    width = norms[0].shape[1]
    up_rows = -(-up_sums[0].shape[1] // width)
    flat = [*norms, *up_sums, biases]

    def body(*refs):
        *refs, out_ref = refs
        out_ref[...] = jnp.zeros_like(out_ref)
        out_ref[0:8, :] = functools.reduce(jnp.add, [r[...] for r in refs[: len(norms)]])
        ups = functools.reduce(jnp.add, [r[...] for r in refs[len(norms) : -1]])
        for n in range(up_rows):
            part = ups[:, n * width : (n + 1) * width]
            out_ref[8 + n : 9 + n, 0 : part.shape[1]] = part
        bias = refs[-1][0:1]
        out_ref[8 + up_rows : 9 + up_rows, 0 : bias.shape[1]] = bias

    vmem = pl.BlockSpec(memory_space=pltpu.VMEM)
    return pl.pallas_call(
        body,
        in_specs=[vmem] * len(flat),
        out_specs=vmem,
        out_shape=jax.ShapeDtypeStruct((size, width), jnp.float32),
        compiler_params=pltpu.CompilerParams(vmem_limit_bytes=4 << 20),
        cost_estimate=COST,
        name="row_values",
    )(*flat)


def ffn_forward(x, up_w, up_b, down_w, out_type):
    rows, width = x.shape
    units = up_w.shape[1]
    tile = min(512, units)
    steps = units // tile

    def body(x_ref, up_ref, b_ref, down_ref, act_ref, slope_ref, out_ref, acc_ref):
        step = pl.program_id(0)
        up = dot_on(x_ref[...], up_ref[...], 1, 0) + b_ref[...].astype(jnp.float32)
        act, slope = gelu_parts(up)
        act = act.astype(LOW)
        act_ref[...] = act
        slope_ref[...] = slope.astype(LOW)
        accumulate(step, steps, dot_on(act, down_ref[...], 1, 0), acc_ref, out_ref)

    part = pl.BlockSpec((rows, tile), lambda i: (0, i))
    whole = pl.BlockSpec((rows, width), lambda i: (0, 0))
    return pl.pallas_call(
        body,
        grid=(steps,),
        in_specs=[
            whole,
            pl.BlockSpec((width, tile), lambda i: (0, i)),
            pl.BlockSpec((1, tile), lambda i: (0, i)),
            pl.BlockSpec((tile, width), lambda i: (i, 0)),
        ],
        out_specs=[part, part, whole],
        out_shape=[jax.ShapeDtypeStruct((rows, units), LOW)] * 2
        + [jax.ShapeDtypeStruct((rows, width), out_type)],
        scratch_shapes=[pltpu.VMEM((rows, width), jnp.float32)],
        compiler_params=pltpu.CompilerParams(vmem_limit_bytes=16 << 20),
        cost_estimate=COST,
        name="ffn_forward",
    )(x, up_w, up_b, down_w)


def ffn_back(grad, slope, down_w, up_w, out_type):
    rows, width = grad.shape
    units = up_w.shape[1]
    tile = min(512, units)
    steps = units // tile

    def body(g_ref, slope_ref, down_ref, up_ref, dup_ref, sum_ref, out_ref, acc_ref):
        step = pl.program_id(0)
        dact = dot_on(g_ref[...], down_ref[...], 1, 1)
        dup = (dact * slope_ref[...].astype(jnp.float32)).astype(LOW)
        dup_ref[...] = dup
        sum_ref[...] = jnp.sum(dup.astype(jnp.float32), 0, keepdims=True)
        accumulate(step, steps, dot_on(dup, up_ref[...], 1, 1), acc_ref, out_ref)

    part = pl.BlockSpec((rows, tile), lambda i: (0, i))
    whole = pl.BlockSpec((rows, width), lambda i: (0, 0))
    return pl.pallas_call(
        body,
        grid=(steps,),
        in_specs=[
            whole,
            part,
            pl.BlockSpec((tile, width), lambda i: (i, 0)),
            pl.BlockSpec((width, tile), lambda i: (0, i)),
        ],
        out_specs=[part, pl.BlockSpec((1, tile), lambda i: (0, i)), whole],
        out_shape=[
            jax.ShapeDtypeStruct((rows, units), LOW),
            jax.ShapeDtypeStruct((1, units), jnp.float32),
            jax.ShapeDtypeStruct((rows, width), out_type),
        ],
        scratch_shapes=[pltpu.VMEM((rows, width), jnp.float32)],
        compiler_params=pltpu.CompilerParams(vmem_limit_bytes=16 << 20),
        cost_estimate=COST,
        name="ffn_back",
    )(grad, slope, down_w, up_w)


def accumulate(step, steps, term, acc_ref, out_ref):
    if steps == 1:
        out_ref[...] = term.astype(out_ref.dtype)
        return

    @pl.when(step == 0)
    def _():
        acc_ref[...] = term

    @pl.when((step > 0) & (step < steps - 1))
    def _():
        acc_ref[...] += term

    @pl.when(step == steps - 1)
    def _():
        out_ref[...] = (acc_ref[...] + term).astype(out_ref.dtype)


def mean(rows):
    return jnp.mean(rows, -1, keepdims=True)


def normalise(rows):
    centre = rows - mean(rows)
    inverse = lax.rsqrt(mean(centre * centre) + EPS)
    return centre * inverse, inverse


def norm_back(grad, normed, inverse, gain):
    scaled = grad * gain
    return inverse * (scaled - mean(scaled) - normed * mean(scaled * normed))


def gelu_parts(values):
    square = values * values
    rate = -2.0 * GELU_C
    gate = 1.0 / (1.0 + jnp.exp(values * (rate + rate * 0.044715 * square)))
    output = values * gate
    slope = gate + output * (1.0 - gate) * (2.0 * GELU_C + 6.0 * GELU_C * 0.044715 * square)
    return output, slope


def dot(a, b):
    return jnp.dot(a, b, preferred_element_type=jnp.float32)


def dot_nt(a, b):
    return dot_on(a, b, 1, 1)


def dot_tn(a, b):
    return dot_on(a, b, 0, 0)


def column_sums(rows):
    ones = jnp.ones((8, rows.shape[0]), LOW)
    return dot(ones, rows)[0]


def local(
    dp_size,
    ranks,
    hidden_in,
    query_w,
    key_w,
    value_w,
    query_b,
    value_b,
    out_w,
    out_b,
    gain_attn,
    shift_attn,
    up_w,
    up_b,
    down_w,
    down_b,
    gain_ffn,
    shift_ffn,
    random_blocks,
    cotangent,
):
    own_rows, seqs_here, width = hidden_in.shape
    channels, hidden_units = query_w.shape[1], up_w.shape[1]
    length = own_rows * ranks
    chunks = CHUNKS
    piece = own_rows // chunks
    every = range(chunks)
    others = range(1, ranks)
    ring = Ring(dp_size)
    rows_in = hidden_in.reshape(own_rows, width)
    grad_out = cotangent.reshape(own_rows, width)
    lows = [c * piece for c in every]
    order = Order()
    run, tie = order.run, order.tie

    far_rows = fetch(rows_in, ranks)

    def project(x, *w):
        return (dot(x, w[0]) + w[1]).astype(LOW)

    def set_up(ids, q_w, k_w, v_w, q_b, v_b, *vectors):
        return (
            ring.table(own_rows // BLOCK),
            ids.reshape(ids.shape[0], -1),
            jnp.concatenate([q_w, k_w, v_w], 1),
            jnp.concatenate([q_b, jnp.zeros_like(q_b), v_b]).astype(jnp.float32),
            [v.reshape(1, -1) for v in vectors],
        )

    table, random_ids, qkv_w, qkv_b, vectors = run(
        set_up,
        random_blocks,
        query_w,
        key_w,
        value_w,
        query_b,
        value_b,
        out_b,
        gain_attn,
        shift_attn,
        up_b,
        down_b,
        gain_ffn,
        shift_ffn,
    )
    out_b, gain_attn, shift_attn, up_b, down_b, gain_ffn, shift_ffn = vectors
    near = run(project, rows_in, qkv_w, qkv_b)
    qkv = run(
        lambda n, w, b, *x: jnp.concatenate([n] + [project(p, w, b) for p in x], 0),
        near,
        qkv_w,
        qkv_b,
        *far_rows,
    )

    contexts, lses, attn_moved, attn_own = [], [], [], []
    for c in every:
        context, lse = run(lambda v: attend(v, random_ids, table, c, chunks, ranks), qkv)
        contexts.append(context)
        lses.append(lse)
        shares = [
            run(lambda x: product(x, j * piece, piece, out_w, False, LOW), context) for j in others
        ]
        attn_moved.append(hand_over(shares, ranks))
    for c in every:
        attn_own.append(
            run(lambda x: product(x, 0, piece, out_w, False, jnp.float32), contexts[c])
        )

    low_rows = (width, LOW)

    def norm_one(low, own, *moved):
        def body(*values):
            *terms, source, bias, gain, shift = values
            attn_out = functools.reduce(jnp.add, terms)
            resid = source + attn_out + bias
            normed, inverse = normalise(resid)
            hidden = gain * normed + shift
            inverse = jnp.broadcast_to(inverse, (inverse.shape[0], 128))
            return [hidden, normed, inverse], [resid * resid, attn_out * attn_out]

        return row_kernel(
            "norm_one",
            body,
            piece,
            [(own, 0)] + [(m, 0) for m in moved] + [(rows_in, low)],
            [out_b, gain_attn, shift_attn],
            [low_rows, low_rows, (128, jnp.float32)],
            8,
        )

    x, n1, i1, squares, acts, slopes, mlp_moved, mlp_own = ([] for _ in range(8))
    for c in every:
        low, n, i, sq = run(functools.partial(norm_one, lows[c]), attn_own[c], *attn_moved[c])
        n1.append(n)
        i1.append(i)
        squares.append(sq)
        x.append([low] + fetch(low, ranks))
        act, slope, own = run(lambda v: ffn_forward(v, up_w, up_b, down_w, jnp.float32), low)
        acts.append([act])
        slopes.append([slope])
        mlp_own.append(own)
    for c in every:
        shares = []
        for j in others:
            act, slope, share = run(lambda v: ffn_forward(v, up_w, up_b, down_w, LOW), x[c][j])
            acts[c].append(act)
            slopes[c].append(slope)
            shares.append(share)
        mlp_moved.append(hand_over(shares, ranks))

    def norm_two(low, own, h, *moved):
        def body(*values):
            *terms, before, g, bias, gain, shift = values
            mlp_out = functools.reduce(jnp.add, terms)
            normed, inverse = normalise(before + mlp_out + bias)
            back = norm_back(g, normed, inverse, gain)
            sums = [back, g * normed, g, mlp_out * mlp_out]
            return [back, gain * normed + shift], sums

        return row_kernel(
            "norm_two",
            body,
            piece,
            [(own, 0)] + [(m, 0) for m in moved] + [(h, 0), (grad_out, low)],
            [down_b, gain_ffn, shift_ffn],
            [low_rows, low_rows],
            8,
        )

    dmlp, layer_out, sums2 = [], [], []
    for c in every:
        low, out, sums = run(
            functools.partial(norm_two, lows[c]), mlp_own[c], x[c][0], *mlp_moved[c]
        )
        layer_out.append(out)
        sums2.append(sums)
        dmlp.append([low] + fetch(low, ranks))

    dups, dhid_moved, dhid_own, up_sums = [], [], [], []
    for c in every:
        dup, total, own = run(
            lambda d, s: ffn_back(d, s, down_w, up_w, jnp.float32), dmlp[c][0], slopes[c][0]
        )
        dups.append([dup])
        up_sums.append(total)
        dhid_own.append(own)
    for c in every:
        shares = []
        for j in others:
            dup, total, share = run(
                lambda d, s: ffn_back(d, s, down_w, up_w, LOW), dmlp[c][j], slopes[c][j]
            )
            dups[c].append(dup)
            up_sums.append(total)
            shares.append(share)
        dhid_moved.append(hand_over(shares, ranks))

    under_way = []

    def advance(*names):
        for name in names or [n for n, _ in under_way]:
            for entry in [e for e in under_way if e[0] == name]:
                if next(entry[1], "end") == "end":
                    under_way.remove(entry)

    class Grads:
        def __init__(self, rows, shares, sides, extra=None):
            self.rows, self.shares, self.extra = rows, shares, extra
            self.leaves, self.tree = jax.tree.flatten(sides)
            leaves = [x for x in self.leaves if not isinstance(x, int)]
            self.arrays = list({id(x): x for x in leaves}.values())
            self.results = []

        def halves(self, *cores):
            def call(t, extra, *tied):
                known = {id(x): v for x, v in zip(self.arrays, tied)}
                found = [x if isinstance(x, int) else known[id(x)] for x in self.leaves]
                sides = jax.tree.unflatten(self.tree, found)
                return grad_halves(t, cores, ring.chips, self.rows, self.shares, sides, extra)

            return run(call, table, self.extra, *self.arrays)

        def ring(self, name, kept, moved, pair=None):
            under_way.append((name, ring.steps(order, table, kept, moved, self.results, pair)))

    def pieces_of(parts):
        return [(p, 0, piece) for part in parts for p in part]

    ffn_rows = hidden_units // dp_size
    down_share = Share(dp_size, (hidden_units, width), ffn_rows, 0)
    up_share = Share(dp_size, (width, hidden_units), ffn_rows, down_share.end)
    ffn = Grads(
        ffn_rows,
        [down_share, up_share],
        [(pieces_of(acts), pieces_of(dmlp)), (pieces_of(x), pieces_of(dups))],
    )
    ffn_given, ffn_kept = ffn.halves(MATE, CORE)

    def norm_one_back(own, d2, n, i, *moved):
        def body(*values):
            *terms, normed, inverse, gain = values
            dhidden = functools.reduce(jnp.add, terms)
            back = norm_back(dhidden, normed, inverse[:, :1], gain)
            return [back], [back, dhidden * normed, dhidden]

        return row_kernel(
            "norm_one_back",
            body,
            piece,
            [(a, 0) for a in (own, *moved, d2, n, i)],
            [gain_attn],
            [low_rows],
            8,
        )

    dattn, sums1, dcontexts = [], [], []
    for c in every:
        low, sums = run(
            norm_one_back, dhid_own[c], dmlp[c][0], n1[c], i1[c], *dhid_moved[c]
        )
        sums1.append(sums)
        dattn.append([low] + fetch(low, ranks))
    ffn_moved = ring.mate(tie(ffn_given))
    for c in every:
        dcontexts.append(
            run(lambda d: product(d, 0, piece, out_w, True, LOW, None, ranks, 0), dattn[c][0])
        )
    norms = run(sum_kernel, sums1, sums2, squares)
    norms = [norms] + fetch(norms, ranks)
    ffn.ring("ffn", ffn_kept, ffn_moved)
    advance("ffn")

    dq_parts, sums = [], []
    for c in every:
        dcontext = dcontexts[c]
        for j in others:
            dcontext = run(
                lambda d, whole: product(d, 0, piece, out_w, True, LOW, whole, ranks, j),
                dattn[c][j],
                dcontext,
            )
        advance("ffn")
        dq, *sums = run(
            lambda v, d, l, e, s: jax.tree.leaves(
                attend_back(v, d, l, random_ids, table, e, s, c, chunks, ranks)
            ),
            qkv,
            dcontext,
            lses[c],
            dq_parts,
            sums,
        )
        dq_parts.append(dq)
    dqkv, bias_sums = dq, sums[0]

    attn_rows = width // dp_size
    attn_shares = [Share(dp_size, (width, 3 * channels), attn_rows, 0)]
    attn_sides = [
        (
            [(x, 0, own_rows) for x in [rows_in] + far_rows],
            [(dqkv, j * own_rows, own_rows) for j in range(ranks)],
        )
    ]
    with_out = channels % 256 == 0
    if with_out:
        attn_shares.append(Share(dp_size, (channels, width), attn_rows, attn_shares[0].end))
        attn_sides.append(
            (
                [(contexts[c], j * piece, piece) for c in every for j in range(ranks)],
                [(dattn[c][j], 0, piece) for c in every for j in range(ranks)],
            )
        )
    values = run(functools.partial(row_values, dp_size), norms, up_sums, bias_sums)
    pair = attn_shares[-1].end
    attn = Grads(attn_rows, attn_shares, attn_sides, values)
    (given,) = attn.halves(MATE)
    advance("ffn")
    moved = ring.mate(tie(given))
    shares = [
        run(lambda d: product(d, j * own_rows, own_rows, qkv_w, True, LOW), dqkv) for j in others
    ]
    dinput_moved = hand_over(shares, ranks)
    (kept,) = attn.halves(CORE)
    attn.ring("attn", kept, moved, pair)
    advance("attn")
    dinput_own = run(lambda d: product(d, 0, own_rows, qkv_w, True, jnp.float32), dqkv)
    advance("ffn", "attn")
    grad_input = run(
        lambda own, d, *m: (plus(own, m) + jnp.concatenate(d, 0)).astype(LOW),
        dinput_own,
        [d[0] for d in dattn],
        *dinput_moved,
    )
    totals = {}
    entries = float(own_rows * ranks * dp_size * seqs_here * width)
    ffn_outs = [((g.shard, g.columns), g.moves) for g in (down_share, up_share)]
    up_rows = -(-hidden_units // width)

    def spread(value):
        lines = width // 128

        def rows(low, high):
            return value[low * lines : high * lines].reshape(-1)

        bias = rows(8 + up_rows, 9 + up_rows)
        return (
            [rows(i, i + 1) for i in range(6)],
            jnp.sqrt(value[6 * lines, :3] / entries),
            bias[:channels],
            bias[channels : 2 * channels],
            rows(8, 8 + up_rows)[:hidden_units],
        )

    while under_way:
        advance()
        for n, name in enumerate(("down", "up")):
            if ffn.results and name not in totals:
                (totals[name],) = run(
                    lambda *p: ring.place_pieces(table, p, [ffn_outs[n]]), *ffn.results
                )
                break
    everything = slice(0, attn_rows)
    attn_outs = []
    for i in range(3):
        cut = slice(i * channels, (i + 1) * channels)
        attn_outs.append(
            ((attn_rows, channels), [(everything, slice(0, channels), everything, cut)])
        )
    lines = slice(0, 8)
    attn_outs.append(
        ((8, 128), [(lines, slice(0, 128), (lines, slice(8, 16)), slice(pair, pair + 128))])
    )
    if with_out:
        attn_outs.append(((attn_shares[1].shard, width), attn_shares[1].moves))
    grad_q, grad_k, grad_v, value, *rest = run(lambda *p: ring.place_pieces(table, p, attn_outs), *attn.results)
    if with_out:
        (grad_out_w,) = rest
    else:
        partial = sum(
            dot_tn(contexts[c], jnp.concatenate(dattn[c], 0)) for c in every
        )
        grad_out_w = lax.psum(partial.astype(LOW), "dp").astype(jnp.float32)
    grad_down_w, grad_up_w = totals["down"], totals["up"]
    vectors, rms_stats, *biases = spread(value)
    shape = hidden_in.shape
    return (
        jnp.concatenate(layer_out, 0).reshape(shape),
        grad_input.reshape(shape),
        grad_q,
        grad_k,
        grad_v,
        biases[0],
        biases[1],
        grad_out_w,
        vectors[0],
        vectors[1],
        vectors[2],
        grad_up_w,
        biases[2],
        grad_down_w,
        vectors[3],
        vectors[4],
        vectors[5],
        rms_stats,
    )


def solution(mesh):
    rows = P("tensor", "dp", None)
    columns, split, whole = P(None, "tensor"), P("tensor"), P()
    first = P("tensor", None)
    return jax.shard_map(
        functools.partial(local, mesh.shape["dp"], mesh.shape["tensor"]),
        mesh=mesh,
        in_specs=(
            rows,
            columns,
            columns,
            columns,
            split,
            split,
            first,
            whole,
            whole,
            whole,
            columns,
            split,
            first,
            whole,
            whole,
            whole,
            P("tensor", None, None),
            rows,
        ),
        out_specs=(
            rows,
            rows,
            columns,
            columns,
            columns,
            split,
            split,
            first,
            whole,
            whole,
            whole,
            columns,
            split,
            first,
            whole,
            whole,
            whole,
            whole,
        ),
        check_vma=False,
    )
```
